32 devices in a mesh: fsdp: 2 (over y), ctx: 4 (over x, core), tp: 4 (over z).
Axes of the slice: x: 2, y: 2, z: 4, core: 2. Of those that a mesh axis runs over, the one named last changes fastest.
Arguments:
- tokens: bfloat16 [4, 2048, 2048], P('fsdp', 'ctx', 'tp'), may hold values from -6 to 6
- lengths: int32 [4], P('fsdp'), may hold values from 1024 to 2048, as said below
- cotangent: bfloat16 [4, 2048, 2048], P('fsdp', 'ctx', 'tp'), may hold values from -6 to 6
- first_gain: bfloat16 [2048], P(('fsdp', 'ctx')), may hold values from 0.25 to 1.75
- first_shift: bfloat16 [2048], P(('fsdp', 'ctx')), may hold values from -1.75 to 1.75
- joined_weight: bfloat16 [2048, 8, 768], P(('fsdp', 'ctx'), 'tp'), may hold values from -0.125 to 0.125
- joined_bias: bfloat16 [8, 768], P('tp', ('fsdp', 'ctx')), may hold values from -1.75 to 1.75
- output_weight: bfloat16 [2048, 8, 256], P(('fsdp', 'ctx'), 'tp'), may hold values from -0.75 to 0.75
- output_bias: bfloat16 [2048], P(('fsdp', 'ctx')), may hold values from -1.75 to 1.75
- second_gain: bfloat16 [2048], P(('fsdp', 'ctx')), may hold values from 0.25 to 1.75
- second_shift: bfloat16 [2048], P(('fsdp', 'ctx')), may hold values from -1.75 to 1.75
- inner_weight: bfloat16 [2048, 8192], P(('fsdp', 'ctx'), 'tp'), may hold values from -0.125 to 0.125
- inner_bias: bfloat16 [256, 32], P('tp', ('fsdp', 'ctx')), may hold values from -3 to 3
- outer_weight: bfloat16 [2048, 8192], P(('fsdp', 'ctx'), 'tp'), may hold values from -0.0625 to 0.0625
- outer_bias: bfloat16 [2048], P(('fsdp', 'ctx')), may hold values from -1.75 to 1.75
Outputs:
- layer_out: bfloat16 [4, 2048, 2048], P('fsdp', 'ctx', 'tp')
- tokens_grad: float32 [4, 2048, 2048], P('fsdp', 'ctx', 'tp')
- first_gain_grad: float32 [2048], P(('fsdp', 'ctx'))
- first_shift_grad: float32 [2048], P(('fsdp', 'ctx'))
- joined_weight_grad: float32 [2048, 8, 768], P(('fsdp', 'ctx'), 'tp')
- joined_bias_grad: float32 [8, 768], P('tp', ('fsdp', 'ctx'))
- output_weight_grad: float32 [2048, 8, 256], P(('fsdp', 'ctx'), 'tp')
- output_bias_grad: float32 [2048], P(('fsdp', 'ctx'))
- second_gain_grad: float32 [2048], P(('fsdp', 'ctx'))
- second_shift_grad: float32 [2048], P(('fsdp', 'ctx'))
- inner_weight_grad: float32 [2048, 8192], P(('fsdp', 'ctx'), 'tp')
- inner_bias_grad: float32 [256, 32], P('tp', ('fsdp', 'ctx'))
- outer_weight_grad: float32 [2048, 8192], P(('fsdp', 'ctx'), 'tp')
- outer_bias_grad: float32 [2048], P(('fsdp', 'ctx'))
The draws below stay inside these ranges and needn't reach their ends.
Inputs may be any that keep to these rules, and one draw needn't show every extreme that they name: `lengths`: positions at or past a sequence's length are padding. In every draw some sequence has the full length 2048 and another has exactly 1024.
All inputs are finite; a program needn't handle non-finite values.
Results may differ from the reference program's by a relative error of at most 0.018.
Values may be sent and summed in bfloat16 or wider, within the bound.
No kernel may reach another device: no remote copies, remote signals or barrier semaphores. Data moves between devices by JAX's collectives and lax.ppermute only.
A program may use at most 256 MiB of HBM per device.

```python
import jax
import jax.numpy as jnp
from jax import lax

D = 2048
HEADS = 8
HEAD = 256
ROTARY = 64
FF = 8192
SEQ = 2048
MIN_LEN = 1024
SEQS = 4


def draw_lengths(key, part):
    first, second = jax.random.split(key)
    drawn = jax.random.randint(first, (SEQS,), MIN_LEN, SEQ + 1)
    order = jax.random.permutation(second, SEQS)
    drawn = drawn.at[order[0]].set(SEQ)
    drawn = drawn.at[order[1]].set(MIN_LEN)
    return drawn.astype(jnp.int32)


def level_of(own_key, extent, cuts, smallest, top_value):
    level = 1.0
    for dim, parts in cuts:
        draws = jax.random.uniform(jax.random.fold_in(jax.random.fold_in(own_key, 6), dim), (parts,), jnp.float32, smallest / len(cuts), top_value / len(cuts))
        level = level * jnp.repeat(jnp.exp(draws), extent[dim] // parts).reshape((-1,) + (1,) * (len(extent) - 1 - dim))
    return level


def gaussian(stream_key, dims, deviation, reach, cuts=(), kind=jnp.bfloat16):
    level = level_of(stream_key, dims, cuts, -0.22, 0.18) if cuts else 1.0
    values = jax.random.normal(stream_key, dims, jnp.float32) * deviation * level
    return jnp.minimum(jnp.maximum(values, -reach), reach).astype(kind)


def setup_inputs(seed: int = 0) -> dict:
    key_of = jax.random.split(jax.random.key(seed), 16)
    return {
        "tokens": gaussian(key_of[0], (SEQS, SEQ, D), 1.0, 6.0, ((0, 2), (1, 4), (2, 4))),
        "lengths": draw_lengths(jax.random.fold_in(key_of[15], 71), 0),
        "cotangent": gaussian(key_of[2], (SEQS, SEQ, D), 1.0, 6.0, ((0, 2), (1, 4), (2, 4))),
        "first_gain": jnp.clip(1.0 + 0.15 * jax.random.normal(key_of[3], (D,), jnp.float32), 0.25, 1.75).astype(jnp.bfloat16),
        "first_shift": gaussian(key_of[4], (D,), 0.3, 1.75, ((0, 8),)),
        "joined_weight": gaussian(key_of[5], (D, HEADS, 3 * HEAD), D ** -0.5, 0.125, ((0, 8), (1, 4))),
        "joined_bias": gaussian(key_of[6], (HEADS, 3 * HEAD), 0.3, 1.75, ((0, 4), (1, 8))),
        "output_weight": gaussian(key_of[7], (D, HEADS, HEAD), (D // 32) ** -0.5, 0.75, ((0, 8), (1, 4))),
        "output_bias": gaussian(key_of[8], (D,), 0.3, 1.75, ((0, 8),)),
        "second_gain": jnp.clip(1.0 + 0.15 * jax.random.normal(key_of[9], (D,), jnp.float32), 0.25, 1.75).astype(jnp.bfloat16),
        "second_shift": gaussian(key_of[10], (D,), 0.3, 1.75, ((0, 8),)),
        "inner_weight": gaussian(key_of[11], (D, FF), D ** -0.5, 0.125, ((0, 8), (1, 4))),
        "inner_bias": gaussian(key_of[12], (FF // 32, 32), 0.5, 3.0, ((0, 4), (1, 8))),
        "outer_weight": gaussian(key_of[13], (D, FF), FF ** -0.5, 0.0625, ((0, 8), (1, 4))),
        "outer_bias": gaussian(key_of[14], (D,), 0.3, 1.75, ((0, 8),)),
    }


@jax.custom_vjp
def low(v):
    return lax.optimization_barrier(v.astype(jnp.bfloat16)).astype(jnp.float32)

@jax.custom_vjp
def low_back(v):
    return v

def low_keep(v):
    return (low(v), None)

def low_pass(kept, grad):
    return (grad,)

def back_keep(v):
    return (v, None)

def back_low(kept, grad):
    return (low(grad),)
low.defvjp(low_keep, low_pass)
low_back.defvjp(back_keep, back_low)
highest = lax.Precision.HIGHEST

def layer_norm(rows, gain, shift):
    center = lax.optimization_barrier(jnp.mean(rows, axis=-1, keepdims=True))
    shifted = rows - center
    variance = lax.optimization_barrier(jnp.mean(shifted * shifted, axis=-1, keepdims=True))
    return shifted * lax.rsqrt(variance + 1e-05) * gain + shift

def rotate(values, cosine, sine):
    half = ROTARY // 2
    front = values[..., :half]
    back = values[..., half:ROTARY]
    return jnp.concatenate([front * cosine - back * sine, back * cosine + front * sine, values[..., ROTARY:]], axis=-1)

@jax.checkpoint
def head_attention(query, key_rows, value_rows, allowed):
    scores = low_back(jnp.dot(query, key_rows.T, precision=highest) * HEAD ** (-0.5))
    scores = jnp.where(allowed, scores, -1e+30)
    probs = low(jax.nn.softmax(scores, axis=-1))
    return jnp.dot(probs, value_rows, precision=highest)

def forward(params, rows, valid, allowed, cosine, sine):
    first_gain, first_shift, joined_weight, joined_bias, output_weight, output_bias, second_gain, second_shift, inner_weight, inner_bias, outer_weight, outer_bias = params
    first_in = low(layer_norm(rows, first_gain, first_shift))
    second_in = low(layer_norm(rows, second_gain, second_shift))
    joined = low_back(jnp.einsum('tc,chk->thk', first_in, joined_weight, precision=highest) + joined_bias)
    query = low(rotate(joined[..., :HEAD], cosine, sine))
    keys = low(rotate(joined[..., HEAD:2 * HEAD], cosine, sine))
    values = low(joined[..., 2 * HEAD:])
    heads_out = lax.map(lambda item: head_attention(item[0], item[1], item[2], allowed), (query.transpose(1, 0, 2), keys.transpose(1, 0, 2), values.transpose(1, 0, 2)))
    context = low(low_back(heads_out.transpose(1, 0, 2)))
    attention = jnp.einsum('thd,ehd->te', context, output_weight, precision=highest)
    upper = low_back(jnp.dot(second_in, inner_weight, precision=highest) + inner_bias.reshape(FF))
    active = low(jax.nn.gelu(upper, approximate=False))
    feed = jnp.einsum('tf,ef->te', active, outer_weight, precision=highest)
    return valid[:, None] * (rows + attention + feed + output_bias + outer_bias)

def reference(tokens, lengths, cotangent, first_gain, first_shift, joined_weight, joined_bias, output_weight, output_bias, second_gain, second_shift, inner_weight, inner_bias, outer_weight, outer_bias):
    params = tuple((p.astype(jnp.float32) for p in (first_gain, first_shift, joined_weight, joined_bias, output_weight, output_bias, second_gain, second_shift, inner_weight, inner_bias, outer_weight, outer_bias)))
    half = ROTARY // 2
    frequency = 1.0 / 10000.0 ** (jnp.arange(half, dtype=jnp.float32) * 2.0 / ROTARY)
    position = jnp.arange(SEQ, dtype=jnp.int32)
    angles = position.astype(jnp.float32)[:, None] * frequency[None, :]
    cosine = jnp.cos(angles)[:, None, :]
    sine = jnp.sin(angles)[:, None, :]

    def one(carry, item):
        rows, length, grad_out = item
        valid = (position < length).astype(jnp.float32)
        allowed = (position[None, :] <= position[:, None]) & (position[None, :] < length)
        result, pullback = jax.vjp(lambda p, r: forward(p, r, valid, allowed, cosine, sine), params, rows.astype(jnp.float32))
        grads, grad_rows = pullback(grad_out.astype(jnp.float32))
        carry = jax.tree.map(lambda a, b: a + b, carry, grads)
        return (carry, (result.astype(jnp.bfloat16), grad_rows))
    zeros = tuple((jnp.zeros(p.shape, jnp.float32) for p in params))
    totals, (layer_out, tokens_grad) = lax.scan(one, zeros, (tokens, lengths, cotangent))
    return (layer_out, tokens_grad) + tuple(totals)
```

```python
import functools

import jax
import jax.numpy as jnp
from jax import lax
from jax.experimental import pallas as pl
from jax.experimental.pallas import tpu as pltpu
from jax.sharding import PartitionSpec as P

HEAD = 256
ROTARY = 64
F32 = jnp.float32
BF16 = jnp.bfloat16
VMEM_LIMIT = 56 << 20
NN = (((1,), (0,)), ((), ()))
NT = (((1,), (1,)), ((), ()))
TN = (((0,), (0,)), ((), ()))


def dot(a, b, dims):
    return lax.dot_general(a, b, dims, preferred_element_type=F32)


def params(*semantics):
    return pltpu.CompilerParams(
        dimension_semantics=semantics or None, vmem_limit_bytes=VMEM_LIMIT
    )


def cost(flops, moved, transcendentals=0):
    return pl.CostEstimate(flops=flops, bytes_accessed=moved, transcendentals=transcendentals)


def line_gather(piece, axis):
    size = lax.axis_size(axis)
    up = [(i, i + 1) for i in range(size - 1)]
    down = [(i + 1, i) for i in range(size - 1)]
    right, left = [], []
    a = b = piece
    for _ in range(size - 1):
        a = lax.ppermute(a, axis, up)
        b = lax.ppermute(b, axis, down)
        right.append(a)
        left.append(b)
    return [(right[s - 1], left[size - s - 1]) for s in range(1, size)]


def norm_kernel(size, me_ref, own, *refs):
    pairs = refs[: 2 * (size - 1)]
    gains, first_out, second_out, token_out, stat_out, work = refs[2 * (size - 1) :]
    part = own.shape[1]
    me = me_ref[0]
    for s in range(size):
        if s == 0:
            piece = own[...].astype(F32)
        else:
            piece = pairs[2 * s - 2][...].astype(F32) + pairs[2 * s - 1][...].astype(F32)
        at = lax.rem(me - s + size, size)
        work[:, pl.ds(pl.multiple_of(at * part, part), part)] = piece
    rows = work[...]
    token_out[...] = rows.astype(BF16)
    width = rows.shape[1]
    center = jnp.sum(rows, axis=1, keepdims=True) * (1.0 / width)
    shifted = rows - center
    inverse = lax.rsqrt(jnp.sum(shifted * shifted, axis=1, keepdims=True) * (1.0 / width) + 1e-05)
    normed = shifted * inverse
    first_out[...] = (normed * gains[0:1, :] + gains[1:2, :]).astype(BF16)
    second_out[...] = (normed * gains[2:3, :] + gains[3:4, :]).astype(BF16)
    lane = lax.broadcasted_iota(jnp.int32, stat_out.shape, 1)
    stat_out[...] = jnp.where(lane == 0, center, inverse)


def norm_call(me, own, pairs, gains, tile=128):
    count, part = own.shape
    size = len(pairs) + 1
    width = part * size
    flat = [p for pair in pairs for p in pair]
    block = pl.BlockSpec((tile, part), lambda i, *_: (i, 0))
    wide = pl.BlockSpec((tile, width), lambda i, *_: (i, 0))
    return pl.pallas_call(
        functools.partial(norm_kernel, size),
        grid_spec=pltpu.PrefetchScalarGridSpec(
            num_scalar_prefetch=1,
            grid=(count // tile,),
            in_specs=[block] * (1 + len(flat)) + [pl.BlockSpec((4, width), lambda i, *_: (0, 0))],
            out_specs=[wide, wide, wide, pl.BlockSpec((tile, 128), lambda i, *_: (i, 0))],
            scratch_shapes=[pltpu.VMEM((tile, width), F32)],
        ),
        out_shape=[
            jax.ShapeDtypeStruct((count, width), BF16),
            jax.ShapeDtypeStruct((count, width), BF16),
            jax.ShapeDtypeStruct((count, width), BF16),
            jax.ShapeDtypeStruct((count, 128), F32),
        ],
        compiler_params=params("arbitrary"),
        cost_estimate=cost(count * width * 16, count * width * 10),
        name="norm",
    )(me, own, *flat, gains)


def cot_kernel(size, local_len, tile, me_ref, len_ref, own, *refs):
    pairs = refs[: 2 * (size - 1)]
    rows_out, sum_out = refs[2 * (size - 1) :]
    part = own.shape[1]
    me, ctx = me_ref[0], me_ref[1]
    step = pl.program_id(0)
    start = step * tile
    seq = start // local_len
    length = len_ref[seq]
    position = ctx * local_len + lax.rem(start, local_len)
    position = position + lax.broadcasted_iota(jnp.int32, (tile, 1), 0)
    keep = position < length

    @pl.when(step == 0)
    def _():
        sum_out[...] = jnp.zeros_like(sum_out)

    for s in range(size):
        if s == 0:
            piece = own[...].astype(F32)
        else:
            piece = pairs[2 * s - 2][...].astype(F32) + pairs[2 * s - 1][...].astype(F32)
        piece = jnp.where(keep, piece, 0.0)
        at = lax.rem(me - s + size, size)
        cols = pl.ds(pl.multiple_of(at * part, part), part)
        rows_out[:, cols] = piece.astype(BF16)
        sum_out[0:1, cols] += jnp.sum(piece, axis=0, keepdims=True)


def cot_call(places, lengths, own, pairs, local_len, tile=256):
    count, part = own.shape
    size = len(pairs) + 1
    width = part * size
    flat = [p for pair in pairs for p in pair]
    block = pl.BlockSpec((tile, part), lambda i, *_: (i, 0))
    return pl.pallas_call(
        functools.partial(cot_kernel, size, local_len, tile),
        grid_spec=pltpu.PrefetchScalarGridSpec(
            num_scalar_prefetch=2,
            grid=(count // tile,),
            in_specs=[block] * (1 + len(flat)),
            out_specs=[
                pl.BlockSpec((tile, width), lambda i, *_: (i, 0)),
                pl.BlockSpec((8, width), lambda i, *_: (0, 0)),
            ],
        ),
        out_shape=[
            jax.ShapeDtypeStruct((count, width), BF16),
            jax.ShapeDtypeStruct((8, width), F32),
        ],
        compiler_params=params("arbitrary"),
        cost_estimate=cost(count * width * 4, count * width * 6),
        name="cotangent_rows",
    )(places, lengths, own, *flat)


def joined_kernel(seqs, rows_ref, weight_ref, bias_ref, table_ref, query_ref, pair_ref):
    kind = lax.rem(pl.program_id(0), 3)
    out = dot(rows_ref[...], weight_ref[...], NN) + bias_ref[0:1, :]

    def turned():
        front = out[:, :128]
        up = pltpu.roll(front, 128 - ROTARY // 2, 1)
        down = pltpu.roll(front, ROTARY // 2, 1)
        table = table_ref[...]
        if seqs > 1:
            table = jnp.concatenate([table] * seqs, axis=0)
        front = front * table[:, :128] + up * table[:, 128:256] + down * table[:, 256:]
        return jnp.concatenate([front, out[:, 128:]], axis=1)

    @pl.when(kind == 0)
    def _():
        query_ref[...] = (turned().astype(BF16).astype(F32) * HEAD ** (-0.5)).astype(BF16)

    @pl.when(kind == 1)
    def _():
        pair_ref[...] = turned().astype(BF16)

    @pl.when(kind == 2)
    def _():
        pair_ref[...] = out.astype(BF16)


def joined_call(rows, weight, bias, table, seqs, heads):
    count, width = rows.shape
    return pl.pallas_call(
        functools.partial(joined_kernel, seqs),
        grid=(3 * heads,),
        in_specs=[
            pl.BlockSpec((count, width), lambda j: (0, 0)),
            pl.BlockSpec((width, HEAD), lambda j: (0, j)),
            pl.BlockSpec((8, HEAD), lambda j: (0, j)),
            pl.BlockSpec(table.shape, lambda j: (0, 0)),
        ],
        out_specs=[
            pl.BlockSpec((count, HEAD), lambda j: (0, j // 3)),
            pl.BlockSpec((count, HEAD), lambda j: (0, 2 * (j // 3) + (j % 3) // 2)),
        ],
        out_shape=[
            jax.ShapeDtypeStruct((count, heads * HEAD), BF16),
            jax.ShapeDtypeStruct((count, 2 * heads * HEAD), BF16),
        ],
        compiler_params=params("arbitrary"),
        cost_estimate=cost(6 * heads * HEAD * count * width, 2 * (count + 3 * heads * HEAD) * width),
        name="joined",
    )(rows, weight, jnp.broadcast_to(bias.reshape(1, -1), (8, bias.size)), table)


def visit(slot, local_len, half, block, place, length):
    first_key = block * local_len
    last_query = place * local_len + (half + 1) * (local_len // 2) - 1
    return (block >= 0) & (first_key <= last_query) & (first_key < length)


def masked(scores, first_key, first_query, length, axis_key):
    shape = scores.shape
    key = first_key + lax.broadcasted_iota(jnp.int32, shape, axis_key)
    query = first_query + lax.broadcasted_iota(jnp.int32, shape, 1 - axis_key)
    return (key <= query) & (key < length)


def forward_kernel(slots, local_len, info, lens, query_ref, *refs):
    pair_refs = refs[:slots]
    context_ref, lse_ref, top, total, acc = refs[slots:]
    seq = pl.program_id(0)
    length = lens[seq]
    place = info[slots]
    top[...] = jnp.full_like(top, -1e30)
    total[...] = jnp.zeros_like(total)
    acc[...] = jnp.zeros_like(acc)
    query = query_ref[...]
    for slot in range(slots):
        block = info[slot]
        first_key = block * local_len

        @pl.when((block >= 0) & (block <= place) & (first_key < length))
        def _():
            keys = pair_refs[slot][:, :HEAD]
            vals = pair_refs[slot][:, HEAD:]
            scores = dot(query, keys, NT)
            ok = masked(scores, first_key, place * local_len, length, 1)
            scores = jnp.where(ok, scores, -1e30)
            best = jnp.maximum(top[...], jnp.max(scores, axis=1, keepdims=True))
            scale = jnp.exp(top[...] - best)
            weights = jnp.exp(scores - best[:, :1])
            weights = jnp.where(ok, weights, 0.0)
            total[...] = total[...] * scale + jnp.sum(weights, axis=1, keepdims=True)
            acc[...] = acc[...] * scale[:, :1] + dot(weights.astype(BF16), vals, NN)
            top[...] = best

    context_ref[...] = (acc[...] / total[:, :1]).astype(BF16)
    lse_ref[...] = top[...] + jnp.log(total[...])


def forward_call(info, lengths, query, pairs, seqs, heads):
    count = query.shape[0]
    local_len = count // seqs
    slots = len(pairs)
    return pl.pallas_call(
        functools.partial(forward_kernel, slots, local_len),
        grid_spec=pltpu.PrefetchScalarGridSpec(
            num_scalar_prefetch=2,
            grid=(seqs, heads),
            in_specs=[pl.BlockSpec((local_len, HEAD), lambda s, h, *_: (s, h))]
            + [pl.BlockSpec((local_len, 2 * HEAD), lambda s, h, *_: (s, h))] * slots,
            out_specs=[
                pl.BlockSpec((local_len, HEAD), lambda s, h, *_: (s, h)),
                pl.BlockSpec((local_len, 128), lambda s, h, *_: (s, h)),
            ],
            scratch_shapes=[
                pltpu.VMEM((local_len, 128), F32),
                pltpu.VMEM((local_len, 128), F32),
                pltpu.VMEM((local_len, HEAD), F32),
            ],
        ),
        out_shape=[
            jax.ShapeDtypeStruct((count, heads * HEAD), BF16),
            jax.ShapeDtypeStruct((count, heads * 128), F32),
        ],
        compiler_params=params("arbitrary", "arbitrary"),
        cost_estimate=cost(
            4 * count * heads * HEAD * local_len * slots,
            4 * count * heads * HEAD * slots,
            count * heads * local_len * slots,
        ),
        name="attention_forward",
    )(info, lengths, query, *pairs)


def backward_kernel(slots, local_len, info, lens, query_ref, context_ref, grad_ref, lse_ref, *refs):
    pair_refs = refs[:slots]
    query_out = refs[slots]
    pair_outs = refs[slots + 1 : 2 * slots + 1]
    acc = refs[2 * slots + 1]
    seq = pl.program_id(0)
    length = lens[seq]
    place = info[slots]
    query = query_ref[...]
    grad = grad_ref[...]
    lse = lse_ref[:, :1]
    shared = jnp.sum(grad.astype(F32) * context_ref[...].astype(F32), axis=1, keepdims=True)
    acc[...] = jnp.zeros_like(acc)
    for slot in range(slots):
        block = info[slot]
        first_key = block * local_len
        seen = (block >= 0) & (block <= place) & (first_key < length)

        @pl.when(seen)
        def _():
            keys = pair_refs[slot][:, :HEAD]
            vals = pair_refs[slot][:, HEAD:]
            scores = dot(query, keys, NT)
            ok = masked(scores, first_key, place * local_len, length, 1)
            probs = jnp.where(ok, jnp.exp(scores - lse), 0.0)
            prob_grad = dot(grad, vals, NT)
            score_grad = (probs * (prob_grad - shared)).astype(BF16)
            acc[...] += dot(score_grad, keys, NN)
            pair_outs[slot][:, :HEAD] = dot(score_grad, query, TN).astype(BF16)
            pair_outs[slot][:, HEAD:] = dot(probs.astype(BF16), grad, TN).astype(BF16)

        @pl.when(jnp.logical_not(seen))
        def _():
            pair_outs[slot][...] = jnp.zeros_like(pair_outs[slot])

    query_out[...] = (acc[...] * HEAD ** (-0.5)).astype(BF16)


def backward_call(info, lengths, query, context, grad, lse, pairs, seqs, heads):
    count = query.shape[0]
    local_len = count // seqs
    slots = len(pairs)
    one = pl.BlockSpec((local_len, HEAD), lambda s, h, *_: (s, h))
    two = pl.BlockSpec((local_len, 2 * HEAD), lambda s, h, *_: (s, h))
    return pl.pallas_call(
        functools.partial(backward_kernel, slots, local_len),
        grid_spec=pltpu.PrefetchScalarGridSpec(
            num_scalar_prefetch=2,
            grid=(seqs, heads),
            in_specs=[one, one, one, pl.BlockSpec((local_len, 128), lambda s, h, *_: (s, h))]
            + [two] * slots,
            out_specs=[one] + [two] * slots,
            scratch_shapes=[pltpu.VMEM((local_len, HEAD), F32)],
        ),
        out_shape=[jax.ShapeDtypeStruct((count, heads * HEAD), BF16)]
        + [jax.ShapeDtypeStruct((count, 2 * heads * HEAD), BF16)] * slots,
        compiler_params=params("arbitrary", "arbitrary"),
        cost_estimate=cost(
            10 * count * heads * HEAD * local_len * slots,
            8 * count * heads * HEAD * slots,
            count * heads * local_len * slots,
        ),
        name="attention_backward",
    )(info, lengths, query, context, grad, lse, *pairs)


def share_pairs(own, axis):
    swap = [(0, 1), (1, 0), (2, 3), (3, 2)]
    sibling = lax.ppermute(own, axis, swap)
    below = lax.ppermute(own, axis, [(0, 2), (1, 3)])
    below_sibling = lax.ppermute(below, axis, [(2, 3), (3, 2)])
    return [own, sibling, below, below_sibling]


def return_pairs(grads, axis):
    own, sibling, below, below_sibling = grads
    from_sibling = lax.ppermute(sibling, axis, [(1, 0), (3, 2)])
    crossed = lax.ppermute(below_sibling, axis, [(2, 3), (3, 2)])
    lower = (below.astype(F32) + crossed.astype(F32)).astype(BF16)
    above = lax.ppermute(lower, axis, [(2, 0), (3, 1)])
    return [own, from_sibling, above]


def gelu_parts(upper):
    phi = 0.5 * (1.0 + lax.erf(upper * 0.7071067811865476))
    slope = phi + upper * jnp.exp(-0.5 * upper * upper) * 0.3989422804014327
    return upper * phi, slope


def body(
    tokens,
    lengths,
    cotangent,
    first_gain,
    first_shift,
    joined_weight,
    joined_bias,
    output_weight,
    output_bias,
    second_gain,
    second_shift,
    inner_weight,
    inner_bias,
    outer_weight,
    outer_bias,
):
    group = ("fsdp", "ctx")
    seqs, local_len, part = tokens.shape
    count = seqs * local_len
    ranks = lax.axis_size("tp")
    width = part * ranks
    shards = lax.axis_size("fsdp") * lax.axis_size("ctx")
    rows_part = width // shards
    heads = joined_weight.shape[1]
    hidden = inner_weight.shape[1]
    me, ctx = lax.axis_index("tp"), lax.axis_index("ctx")

    pack_a = jnp.concatenate([joined_weight.reshape(rows_part, -1), inner_weight], axis=1)
    pack_b = jnp.concatenate([output_weight.reshape(rows_part, -1), outer_weight], axis=1)
    whole_a = lax.all_gather(pack_a, group, axis=0, tiled=True)
    whole_b = lax.all_gather(pack_b, group, axis=0, tiled=True)
    joined_width = heads * 3 * HEAD
    inner = whole_a[:, joined_width:]
    output = whole_b[:, : heads * HEAD]
    outer = whole_b[:, heads * HEAD :]

    own_tokens = tokens.reshape(count, part)
    own_cot = cotangent.reshape(count, part)
    token_pairs = line_gather(own_tokens, "tp")
    own_cot_late, _ = lax.optimization_barrier((own_cot, token_pairs))
    cot_pairs = line_gather(own_cot_late, "tp")

    vectors = [first_gain, first_shift, second_gain, second_shift, output_bias, outer_bias]
    flat = jnp.concatenate(vectors + [joined_bias.reshape(-1), inner_bias.reshape(-1)])
    small = lax.all_gather(flat, group, axis=0, tiled=False).reshape(shards, -1).astype(F32)
    whole = [small[:, i * rows_part : (i + 1) * rows_part].reshape(width) for i in range(6)]
    at = 6 * rows_part
    whole_joined_bias = (
        small[:, at : at + joined_bias.size]
        .reshape((shards,) + joined_bias.shape)
        .transpose(1, 0, 2)
        .reshape(-1)
    )
    at += joined_bias.size
    whole_inner_bias = (
        small[:, at:].reshape((shards,) + inner_bias.shape).transpose(1, 0, 2).reshape(-1)
    )
    gains = jnp.stack(whole[:4])

    places = jnp.stack([me, ctx]).astype(jnp.int32)
    first_in, second_in, rows, stats = norm_call(places[:1], own_tokens, token_pairs, gains)
    center, inverse = stats[:, 0:1], stats[:, 1:2]
    positions = ctx * local_len + jnp.arange(local_len, dtype=jnp.int32)
    half = ROTARY // 2
    frequency = 1.0 / 10000.0 ** (jnp.arange(half, dtype=F32) * 2.0 / ROTARY)
    angles = positions.astype(F32)[:, None] * frequency[None, :]
    cosine, sine = jnp.cos(angles), jnp.sin(angles)
    ones = jnp.ones((local_len, 128 - ROTARY), F32)
    nothing = jnp.zeros((local_len, half), F32)
    blank = jnp.zeros((local_len, 128 - ROTARY), F32)
    table = jnp.concatenate(
        [cosine, cosine, ones, -sine, nothing, blank, nothing, sine, blank], axis=1
    )
    query, pair = joined_call(first_in, whole_a, whole_joined_bias, table, seqs, heads)
    pairs = share_pairs(pair, "ctx")
    low, odd = ctx - 2, ctx + 1 - 2 * lax.rem(ctx, 2)
    info = jnp.stack([ctx, odd, low, jnp.where(low >= 0, odd - 2, -1), ctx]).astype(jnp.int32)
    upper = dot(second_in, inner, NN) + whole_inner_bias
    active, slope = gelu_parts(upper)
    active = active.astype(BF16)
    context, lse = forward_call(info, lengths, query, pairs, seqs, heads)
    branch = dot(active, outer, NT) + dot(context, output, NT)
    summed = lax.psum_scatter(
        branch.astype(BF16), "tp", scatter_dimension=1, tiled=True
    ).astype(F32)
    own_start = me * part
    own_bias = lax.dynamic_slice_in_dim(whole[4] + whole[5], own_start, part)
    valid = (positions[None, :] < lengths[:, None]).astype(F32).reshape(count, 1)
    layer_out = (valid * (own_tokens.astype(F32) + summed + own_bias)).astype(BF16)

    grad_rows, bias_sums = cot_call(places, lengths, own_cot_late, cot_pairs, local_len)
    bias_grad = bias_sums[0]
    context_grad = dot(grad_rows, output, NN).astype(BF16)
    upper_grad = (dot(grad_rows, outer, NN) * slope).astype(BF16)
    outer_grad = dot(grad_rows, active, TN).astype(BF16)
    inner_grad = dot(second_in, upper_grad, TN).astype(BF16)
    output_grad = dot(grad_rows, context, TN).astype(BF16)
    inner_bias_grad = jnp.sum(upper_grad, axis=0, dtype=F32)
    second_in_grad = dot(upper_grad, inner, NT)
    query_grad, *pair_grads = backward_call(
        info, lengths, query, context, context_grad, lse, pairs, seqs, heads
    )
    sums = return_pairs(pair_grads, "ctx")
    pair_grad = sum(p.astype(F32) for p in sums).reshape(count, heads, 2, HEAD)
    cos_rows = jnp.tile(cosine, (seqs, 1))[:, None, :]
    sin_rows = jnp.tile(sine, (seqs, 1))[:, None, :]

    def turn_back(v):
        front, back = v[..., :half], v[..., half : 2 * half]
        return jnp.concatenate(
            [
                front * cos_rows + back * sin_rows,
                back * cos_rows - front * sin_rows,
                v[..., 2 * half :],
            ],
            axis=-1,
        )

    joined_grad = (
        jnp.stack(
            [
                turn_back(query_grad.astype(F32).reshape(count, heads, HEAD)),
                turn_back(pair_grad[:, :, 0]),
                pair_grad[:, :, 1],
            ],
            axis=2,
        )
        .astype(BF16)
        .reshape(count, joined_width)
    )
    joined_bias_grad = jnp.sum(joined_grad, axis=0, dtype=F32)
    first_in_grad = dot(joined_grad, whole_a[:, :joined_width], NT)
    joined_grad_weight = dot(first_in, joined_grad, TN).astype(BF16)

    normed = (rows.astype(F32) - center) * inverse
    column = jnp.stack(
        [
            jnp.sum(first_in_grad * normed, axis=0),
            jnp.sum(first_in_grad, axis=0),
            jnp.sum(second_in_grad * normed, axis=0),
            jnp.sum(second_in_grad, axis=0),
        ]
    )
    scaled = first_in_grad * whole[0] + second_in_grad * whole[2]
    row_terms = jnp.stack([jnp.sum(scaled, axis=1), jnp.sum(scaled * normed, axis=1)])
    share = lax.psum_scatter(scaled.astype(BF16), "tp", scatter_dimension=1, tiled=True)
    means = lax.psum(row_terms, "tp") / width
    own_normed = (own_tokens.astype(F32) - center) * inverse
    own_rows = lax.dynamic_slice_in_dim(grad_rows, own_start, part, 1).astype(F32)
    tokens_grad = own_rows + inverse * (
        share.astype(F32) - means[0][:, None] - own_normed * means[1][:, None]
    )

    def scatter(v):
        return lax.psum_scatter(v, group, scatter_dimension=0, tiled=True).astype(F32)

    outer_out = scatter(outer_grad)
    inner_out = scatter(inner_grad)
    output_out = scatter(output_grad)
    joined_out = scatter(joined_grad_weight)
    column = lax.psum(column, "tp")
    small_grads = jnp.concatenate(
        [column.reshape(-1), bias_grad, joined_bias_grad, inner_bias_grad]
    )
    small_sums = lax.psum(small_grads, group)
    place = lax.axis_index("fsdp") * lax.axis_size("ctx") + ctx
    vector = lax.dynamic_slice_in_dim(
        small_sums[: 5 * width].reshape(5, width), place * rows_part, rows_part, 1
    )
    joined_bias_out = lax.dynamic_slice_in_dim(
        small_sums[5 * width : 5 * width + joined_width].reshape(heads, 3 * HEAD),
        place * joined_bias.shape[1],
        joined_bias.shape[1],
        1,
    )
    inner_bias_out = lax.dynamic_slice_in_dim(
        small_sums[5 * width + joined_width :].reshape(inner_bias.shape[0], -1),
        place * inner_bias.shape[1],
        inner_bias.shape[1],
        1,
    )
    return (
        layer_out.reshape(tokens.shape),
        tokens_grad.reshape(tokens.shape),
        vector[0],
        vector[1],
        joined_out.reshape(joined_weight.shape),
        joined_bias_out,
        output_out.reshape(output_weight.shape),
        vector[4],
        vector[2],
        vector[3],
        inner_out,
        inner_bias_out,
        outer_out,
        vector[4],
    )


def solution(mesh):
    both = ("fsdp", "ctx")
    return jax.shard_map(
        body,
        mesh=mesh,
        in_specs=(
            P("fsdp", "ctx", "tp"),
            P("fsdp"),
            P("fsdp", "ctx", "tp"),
            P(both),
            P(both),
            P(both, "tp", None),
            P("tp", both),
            P(both, "tp", None),
            P(both),
            P(both),
            P(both),
            P(both, "tp"),
            P("tp", both),
            P(both, "tp"),
            P(both),
        ),
        out_specs=(
            P("fsdp", "ctx", "tp"),
            P("fsdp", "ctx", "tp"),
            P(both),
            P(both),
            P(both, "tp", None),
            P("tp", both),
            P(both, "tp", None),
            P(both),
            P(both),
            P(both),
            P(both, "tp"),
            P("tp", both),
            P(both, "tp"),
            P(both),
        ),
        check_vma=False,
    )
```

```python
import functools

import jax
import jax.numpy as jnp
from jax import lax
from jax.experimental import pallas as pl
from jax.experimental.pallas import tpu as pltpu
from jax.sharding import PartitionSpec as P

HEAD = 256
ROTARY = 64
F32 = jnp.float32
BF16 = jnp.bfloat16
VMEM_LIMIT = 40 << 20
SHARE = 1
NN = (((1,), (0,)), ((), ()))
NT = (((1,), (1,)), ((), ()))
TN = (((0,), (0,)), ((), ()))


def dot(a, b, dims):
    return lax.dot_general(a, b, dims, preferred_element_type=F32)


def after(value, *earlier):
    return lax.optimization_barrier((value, earlier))[0]


def params(*semantics):
    return pltpu.CompilerParams(
        dimension_semantics=semantics or None, vmem_limit_bytes=VMEM_LIMIT
    )


def cost(flops, moved, transcendentals=0):
    return pl.CostEstimate(
        flops=flops // SHARE, bytes_accessed=moved // SHARE, transcendentals=0
    )


def line_gather(piece, axis):
    size = lax.axis_size(axis)
    up = [(i, i + 1) for i in range(size - 1)]
    down = [(i + 1, i) for i in range(size - 1)]
    right, left = [], []
    a = b = piece
    for _ in range(size - 1):
        a = lax.ppermute(a, axis, up)
        b = lax.ppermute(b, axis, down)
        right.append(a)
        left.append(b)
    pairs = [(right[s - 1], left[size - s - 1]) for s in range(1, size)]
    return pairs, list(zip(right, left))


def send_chunks(chunks, axis):
    size = lax.axis_size(axis)
    return [chunks[0]] + [
        lax.ppermute(chunks[k], axis, [(i, (i + k) % size) for i in range(size)])
        for k in range(1, size)
    ]


def norm_kernel(size, me_ref, own, *refs):
    pairs = refs[: 2 * (size - 1)]
    gains, first_out, second_out, token_out, stat_out, work = refs[2 * (size - 1) :]
    part = own.shape[1]
    me = me_ref[0]
    for s in range(size):
        if s == 0:
            piece = own[...].astype(F32)
        else:
            piece = pairs[2 * s - 2][...].astype(F32) + pairs[2 * s - 1][...].astype(F32)
        at = lax.rem(me - s + size, size)
        work[:, pl.ds(pl.multiple_of(at * part, part), part)] = piece
    rows = work[...]
    token_out[...] = rows.astype(BF16)
    width = rows.shape[1]
    center = jnp.sum(rows, axis=1, keepdims=True) * (1.0 / width)
    shifted = rows - center
    inverse = lax.rsqrt(jnp.sum(shifted * shifted, axis=1, keepdims=True) * (1.0 / width) + 1e-05)
    normed = shifted * inverse
    first_out[...] = (normed * gains[0:1, :] + gains[1:2, :]).astype(BF16)
    second_out[...] = (normed * gains[2:3, :] + gains[3:4, :]).astype(BF16)
    lane = lax.broadcasted_iota(jnp.int32, stat_out.shape, 1)
    stat_out[...] = jnp.where(lane == 0, center, inverse)


def norm_call(me, own, pairs, gains, tile=128):
    count, part = own.shape
    size = len(pairs) + 1
    width = part * size
    flat = [p for pair in pairs for p in pair]
    block = pl.BlockSpec((tile, part), lambda i, *_: (i, 0))
    wide = pl.BlockSpec((tile, width), lambda i, *_: (i, 0))
    return pl.pallas_call(
        functools.partial(norm_kernel, size),
        grid_spec=pltpu.PrefetchScalarGridSpec(
            num_scalar_prefetch=1,
            grid=(count // tile,),
            in_specs=[block] * (1 + len(flat)) + [pl.BlockSpec((4, width), lambda i, *_: (0, 0))],
            out_specs=[wide, wide, wide, pl.BlockSpec((tile, 128), lambda i, *_: (i, 0))],
            scratch_shapes=[pltpu.VMEM((tile, width), F32)],
        ),
        out_shape=[
            jax.ShapeDtypeStruct((count, width), BF16),
            jax.ShapeDtypeStruct((count, width), BF16),
            jax.ShapeDtypeStruct((count, width), BF16),
            jax.ShapeDtypeStruct((count, 128), F32),
        ],
        compiler_params=params("arbitrary"),
        cost_estimate=cost(count * width * 16, count * width * 10),
        name="norm",
    )(me, own, *flat, gains)


def cot_kernel(size, local_len, tile, me_ref, len_ref, own, *refs):
    pairs = refs[: 2 * (size - 1)]
    rows_out, sum_out = refs[2 * (size - 1) :]
    part = own.shape[1]
    me, ctx = me_ref[0], me_ref[1]
    step = pl.program_id(0)
    start = step * tile
    seq = start // local_len
    length = len_ref[seq]
    position = ctx * local_len + lax.rem(start, local_len)
    position = position + lax.broadcasted_iota(jnp.int32, (tile, 1), 0)
    keep = position < length

    @pl.when(step == 0)
    def _():
        sum_out[...] = jnp.zeros_like(sum_out)

    for s in range(size):
        if s == 0:
            piece = own[...].astype(F32)
        else:
            piece = pairs[2 * s - 2][...].astype(F32) + pairs[2 * s - 1][...].astype(F32)
        piece = jnp.where(keep, piece, 0.0)
        at = lax.rem(me - s + size, size)
        cols = pl.ds(pl.multiple_of(at * part, part), part)
        rows_out[:, cols] = piece.astype(BF16)
        sum_out[0:1, cols] += jnp.sum(piece, axis=0, keepdims=True)


def cot_call(places, lengths, own, pairs, local_len, tile=256):
    count, part = own.shape
    size = len(pairs) + 1
    width = part * size
    flat = [p for pair in pairs for p in pair]
    block = pl.BlockSpec((tile, part), lambda i, *_: (i, 0))
    return pl.pallas_call(
        functools.partial(cot_kernel, size, local_len, tile),
        grid_spec=pltpu.PrefetchScalarGridSpec(
            num_scalar_prefetch=2,
            grid=(count // tile,),
            in_specs=[block] * (1 + len(flat)),
            out_specs=[
                pl.BlockSpec((tile, width), lambda i, *_: (i, 0)),
                pl.BlockSpec((8, width), lambda i, *_: (0, 0)),
            ],
        ),
        out_shape=[
            jax.ShapeDtypeStruct((count, width), BF16),
            jax.ShapeDtypeStruct((8, width), F32),
        ],
        compiler_params=params("arbitrary"),
        cost_estimate=cost(count * width * 4, count * width * 6),
        name="cotangent_rows",
    )(places, lengths, own, *flat)


def flat_rows(ref):
    value = ref[...]
    return value.reshape(value.shape[0] * value.shape[1], value.shape[2])


def joined_kernel(seqs, rows_ref, weight_ref, bias_ref, table_ref, query_ref, pair_ref):
    kind = lax.rem(pl.program_id(0), 3)
    out = dot(rows_ref[...], flat_rows(weight_ref), NN) + bias_ref[0:1, :]
    local_len = out.shape[0] // seqs

    def turned():
        front = out[:, :128]
        up = pltpu.roll(front, 128 - ROTARY // 2, 1)
        down = pltpu.roll(front, ROTARY // 2, 1)
        table = table_ref[...]
        if seqs > 1:
            table = jnp.concatenate([table] * seqs, axis=0)
        front = front * table[:, :128] + up * table[:, 128:256] + down * table[:, 256:]
        return jnp.concatenate([front, out[:, 128:]], axis=1)

    @pl.when(kind == 0)
    def _():
        query_ref[...] = (turned().astype(BF16).astype(F32) * HEAD ** (-0.5)).astype(BF16)

    @pl.when(kind == 1)
    def _():
        value = turned().astype(BF16)
        for s in range(seqs):
            pair_ref[s] = value[s * local_len : (s + 1) * local_len, :]

    @pl.when(kind == 2)
    def _():
        value = out.astype(BF16)
        for s in range(seqs):
            pair_ref[s] = value[s * local_len : (s + 1) * local_len, :]


def joined_call(rows, pack, bias, table, seqs, heads):
    count, width = rows.shape
    shards = pack.shape[0]
    local_len = count // seqs
    return pl.pallas_call(
        functools.partial(joined_kernel, seqs),
        grid=(3 * heads,),
        in_specs=[
            pl.BlockSpec((count, width), lambda j: (0, 0)),
            pl.BlockSpec((shards, width // shards, HEAD), lambda j: (0, 0, j)),
            pl.BlockSpec((8, HEAD), lambda j: (0, j)),
            pl.BlockSpec(table.shape, lambda j: (0, 0)),
        ],
        out_specs=[
            pl.BlockSpec((count, HEAD), lambda j: (0, j // 3)),
        ]
        + [
            pl.BlockSpec(
                (seqs, local_len, HEAD), lambda j: (0, 0, 2 * (j // 3) + (j % 3) // 2)
            )
        ],
        out_shape=[
            jax.ShapeDtypeStruct((count, heads * HEAD), BF16),
            jax.ShapeDtypeStruct((seqs, local_len, 2 * heads * HEAD), BF16),
        ],
        compiler_params=params("arbitrary"),
        cost_estimate=cost(6 * heads * HEAD * count * width, 2 * (count + 3 * heads * HEAD) * width),
        name="joined",
    )(rows, pack, jnp.broadcast_to(bias.reshape(1, -1), (8, bias.size)), table)


def visit(slot, local_len, half, block, place, length):
    first_key = block * local_len
    last_query = place * local_len + (half + 1) * (local_len // 2) - 1
    return (block >= 0) & (first_key <= last_query) & (first_key < length)


def masked(scores, first_key, first_query, length, axis_key):
    shape = scores.shape
    key = first_key + lax.broadcasted_iota(jnp.int32, shape, axis_key)
    query = first_query + lax.broadcasted_iota(jnp.int32, shape, 1 - axis_key)
    return (key <= query) & (key < length)


SLOTS = 4


def slot_refs(own_ref, below_ref, both_ref):
    return [own_ref, below_ref, both_ref.at[0], both_ref.at[1]]


def forward_kernel(slots, local_len, seq, info, lens, query_ref, pair_ref, *refs):
    context_ref, lse_ref, top, total, acc = refs
    length = lens[seq]
    place = info[slots]
    top[...] = jnp.full_like(top, -1e30)
    total[...] = jnp.zeros_like(total)
    acc[...] = jnp.zeros_like(acc)
    query = query_ref[...]
    for slot in range(slots):
        block = info[slot]
        first_key = block * local_len

        @pl.when((block >= 0) & (block <= place) & (first_key < length))
        def _():
            keys = pair_ref[block, :, :HEAD]
            vals = pair_ref[block, :, HEAD:]
            scores = dot(query, keys, NT)
            ok = masked(scores, first_key, place * local_len, length, 1)
            scores = jnp.where(ok, scores, -1e30)
            best = jnp.maximum(top[...], jnp.max(scores, axis=1, keepdims=True))
            scale = jnp.exp(top[...] - best)
            weights = jnp.exp(scores - best[:, :1])
            weights = jnp.where(ok, weights, 0.0)
            total[...] = total[...] * scale + jnp.sum(weights, axis=1, keepdims=True)
            acc[...] = acc[...] * scale[:, :1] + dot(weights.astype(BF16), vals, NN)
            top[...] = best

    context_ref[...] = (acc[...] / total[:, :1]).astype(BF16)
    lse_ref[...] = top[...] + jnp.log(total[...])


def forward_call(info, lengths, query, pairs, seq, heads):
    local_len = pairs.shape[2]
    slots = SLOTS
    return pl.pallas_call(
        functools.partial(forward_kernel, slots, local_len, seq),
        grid_spec=pltpu.PrefetchScalarGridSpec(
            num_scalar_prefetch=2,
            grid=(heads,),
            in_specs=[pl.BlockSpec((local_len, HEAD), lambda h, *_: (seq, h))]
            + [pl.BlockSpec((slots, None, local_len, 2 * HEAD), lambda h, *_: (0, seq, 0, h))],
            out_specs=[
                pl.BlockSpec((local_len, HEAD), lambda h, *_: (0, h)),
                pl.BlockSpec((local_len, 128), lambda h, *_: (0, h)),
            ],
            scratch_shapes=[
                pltpu.VMEM((local_len, 128), F32),
                pltpu.VMEM((local_len, 128), F32),
                pltpu.VMEM((local_len, HEAD), F32),
            ],
        ),
        out_shape=[
            jax.ShapeDtypeStruct((local_len, heads * HEAD), BF16),
            jax.ShapeDtypeStruct((local_len, heads * 128), F32),
        ],
        compiler_params=params("arbitrary"),
        cost_estimate=cost(
            4 * local_len * heads * HEAD * local_len * slots,
            4 * local_len * heads * HEAD * slots,
        ),
        name="attention_forward",
    )(info, lengths, query, pairs)


def backward_kernel(
    slots, local_len, seq, info, lens, query_ref, context_ref, grad_ref, lse_ref, pair_ref, *refs
):
    query_out = refs[0]
    pair_outs = slot_refs(*refs[1:4])
    acc = refs[4]
    length = lens[seq]
    place = info[slots]
    query = query_ref[...]
    grad = grad_ref[...]
    lse = lse_ref[:, :1]
    shared = jnp.sum(grad.astype(F32) * context_ref[...].astype(F32), axis=1, keepdims=True)
    acc[...] = jnp.zeros_like(acc)
    for slot in range(slots):
        block = info[slot]
        first_key = block * local_len
        seen = (block >= 0) & (block <= place) & (first_key < length)

        @pl.when(seen)
        def _():
            keys = pair_ref[block, :, :HEAD]
            vals = pair_ref[block, :, HEAD:]
            scores = dot(query, keys, NT)
            ok = masked(scores, first_key, place * local_len, length, 1)
            probs = jnp.where(ok, jnp.exp(scores - lse), 0.0)
            prob_grad = dot(grad, vals, NT)
            score_grad = (probs * (prob_grad - shared)).astype(BF16)
            acc[...] += dot(score_grad, keys, NN)
            pair_outs[slot][:, :HEAD] = dot(score_grad, query, TN).astype(BF16)
            pair_outs[slot][:, HEAD:] = dot(probs.astype(BF16), grad, TN).astype(BF16)

        @pl.when(jnp.logical_not(seen))
        def _():
            pair_outs[slot][...] = jnp.zeros_like(pair_outs[slot])

    query_out[...] = (acc[...] * HEAD ** (-0.5)).astype(BF16)


def backward_call(info, lengths, query, context, grad, lse, pairs, seq, heads):
    local_len = pairs.shape[2]
    slots = SLOTS
    here = pl.BlockSpec((local_len, HEAD), lambda h, *_: (seq, h))
    one = pl.BlockSpec((local_len, HEAD), lambda h, *_: (0, h))
    two = [pl.BlockSpec((local_len, 2 * HEAD), lambda h, *_: (0, h))] * 2
    two = two + [pl.BlockSpec((2, local_len, 2 * HEAD), lambda h, *_: (0, 0, h))]
    return pl.pallas_call(
        functools.partial(backward_kernel, slots, local_len, seq),
        grid_spec=pltpu.PrefetchScalarGridSpec(
            num_scalar_prefetch=2,
            grid=(heads,),
            in_specs=[here, one, here, pl.BlockSpec((local_len, 128), lambda h, *_: (0, h))]
            + [pl.BlockSpec((slots, None, local_len, 2 * HEAD), lambda h, *_: (0, seq, 0, h))],
            out_specs=[one] + two,
            scratch_shapes=[pltpu.VMEM((local_len, HEAD), F32)],
        ),
        out_shape=[jax.ShapeDtypeStruct((local_len, heads * HEAD), BF16)]
        + [jax.ShapeDtypeStruct((local_len, 2 * heads * HEAD), BF16)] * 2
        + [jax.ShapeDtypeStruct((2, local_len, 2 * heads * HEAD), BF16)],
        compiler_params=params("arbitrary"),
        cost_estimate=cost(
            10 * local_len * heads * HEAD * local_len * slots,
            8 * local_len * heads * HEAD * slots,
        ),
        name="attention_backward",
    )(info, lengths, query, context, grad, lse, pairs)


def return_pairs(own, below, siblings, axis):
    taken = lax.ppermute(siblings, axis, [(0, 1), (1, 0), (2, 3), (3, 2)])
    lower = (below.astype(F32) + taken[1].astype(F32)).astype(BF16)
    above = lax.ppermute(lower, axis, [(2, 0), (3, 1)])
    return [own, taken, above], taken


def branch_kernel(parts, active_ref, *refs):
    context_refs, (outer_ref, output_ref, out_ref) = refs[:parts], refs[parts:]
    out = dot(active_ref[...], outer_ref[...], NT)
    context = jnp.concatenate([ref[...] for ref in context_refs], axis=0)
    out_ref[...] = (out + dot(context, flat_rows(output_ref), NT)).astype(BF16)


def branch_call(active, contexts, outer, pack, column, tile=512):
    count, hidden = active.shape
    width, inside = outer.shape[0], contexts[0].shape[1]
    rows = width // pack.shape[0]
    return pl.pallas_call(
        functools.partial(branch_kernel, len(contexts)),
        grid=(width // tile,),
        in_specs=[pl.BlockSpec((count, hidden), lambda j: (0, 0))]
        + [pl.BlockSpec(c.shape, lambda j: (0, 0)) for c in contexts]
        + [
            pl.BlockSpec((tile, hidden), lambda j: (j, 0)),
            pl.BlockSpec((tile // rows, rows, inside), lambda j: (j, 0, column)),
        ],
        out_specs=pl.BlockSpec((count, tile), lambda j: (0, j)),
        out_shape=jax.ShapeDtypeStruct((count, width), BF16),
        compiler_params=params("arbitrary"),
        cost_estimate=cost(2 * count * width * (hidden + inside), 2 * width * (hidden + inside)),
        name="branch",
    )(active, *contexts, outer, pack)


def upper_kernel(rows_ref, weight_ref, bias_ref, active_ref, slope_ref):
    weight = flat_rows(weight_ref)
    bias = bias_ref[0:1, :]
    count = rows_ref.shape[0]
    piece = count // 4
    for i in range(4):
        here = slice(i * piece, (i + 1) * piece)
        upper = dot(rows_ref[here, :], weight, NN) + bias
        phi = 0.5 * (1.0 + lax.erf(upper * 0.7071067811865476))
        slope = phi + upper * jnp.exp(-0.5 * upper * upper) * 0.3989422804014327
        active_ref[here, :] = (upper * phi).astype(BF16)
        slope_ref[here, :] = slope.astype(BF16)


def upper_call(rows, pack, bias, column, tile=512):
    count, width = rows.shape
    hidden = bias.size
    shards = pack.shape[0]
    out = pl.BlockSpec((count, tile), lambda j: (0, j))
    first = column // tile
    return pl.pallas_call(
        upper_kernel,
        grid=(hidden // tile,),
        in_specs=[
            pl.BlockSpec((count, width), lambda j: (0, 0)),
            pl.BlockSpec((shards, width // shards, tile), lambda j: (0, 0, first + j)),
            pl.BlockSpec((8, tile), lambda j: (0, j)),
        ],
        out_specs=[out, out],
        out_shape=[jax.ShapeDtypeStruct((count, hidden), BF16)] * 2,
        compiler_params=params("arbitrary"),
        cost_estimate=cost(2 * count * width * hidden, 2 * width * (count + hidden)),
        name="upper",
    )(rows, pack, jnp.broadcast_to(bias.reshape(1, -1), (8, hidden)))


def context_grad_kernel(rows_ref, weight_ref, out_ref):
    out_ref[...] = dot(rows_ref[...], flat_rows(weight_ref), NN).astype(BF16)


def context_grad_call(rows, pack, column, inside, tile=512):
    count, width = rows.shape
    return pl.pallas_call(
        context_grad_kernel,
        grid=(count // tile,),
        in_specs=[
            pl.BlockSpec((tile, width), lambda i: (i, 0)),
            pl.BlockSpec(
                (pack.shape[0], width // pack.shape[0], inside), lambda i: (0, 0, column)
            ),
        ],
        out_specs=pl.BlockSpec((tile, inside), lambda i: (i, 0)),
        out_shape=jax.ShapeDtypeStruct((count, inside), BF16),
        compiler_params=params("arbitrary"),
        cost_estimate=cost(2 * count * width * inside, 2 * width * (count + inside)),
        name="context_grad",
    )(rows, pack)


def column_sums(grad, normed, out_ref):
    count, tile = grad.shape
    out_ref[0:1, :] = jnp.sum(grad * normed, axis=0, keepdims=True)
    out_ref[1:2, :] = jnp.sum(grad, axis=0, keepdims=True)
    out_ref[2:8, :] = jnp.zeros((6, tile), F32)


def second_kernel(grad_ref, weight_ref, rows_ref, stat_ref, gain_ref, out_ref, sum_ref):
    grad = dot(grad_ref[...], flat_rows(weight_ref), NT)
    normed = (rows_ref[...].astype(F32) - stat_ref[:, 0:1]) * stat_ref[:, 1:2]
    column_sums(grad, normed, sum_ref)
    out_ref[...] = (grad * gain_ref[2:3, :]).astype(BF16)


def second_call(grad, pack, column, rows, stats, gains, tile=512):
    count, hidden = grad.shape
    width = rows.shape[1]
    deep = width // pack.shape[0]
    return pl.pallas_call(
        second_kernel,
        grid=(width // tile,),
        in_specs=[
            pl.BlockSpec((count, hidden), lambda j: (0, 0)),
            pl.BlockSpec((tile // deep, deep, hidden), lambda j: (j, 0, column)),
            pl.BlockSpec((count, tile), lambda j: (0, j)),
            pl.BlockSpec((count, 128), lambda j: (0, 0)),
            pl.BlockSpec((4, tile), lambda j: (0, j)),
        ],
        out_specs=[
            pl.BlockSpec((count, tile), lambda j: (0, j)),
            pl.BlockSpec((8, tile), lambda j: (0, j)),
        ],
        out_shape=[
            jax.ShapeDtypeStruct((count, width), BF16),
            jax.ShapeDtypeStruct((8, width), F32),
        ],
        compiler_params=params("arbitrary"),
        cost_estimate=cost(2 * count * width * hidden, 2 * (width * hidden + 3 * count * width)),
        name="second_in_grad",
    )(grad, pack, rows, stats, gains)


def joined_grad_kernel(heads, *refs):
    (table_ref, out_ref, sum_ref), refs = refs[-3:], refs[:-3]
    table = table_ref[...]
    local_len = table.shape[0]

    def back(value):
        front = value[:, :128]
        up = pltpu.roll(front, 128 - ROTARY // 2, 1)
        down = pltpu.roll(front, ROTARY // 2, 1)
        front = front * table[:, :128] - up * table[:, 128:256] - down * table[:, 256:]
        return jnp.concatenate([front, value[:, 128:]], axis=1)

    sum_ref[...] = jnp.zeros_like(sum_ref)
    for seq in range(len(refs) // 4):
        query_ref, own_ref, near_ref, far_ref = refs[4 * seq : 4 * seq + 4]
        here = slice(seq * local_len, (seq + 1) * local_len)
        for head in range(heads):
            at = 3 * HEAD * head
            pair = slice(2 * HEAD * head, 2 * HEAD * (head + 1))
            total = own_ref[:, pair].astype(F32) + near_ref[0, :, pair].astype(F32)
            total = total + far_ref[:, pair].astype(F32)
            query = query_ref[:, HEAD * head : HEAD * (head + 1)].astype(F32)
            parts = [back(query), back(total[:, :HEAD]), total[:, HEAD:]]
            for i, part in enumerate(parts):
                cols = slice(at + HEAD * i, at + HEAD * (i + 1))
                low = part.astype(BF16)
                out_ref[here, cols] = low
                sum_ref[0:1, cols] += jnp.sum(low.astype(F32), axis=0, keepdims=True)


def joined_grad_call(queries, sums, table, heads):
    seqs = len(queries)
    count = seqs * queries[0].shape[0]
    width = 3 * heads * HEAD
    flat = [a for query, three in zip(queries, sums) for a in (query, *three)]
    return pl.pallas_call(
        functools.partial(joined_grad_kernel, heads),
        out_shape=[
            jax.ShapeDtypeStruct((count, width), BF16),
            jax.ShapeDtypeStruct((8, width), F32),
        ],
        compiler_params=params(),
        cost_estimate=cost(10 * count * width, 10 * count * width),
        name="joined_grad",
    )(*flat, table)


EXTRA = 8


def first_kernel(ranks, order, grad_ref, weight_ref, rows_ref, stat_ref, gain_ref, second_ref, *refs):
    out_refs, (sum_ref, row_ref) = refs[:ranks], refs[ranks:]
    step = pl.program_id(0)
    grad = dot(grad_ref[...], flat_rows(weight_ref), NT)
    count, tile = grad.shape
    normed = (rows_ref[...].astype(F32) - stat_ref[:, 0:1]) * stat_ref[:, 1:2]
    column_sums(grad, normed, sum_ref)
    total = grad * gain_ref[0:1, :] + second_ref[...].astype(F32)
    low = total.astype(BF16)
    for k in range(ranks):

        @pl.when(step == k)
        def _():
            out_refs[k][:count, :] = low

    plain = jnp.sum(total, axis=1, keepdims=True)
    along = jnp.sum(total * normed, axis=1, keepdims=True)
    lane = lax.broadcasted_iota(jnp.int32, row_ref.shape, 1)
    both = jnp.where(lane == 0, plain, along)

    @pl.when(step == 0)
    def _():
        row_ref[...] = both

    @pl.when(step > 0)
    def _():
        row_ref[...] += both

    @pl.when(step == ranks - 1)
    def _():
        turned = row_ref[...].T
        lines = [turned[i : i + 1, j : j + tile] for i in (0, 1) for j in range(0, count, tile)]
        lines.append(jnp.zeros((EXTRA - len(lines), tile), F32))
        extra = jnp.concatenate(lines, axis=0).astype(BF16)
        for ref in out_refs:
            ref[count:, :] = extra


def first_call(order, grad, pack, rows, stats, gains, second, ranks):
    count, inside = grad.shape
    width = rows.shape[1]
    tile = width // ranks
    deep = width // pack.shape[0]
    return pl.pallas_call(
        functools.partial(first_kernel, ranks),
        grid_spec=pltpu.PrefetchScalarGridSpec(
            num_scalar_prefetch=1,
            grid=(ranks,),
            in_specs=[
                pl.BlockSpec((count, inside), lambda j, _: (0, 0)),
                pl.BlockSpec((tile // deep, deep, inside), lambda j, order: (order[j], 0, 0)),
                pl.BlockSpec((count, tile), lambda j, order: (0, order[j])),
                pl.BlockSpec((count, 128), lambda j, _: (0, 0)),
                pl.BlockSpec((4, tile), lambda j, order: (0, order[j])),
                pl.BlockSpec((count, tile), lambda j, order: (0, order[j])),
            ],
            out_specs=[pl.BlockSpec((count + EXTRA, tile), lambda j, _: (0, 0))] * ranks
            + [pl.BlockSpec((8, tile), lambda j, order: (0, order[j]))],
            scratch_shapes=[pltpu.VMEM((count, 128), F32)],
        ),
        out_shape=[jax.ShapeDtypeStruct((count + EXTRA, tile), BF16)] * ranks
        + [jax.ShapeDtypeStruct((8, width), F32)],
        compiler_params=params("arbitrary"),
        cost_estimate=cost(2 * count * width * inside, 2 * (width * inside + 4 * count * width)),
        name="first_in_grad",
    )(order, grad, pack, rows, stats, gains, second)


def flips(size, by):
    return [(i, i ^ by) for i in range(size)]


def paired(group):
    return lax.axis_size(group[0]) == 2 and lax.axis_size(group[1]) == 4


def member(group):
    return lax.axis_size(group[1]) * lax.axis_index(group[0]) + lax.axis_index(group[1])


def gather_small(vector, group):
    if not paired(group):
        return lax.all_gather(vector.reshape(1, 1, -1), group, axis=0, tiled=True)[:, 0]
    rows = jnp.zeros((8, vector.size), vector.dtype)
    rows = lax.dynamic_update_slice_in_dim(rows, vector.reshape(1, -1), member(group), 0)
    for by in (1, 2, 4):
        rows = rows + lax.ppermute(rows, group, flips(8, by))
    return rows


def weight_grad_kernel(sizes, outs, small, order, *refs):
    parts = len(sizes)
    lhs_refs, rhs_refs, refs = refs[: 4 * parts], refs[4 * parts : 5 * parts], refs[5 * parts :]
    small_ref = refs[0] if small else None
    add_ref = refs[small] if outs > 1 else None
    out_refs, turned = refs[-1 - outs : -1], refs[-1]
    rows = lhs_refs[0].shape[1]
    deep = rows + EXTRA * small
    step = pl.program_id(0)

    def put(k, value, start):
        height = value.shape[0]
        if outs == 1:
            out_refs[0][k * deep + start : k * deep + start + height, :] = value.astype(BF16)
        else:
            add = add_ref[k * deep + start : k * deep + start + height, :].astype(F32)
            out_refs[k][start : start + height, :] = (value + add).astype(BF16)

    first = 0
    for i, size in enumerate(sizes):
        lhs, rhs_ref = lhs_refs[4 * i : 4 * i + 4], rhs_refs[i]

        @pl.when(step == first)
        def _():
            for k in range(4):
                turned[k * rows : (k + 1) * rows, :] = lhs[k][...].T

        @pl.when((step >= first) & (step < first + size))
        def _():
            out = dot(turned[...], rhs_ref[...], NN)
            for k in range(4):
                put(k, out[k * rows : (k + 1) * rows, :], 0)

        first += size
    if small:
        for k in range(4):
            put(k, small_ref[order[k]], rows)


def weight_grad_call(order, pairs, add=None, small=None, tile=512):
    count, width = pairs[0][0].shape
    rows = width // 8
    sizes = [rhs.shape[1] // tile for _, rhs in pairs]
    total = sum(sizes) * tile
    outs = 1 if add is None else 4
    height = rows if small is None else rows + EXTRA
    deep = 4 * height if add is None else height
    firsts = [sum(sizes[:i]) for i in range(len(sizes))]

    def column(k):
        return pl.BlockSpec((count, rows), lambda j, order: (0, order[k]))

    def piece(first, size):
        return pl.BlockSpec(
            (count, tile), lambda j, _: (0, jnp.minimum(jnp.maximum(j - first, 0), size - 1))
        )

    out = pl.BlockSpec((deep, tile), lambda j, *_: (0, j))
    extra_specs, extra = [], []
    if small is not None:
        extra_specs.append(pl.BlockSpec((8, EXTRA, tile), lambda j, *_: (0, 0, j)))
        extra.append(small)
    if add is not None:
        extra_specs.append(pl.BlockSpec((4 * height, tile), lambda j, *_: (0, j)))
        extra.append(add)
    return pl.pallas_call(
        functools.partial(weight_grad_kernel, sizes, outs, int(small is not None)),
        grid_spec=pltpu.PrefetchScalarGridSpec(
            num_scalar_prefetch=1,
            grid=(sum(sizes),),
            in_specs=[column(k) for _ in pairs for k in range(4)]
            + [piece(f, n) for f, n in zip(firsts, sizes)]
            + extra_specs,
            out_specs=[out] * outs,
            scratch_shapes=[pltpu.VMEM((4 * rows, count), BF16)],
        ),
        out_shape=[jax.ShapeDtypeStruct((deep, total), BF16)] * outs,
        compiler_params=params("arbitrary"),
        cost_estimate=cost(
            8 * rows * count * total, 2 * (count * (4 * rows + total) + 8 * rows * total)
        ),
        name="weight_grad",
    )(
        order,
        *[lhs for lhs, _ in pairs for _ in range(4)],
        *[rhs for _, rhs in pairs],
        *extra,
    )


def product_kernel(sizes, *refs):
    parts = len(sizes)
    lhs_refs, rhs_refs = refs[:parts], refs[parts : 2 * parts]
    out_ref, turned = refs[2 * parts :]
    step = pl.program_id(0)
    first = 0
    for lhs_ref, rhs_ref, size in zip(lhs_refs, rhs_refs, sizes):

        @pl.when(step == first)
        def _():
            turned[...] = lhs_ref[...].T

        @pl.when((step >= first) & (step < first + size))
        def _():
            out_ref[...] = dot(turned[...], rhs_ref[...], NN).astype(BF16)

        first += size


def product_call(pairs, tile=512):
    count, width = pairs[0][0].shape
    sizes = [rhs.shape[1] // tile for _, rhs in pairs]
    total = sum(sizes) * tile
    firsts = [sum(sizes[:i]) for i in range(len(sizes))]

    def piece(first, size):
        return pl.BlockSpec(
            (count, tile), lambda j: (0, jnp.minimum(jnp.maximum(j - first, 0), size - 1))
        )

    return pl.pallas_call(
        functools.partial(product_kernel, sizes),
        grid=(sum(sizes),),
        in_specs=[pl.BlockSpec((count, width), lambda j: (0, 0)) for _ in pairs]
        + [piece(f, n) for f, n in zip(firsts, sizes)],
        out_specs=pl.BlockSpec((width, tile), lambda j: (0, j)),
        out_shape=jax.ShapeDtypeStruct((width, total), BF16),
        scratch_shapes=[pltpu.VMEM((width, count), BF16)],
        compiler_params=params("arbitrary"),
        cost_estimate=cost(2 * width * count * total, 2 * (count * (width + total) + width * total)),
        name="product",
    )(*[lhs for lhs, _ in pairs], *[rhs for _, rhs in pairs])


STEPS = (0, 2, 4, 6)


def weight_grad_given(pairs, group, small=None):
    if not paired(group):
        return None
    steps = jnp.array(STEPS, jnp.int32)
    (given,) = weight_grad_call((member(group) ^ 1) ^ steps, pairs, small=small)
    return given


def weight_grad_kept(pairs, given, group, small=None):
    if not paired(group):
        whole = jnp.concatenate([dot(lhs, rhs, TN).astype(BF16) for lhs, rhs in pairs], axis=1)
        return [lax.psum_scatter(whole, group, scatter_dimension=0, tiled=True)]
    taken = lax.ppermute(given, group, flips(8, 1))
    sums = weight_grad_call(
        member(group) ^ jnp.array(STEPS, jnp.int32), pairs, taken, small=small
    )
    return [sums[0]] + [
        lax.ppermute(part, group, flips(8, by)) for part, by in zip(sums[1:], STEPS[1:])
    ]


def total_of(terms):
    return functools.reduce(lambda a, b: a + b, [t.astype(F32) for t in terms])


def line_sum(value, axis):
    size = lax.axis_size(axis)
    terms = [value]
    for step in range(1, size):
        terms.append(lax.ppermute(value, axis, [(i, (i + step) % size) for i in range(size)]))
    return functools.reduce(lambda a, b: a + b, terms)


def body(
    tokens,
    lengths,
    cotangent,
    first_gain,
    first_shift,
    joined_weight,
    joined_bias,
    output_weight,
    output_bias,
    second_gain,
    second_shift,
    inner_weight,
    inner_bias,
    outer_weight,
    outer_bias,
):
    group = ("fsdp", "ctx")
    seqs, local_len, part = tokens.shape
    count = seqs * local_len
    ranks = lax.axis_size("tp")
    width = part * ranks
    shards = lax.axis_size("fsdp") * lax.axis_size("ctx")
    rows_part = width // shards
    heads = joined_weight.shape[1]
    hidden = inner_weight.shape[1]
    me, ctx = lax.axis_index("tp"), lax.axis_index("ctx")

    own_tokens, own_cot = tokens.reshape(count, part), cotangent.reshape(count, part)
    joined_width, inside = heads * 3 * HEAD, heads * HEAD
    vectors = [first_gain, first_shift, second_gain, second_shift, output_bias, outer_bias]
    flat = jnp.concatenate(vectors + [joined_bias.reshape(-1), inner_bias.reshape(-1)])
    small = gather_small(jnp.pad(flat, (0, -flat.size % 256)), group)
    shard = jnp.concatenate(
        [joined_weight.reshape(rows_part, -1), output_weight.reshape(rows_part, -1), inner_weight],
        axis=1,
    )
    token_pairs, _ = line_gather(own_tokens, "tp")
    cot_pairs, cot_steps = line_gather(after(own_cot, token_pairs), "tp")
    pack = lax.all_gather(shard, group, axis=0, tiled=False)

    small = small.astype(F32)
    whole = [small[:, i * rows_part : (i + 1) * rows_part].reshape(width) for i in range(6)]
    at = 6 * rows_part
    whole_joined_bias = (
        small[:, at : at + joined_bias.size]
        .reshape((shards,) + joined_bias.shape)
        .transpose(1, 0, 2)
        .reshape(-1)
    )
    at += joined_bias.size
    whole_inner_bias = (
        small[:, at : at + inner_bias.size]
        .reshape((shards,) + inner_bias.shape)
        .transpose(1, 0, 2)
        .reshape(-1)
    )
    gains = jnp.stack(whole[:4])

    places = jnp.stack([me, ctx]).astype(jnp.int32)
    first_in, second_in, rows, stats = norm_call(places[:1], own_tokens, token_pairs, gains)
    center, inverse = stats[:, 0:1], stats[:, 1:2]
    positions = ctx * local_len + jnp.arange(local_len, dtype=jnp.int32)
    half = ROTARY // 2
    frequency = 1.0 / 10000.0 ** (jnp.arange(half, dtype=F32) * 2.0 / ROTARY)
    angles = positions.astype(F32)[:, None] * frequency[None, :]
    cosine, sine = jnp.cos(angles), jnp.sin(angles)
    ones = jnp.ones((local_len, 128 - ROTARY), F32)
    nothing = jnp.zeros((local_len, half), F32)
    blank = jnp.zeros((local_len, 128 - ROTARY), F32)
    table = jnp.concatenate(
        [cosine, cosine, ones, -sine, nothing, blank, nothing, sine, blank], axis=1
    )
    query, pair = joined_call(after(first_in, cot_steps[0]), pack, whole_joined_bias, table, seqs, heads)
    pairs = lax.all_gather(pair, "ctx", axis=0, tiled=False)
    low, odd = ctx - 2, ctx + 1 - 2 * lax.rem(ctx, 2)
    info = jnp.stack([ctx, low, odd, jnp.where(low >= 0, odd - 2, -1), ctx]).astype(jnp.int32)
    active, slope = upper_call(
        after(second_in, query, cot_steps[1:]), pack, whole_inner_bias, joined_width + inside
    )
    outer = lax.all_gather(after(outer_weight, active, pairs), group, axis=0, tiled=True)
    contexts, lses = [], []
    ready = after(query, active)
    for seq in range(seqs):
        context, lse = forward_call(info, lengths, ready, pairs, seq, heads)
        ready = after(query, context)
        contexts.append(context)
        lses.append(lse)

    grad_rows, bias_sums = cot_call(places, after(lengths, context), own_cot, cot_pairs, local_len)
    bias_grad = bias_sums[0]
    context_grad = context_grad_call(grad_rows, pack, joined_width // inside, inside)
    queries, sums = [], []
    for seq in range(seqs):
        query_grad, *pair_grads = backward_call(
            info, lengths, ready, contexts[seq], context_grad, lses[seq], pairs, seq, heads
        )
        ready = after(query, query_grad)
        queries.append(query_grad)
        three, taken = return_pairs(*pair_grads, "ctx")
        ready = after(ready, taken)
        sums.append(three)
    branch = branch_call(
        after(active, query_grad, taken), contexts, outer, pack, joined_width // inside
    )
    summed = lax.psum_scatter(branch, "tp", scatter_dimension=1, tiled=True).astype(F32)
    own_start = me * part
    own_bias = lax.dynamic_slice_in_dim(whole[4] + whole[5], own_start, part)
    valid = (positions[None, :] < lengths[:, None]).astype(F32).reshape(count, 1)
    layer_out = (valid * (own_tokens.astype(F32) + summed + own_bias)).astype(BF16)

    grad_late = after(grad_rows, branch)
    upper_grad = (dot(grad_late, outer, NN) * slope.astype(F32)).astype(BF16)
    inner_bias_grad = jnp.sum(upper_grad, axis=0, dtype=F32)
    feed = product_call([(after(grad_late, upper_grad), active), (second_in, upper_grad)])
    feed_out = lax.psum_scatter(feed, group, scatter_dimension=0, tiled=True)
    second_scaled, second_sums = second_call(
        after(upper_grad, feed),
        pack,
        (joined_width + inside) // hidden,
        rows,
        stats,
        gains,
    )
    joined_grad, joined_sums = joined_grad_call(
        after(queries, second_scaled), sums, table, heads
    )
    joined_bias_grad = joined_sums[0]
    order = lax.rem(me + jnp.arange(ranks, dtype=jnp.int32), ranks)
    *scaled, first_sums = first_call(
        order, joined_grad, pack, rows, stats, gains, second_scaled, ranks
    )

    column = jnp.concatenate([first_sums[:2], second_sums[:2], bias_grad.reshape(1, -1)])
    by_shard = [
        column.reshape(5, shards, rows_part).transpose(1, 0, 2).reshape(shards, -1),
        joined_bias_grad.reshape(heads, shards, -1).transpose(1, 0, 2).reshape(shards, -1),
        inner_bias_grad.reshape(-1, shards, inner_bias.shape[1])
        .transpose(1, 0, 2)
        .reshape(shards, -1),
    ]
    small_grads = jnp.concatenate(by_shard, axis=1)
    size = joined_width + inside
    riders = None
    if paired(group):
        riders = jnp.pad(
            small_grads.astype(BF16)[:, None, :],
            ((0, 0), (0, EXTRA - 1), (0, size - small_grads.shape[1])),
        )
    context = jnp.concatenate(contexts, axis=0)
    head_pairs = [(after(first_in, scaled[0]), joined_grad), (grad_rows, context)]
    head_given = weight_grad_given(head_pairs, group, riders)
    head_pairs = [(after(first_in, head_given), joined_grad), (grad_rows, context)]
    head_terms = weight_grad_kept(head_pairs, head_given, group, riders)
    head_out, feed_out = total_of(head_terms), feed_out.astype(F32)
    if riders is None:
        small_out = lax.psum_scatter(small_grads, group, scatter_dimension=0, tiled=True)[0]
    else:
        small_out = head_out[rows_part]
    vector = line_sum(small_out[: 4 * rows_part].reshape(-1, 128), "tp").reshape(4, -1)
    at = 5 * rows_part
    joined_bias_out = small_out[at : at + joined_bias.size].reshape(joined_bias.shape)
    at += joined_bias.size
    inner_bias_out = small_out[at : at + inner_bias.size].reshape(inner_bias.shape)
    bias_out = small_out[4 * rows_part : 5 * rows_part]

    share = total_of(send_chunks(scaled, "tp"))
    lines = 2 * count // part
    means = share[count : count + lines].reshape(2, count) / width
    share = share[:count]
    own_normed = (own_tokens.astype(F32) - center) * inverse
    own_rows = lax.dynamic_slice_in_dim(grad_rows, own_start, part, 1).astype(F32)
    tokens_grad = own_rows + inverse * (
        share - means[0][:, None] - own_normed * means[1][:, None]
    )

    return (
        layer_out.reshape(tokens.shape),
        tokens_grad.reshape(tokens.shape),
        vector[0],
        vector[1],
        head_out[:rows_part, :joined_width].reshape(joined_weight.shape),
        joined_bias_out,
        head_out[:rows_part, joined_width:].reshape(output_weight.shape),
        bias_out,
        vector[2],
        vector[3],
        feed_out[:, hidden:],
        inner_bias_out,
        feed_out[:, :hidden],
        bias_out,
    )


def solution(mesh):
    both = ("fsdp", "ctx")
    return jax.shard_map(
        body,
        mesh=mesh,
        in_specs=(
            P("fsdp", "ctx", "tp"),
            P("fsdp"),
            P("fsdp", "ctx", "tp"),
            P(both),
            P(both),
            P(both, "tp", None),
            P("tp", both),
            P(both, "tp", None),
            P(both),
            P(both),
            P(both),
            P(both, "tp"),
            P("tp", both),
            P(both, "tp"),
            P(both),
        ),
        out_specs=(
            P("fsdp", "ctx", "tp"),
            P("fsdp", "ctx", "tp"),
            P(both),
            P(both),
            P(both, "tp", None),
            P("tp", both),
            P(both, "tp", None),
            P(both),
            P(both),
            P(both),
            P(both, "tp"),
            P("tp", both),
            P(both, "tp"),
            P(both),
        ),
        check_vma=False,
    )
```

```python
import functools

import jax
import jax.numpy as jnp
from jax import lax
from jax.experimental import pallas as pl
from jax.experimental.pallas import tpu as pltpu
from jax.sharding import PartitionSpec as P

HEAD = 256
ROTARY = 64
F32 = jnp.float32
BF16 = jnp.bfloat16
VMEM_LIMIT = 56 << 20
HEADS_WEIGHT = 1.0
FEED_WEIGHT = 1.0
LAST_WEIGHT = 1.0
NN = (((1,), (0,)), ((), ()))
NT = (((1,), (1,)), ((), ()))
TN = (((0,), (0,)), ((), ()))


def dot(a, b, dims):
    return lax.dot_general(a, b, dims, preferred_element_type=F32)


def after(value, *earlier):
    return lax.optimization_barrier((value, earlier))[0]


def params(*semantics):
    return pltpu.CompilerParams(
        dimension_semantics=semantics or None, vmem_limit_bytes=VMEM_LIMIT
    )


def cost(flops, moved, weight=1.0):
    return pl.CostEstimate(
        flops=int(flops * weight), bytes_accessed=int(moved * weight), transcendentals=0
    )


def line_gather(piece, axis, first=None, gate=None):
    size = lax.axis_size(axis)
    up = [(i, i + 1) for i in range(size - 1)]
    down = [(i + 1, i) for i in range(size - 1)]
    right, left = [], []
    a = b = piece
    for step in range(size - 1):
        if step == 2 and gate is not None:
            a, b = after((a, b), gate)
        if step == 0 and first is not None:
            a, b = first
        else:
            a = lax.ppermute(a, axis, up)
            b = lax.ppermute(b, axis, down)
        right.append(a)
        left.append(b)
    return [(right[s - 1], left[size - s - 1]) for s in range(1, size)]


def send_chunks(chunks, axis):
    size = lax.axis_size(axis)
    return [chunks[0]] + [
        lax.ppermute(chunks[k], axis, [(i, (i + k) % size) for i in range(size)])
        for k in range(1, size)
    ]


def norm_kernel(size, me_ref, own, *refs):
    pairs = refs[: 2 * (size - 1)]
    gains, first_out, second_out, token_out, stat_out, work = refs[2 * (size - 1) :]
    part = own.shape[1]
    me = me_ref[0]
    for s in range(size):
        if s == 0:
            piece = own[...].astype(F32)
        else:
            piece = pairs[2 * s - 2][...].astype(F32) + pairs[2 * s - 1][...].astype(F32)
        at = lax.rem(me - s + size, size)
        work[:, pl.ds(pl.multiple_of(at * part, part), part)] = piece
    rows = work[...]
    token_out[...] = rows.astype(BF16)
    width = rows.shape[1]
    center = jnp.sum(rows, axis=1, keepdims=True) * (1.0 / width)
    shifted = rows - center
    inverse = lax.rsqrt(jnp.sum(shifted * shifted, axis=1, keepdims=True) * (1.0 / width) + 1e-05)
    normed = shifted * inverse
    first_out[...] = (normed * gains[0:1, :] + gains[1:2, :]).astype(BF16)
    second_out[...] = (normed * gains[2:3, :] + gains[3:4, :]).astype(BF16)
    lane = lax.broadcasted_iota(jnp.int32, stat_out.shape, 1)
    stat_out[...] = jnp.where(lane == 0, center, inverse)


def norm_call(me, own, pairs, gains, tile=128):
    count, part = own.shape
    size = len(pairs) + 1
    width = part * size
    flat = [p for pair in pairs for p in pair]
    block = pl.BlockSpec((tile, part), lambda i, *_: (i, 0))
    wide = pl.BlockSpec((tile, width), lambda i, *_: (i, 0))
    return pl.pallas_call(
        functools.partial(norm_kernel, size),
        grid_spec=pltpu.PrefetchScalarGridSpec(
            num_scalar_prefetch=1,
            grid=(count // tile,),
            in_specs=[block] * (1 + len(flat)) + [pl.BlockSpec((4, width), lambda i, *_: (0, 0))],
            out_specs=[wide, wide, wide, pl.BlockSpec((tile, 128), lambda i, *_: (i, 0))],
            scratch_shapes=[pltpu.VMEM((tile, width), F32)],
        ),
        out_shape=[
            jax.ShapeDtypeStruct((count, width), BF16),
            jax.ShapeDtypeStruct((count, width), BF16),
            jax.ShapeDtypeStruct((count, width), BF16),
            jax.ShapeDtypeStruct((count, 128), F32),
        ],
        compiler_params=params("arbitrary"),
        cost_estimate=cost(count * width * 16, count * width * 10),
        name="norm",
    )(me, own, *flat, gains)


def cot_kernel(size, local_len, tile, me_ref, len_ref, own, *refs):
    pairs = refs[: 2 * (size - 1)]
    rows_out, sum_out = refs[2 * (size - 1) :]
    part = own.shape[1]
    me, ctx = me_ref[0], me_ref[1]
    step = pl.program_id(0)
    start = step * tile
    seq = start // local_len
    length = len_ref[seq]
    position = ctx * local_len + lax.rem(start, local_len)
    position = position + lax.broadcasted_iota(jnp.int32, (tile, 1), 0)
    keep = position < length

    @pl.when(step == 0)
    def _():
        sum_out[...] = jnp.zeros_like(sum_out)

    for s in range(size):
        if s == 0:
            piece = own[...].astype(F32)
        else:
            piece = pairs[2 * s - 2][...].astype(F32) + pairs[2 * s - 1][...].astype(F32)
        piece = jnp.where(keep, piece, 0.0)
        at = lax.rem(me - s + size, size)
        cols = pl.ds(pl.multiple_of(at * part, part), part)
        rows_out[:, cols] = piece.astype(BF16)
        sum_out[0:1, cols] += jnp.sum(piece, axis=0, keepdims=True)


def cot_call(places, lengths, own, pairs, local_len, tile=256):
    count, part = own.shape
    size = len(pairs) + 1
    width = part * size
    flat = [p for pair in pairs for p in pair]
    block = pl.BlockSpec((tile, part), lambda i, *_: (i, 0))
    return pl.pallas_call(
        functools.partial(cot_kernel, size, local_len, tile),
        grid_spec=pltpu.PrefetchScalarGridSpec(
            num_scalar_prefetch=2,
            grid=(count // tile,),
            in_specs=[block] * (1 + len(flat)),
            out_specs=[
                pl.BlockSpec((tile, width), lambda i, *_: (i, 0)),
                pl.BlockSpec((8, width), lambda i, *_: (0, 0)),
            ],
        ),
        out_shape=[
            jax.ShapeDtypeStruct((count, width), BF16),
            jax.ShapeDtypeStruct((8, width), F32),
        ],
        compiler_params=params("arbitrary"),
        cost_estimate=cost(count * width * 4, count * width * 6),
        name="cotangent_rows",
    )(places, lengths, own, *flat)


def flat_rows(ref):
    value = ref[...]
    return value.reshape(value.shape[0] * value.shape[1], value.shape[2])


def joined_kernel(seqs, rows_ref, weight_ref, bias_ref, table_ref, query_ref, pair_ref):
    kind = lax.rem(pl.program_id(0), 3)
    out = dot(rows_ref[...], flat_rows(weight_ref), NN) + bias_ref[0:1, :]
    local_len = out.shape[0] // seqs

    def turned():
        front = out[:, :128]
        up = pltpu.roll(front, 128 - ROTARY // 2, 1)
        down = pltpu.roll(front, ROTARY // 2, 1)
        table = table_ref[...]
        if seqs > 1:
            table = jnp.concatenate([table] * seqs, axis=0)
        front = front * table[:, :128] + up * table[:, 128:256] + down * table[:, 256:]
        return jnp.concatenate([front, out[:, 128:]], axis=1)

    @pl.when(kind == 0)
    def _():
        query_ref[...] = (turned().astype(BF16).astype(F32) * HEAD ** (-0.5)).astype(BF16)

    @pl.when(kind == 1)
    def _():
        value = turned().astype(BF16)
        for s in range(seqs):
            pair_ref[s] = value[s * local_len : (s + 1) * local_len, :]

    @pl.when(kind == 2)
    def _():
        value = out.astype(BF16)
        for s in range(seqs):
            pair_ref[s] = value[s * local_len : (s + 1) * local_len, :]


def joined_call(rows, pack, bias, table, seqs, heads):
    count, width = rows.shape
    shards = pack.shape[0]
    local_len = count // seqs
    return pl.pallas_call(
        functools.partial(joined_kernel, seqs),
        grid=(3 * heads,),
        in_specs=[
            pl.BlockSpec((count, width), lambda j: (0, 0)),
            pl.BlockSpec((shards, width // shards, HEAD), lambda j: (0, 0, j)),
            pl.BlockSpec((8, HEAD), lambda j: (0, j)),
            pl.BlockSpec(table.shape, lambda j: (0, 0)),
        ],
        out_specs=[
            pl.BlockSpec((count, HEAD), lambda j: (0, j // 3)),
        ]
        + [
            pl.BlockSpec(
                (seqs, local_len, HEAD), lambda j: (0, 0, 2 * (j // 3) + (j % 3) // 2)
            )
        ],
        out_shape=[
            jax.ShapeDtypeStruct((count, heads * HEAD), BF16),
            jax.ShapeDtypeStruct((seqs, local_len, 2 * heads * HEAD), BF16),
        ],
        compiler_params=params("arbitrary"),
        cost_estimate=cost(6 * heads * HEAD * count * width, 2 * (count + 3 * heads * HEAD) * width),
        name="joined",
    )(rows, pack, jnp.broadcast_to(bias.reshape(1, -1), (8, bias.size)), table)


SLOTS = 4


def slot_refs(own_ref, below_ref, both_ref):
    return [own_ref, below_ref, both_ref.at[0], both_ref.at[1]]


def masked(scores, slot, first_key, first_query, length):
    keys = first_key + lax.broadcasted_iota(jnp.int32, (1, scores.shape[1]), 1)
    ok = keys < length
    if slot == 0:
        queries = first_query + lax.broadcasted_iota(jnp.int32, (scores.shape[0], 1), 0)
        ok = ok & (keys <= queries)
    return jnp.where(ok, scores, -1e30)


def forward_kernel(heads, seq, info, lens, query_ref, pair_ref, context_ref, lse_ref, *scratch):
    local_len = query_ref.shape[0]
    length = lens[seq]
    place = info[SLOTS]
    top, total, acc = scratch[:heads], scratch[heads : 2 * heads], scratch[2 * heads :]
    for slot in range(SLOTS):
        block = info[slot]
        first_key = block * local_len

        @pl.when((block >= 0) & (block <= place) & (first_key < length))
        def _():
            for head in range(heads):
                at = 2 * HEAD * head
                query = query_ref[:, HEAD * head : HEAD * (head + 1)]
                keys = pair_ref[block, :, at : at + HEAD]
                vals = pair_ref[block, :, at + HEAD : at + 2 * HEAD]
                scores = dot(query, keys, NT)
                scores = masked(scores, slot, first_key, place * local_len, length)
                best = jnp.max(scores, axis=1, keepdims=True)
                if slot > 0:
                    best = jnp.maximum(best, top[head][...])
                weights = jnp.exp(scores - best)
                summed = jnp.sum(weights, axis=1, keepdims=True)
                mixed = dot(weights.astype(BF16), vals, NN)
                if slot > 0:
                    scale = jnp.exp(top[head][...] - best)
                    summed = summed + total[head][...] * scale
                    mixed = mixed + acc[head][...] * scale
                top[head][...] = best
                total[head][...] = summed
                acc[head][...] = mixed

        if slot == 0:

            @pl.when(first_key >= length)
            def _():
                for head in range(heads):
                    top[head][...] = jnp.full_like(top[head], -1e30)
                    total[head][...] = jnp.zeros_like(total[head])
                    acc[head][...] = jnp.zeros_like(acc[head])

    for head in range(heads):
        cols = slice(HEAD * head, HEAD * (head + 1))
        context_ref[:, cols] = (acc[head][...] / total[head][...]).astype(BF16)
        lse = top[head][...] + jnp.log(total[head][...])
        lse_ref[:, 128 * head : 128 * (head + 1)] = jnp.broadcast_to(lse, (local_len, 128))


def forward_call(info, lengths, query, pairs, seq, heads):
    local_len = pairs.shape[2]
    return pl.pallas_call(
        functools.partial(forward_kernel, heads, seq),
        grid_spec=pltpu.PrefetchScalarGridSpec(
            num_scalar_prefetch=2,
            grid=(1,),
            in_specs=[
                pl.BlockSpec((local_len, heads * HEAD), lambda i, *_: (seq, 0)),
                pl.BlockSpec(
                    (SLOTS, None, local_len, 2 * heads * HEAD), lambda i, *_: (0, seq, 0, 0)
                ),
            ],
            out_specs=[
                pl.BlockSpec((local_len, heads * HEAD), lambda i, *_: (0, 0)),
                pl.BlockSpec((local_len, heads * 128), lambda i, *_: (0, 0)),
            ],
            scratch_shapes=[pltpu.VMEM((local_len, 1), F32)] * (2 * heads)
            + [pltpu.VMEM((local_len, HEAD), F32)] * heads,
        ),
        out_shape=[
            jax.ShapeDtypeStruct((local_len, heads * HEAD), BF16),
            jax.ShapeDtypeStruct((local_len, heads * 128), F32),
        ],
        compiler_params=params("arbitrary"),
        cost_estimate=cost(4 * local_len * heads * HEAD * local_len * SLOTS,
            4 * local_len * heads * HEAD * SLOTS, HEADS_WEIGHT),
        name="attention_forward",
    )(info, lengths, query, pairs)


def backward_kernel(
    heads, seq, info, lens, query_ref, context_ref, grad_ref, lse_ref, pair_ref, query_out, *refs
):
    local_len = query_ref.shape[0]
    pair_outs = slot_refs(*refs[:3])
    accs = refs[3:]
    length = lens[seq]
    place = info[SLOTS]
    for slot in range(SLOTS):
        block = info[slot]
        first_key = block * local_len
        seen = (block >= 0) & (block <= place) & (first_key < length)

        @pl.when(seen)
        def _():
            for head in range(heads):
                at = 2 * HEAD * head
                cols = slice(HEAD * head, HEAD * (head + 1))
                query, grad = query_ref[:, cols], grad_ref[:, cols]
                keys = pair_ref[block, :, at : at + HEAD]
                vals = pair_ref[block, :, at + HEAD : at + 2 * HEAD]
                shared = grad.astype(F32) * context_ref[:, cols].astype(F32)
                shared = jnp.sum(shared, axis=1, keepdims=True)
                scores = dot(query, keys, NT)
                scores = masked(scores, slot, first_key, place * local_len, length)
                probs = jnp.exp(scores - lse_ref[:, 128 * head : 128 * head + 1])
                score_grad = (probs * (dot(grad, vals, NT) - shared)).astype(BF16)
                pair_outs[slot][:, at : at + HEAD] = dot(score_grad, query, TN).astype(BF16)
                pair_outs[slot][:, at + HEAD : at + 2 * HEAD] = dot(
                    probs.astype(BF16), grad, TN
                ).astype(BF16)
                mixed = dot(score_grad, keys, NN)
                accs[head][...] = mixed if slot == 0 else accs[head][...] + mixed

        @pl.when(jnp.logical_not(seen))
        def _():
            pair_outs[slot][...] = jnp.zeros_like(pair_outs[slot])
            if slot == 0:
                for head in range(heads):
                    accs[head][...] = jnp.zeros_like(accs[head])

    for head in range(heads):
        query_out[:, HEAD * head : HEAD * (head + 1)] = (
            accs[head][...] * HEAD ** (-0.5)
        ).astype(BF16)


def backward_call(info, lengths, query, context, grad, lse, pairs, seq, heads):
    local_len = pairs.shape[2]
    here = pl.BlockSpec((local_len, heads * HEAD), lambda i, *_: (seq, 0))
    one = pl.BlockSpec((local_len, heads * HEAD), lambda i, *_: (0, 0))
    two = [pl.BlockSpec((local_len, 2 * heads * HEAD), lambda i, *_: (0, 0))] * 2
    two = two + [pl.BlockSpec((2, local_len, 2 * heads * HEAD), lambda i, *_: (0, 0, 0))]
    return pl.pallas_call(
        functools.partial(backward_kernel, heads, seq),
        grid_spec=pltpu.PrefetchScalarGridSpec(
            num_scalar_prefetch=2,
            grid=(1,),
            in_specs=[
                here,
                one,
                here,
                pl.BlockSpec((local_len, heads * 128), lambda i, *_: (0, 0)),
                pl.BlockSpec(
                    (SLOTS, None, local_len, 2 * heads * HEAD), lambda i, *_: (0, seq, 0, 0)
                ),
            ],
            out_specs=[one] + two,
            scratch_shapes=[pltpu.VMEM((local_len, HEAD), F32)] * heads,
        ),
        out_shape=[jax.ShapeDtypeStruct((local_len, heads * HEAD), BF16)]
        + [jax.ShapeDtypeStruct((local_len, 2 * heads * HEAD), BF16)] * 2
        + [jax.ShapeDtypeStruct((2, local_len, 2 * heads * HEAD), BF16)],
        compiler_params=params("arbitrary"),
        cost_estimate=cost(10 * local_len * heads * HEAD * local_len * SLOTS,
            8 * local_len * heads * HEAD * SLOTS, HEADS_WEIGHT),
        name="attention_backward",
    )(info, lengths, query, context, grad, lse, pairs)


def return_pairs(own, below, siblings, axis):
    taken = lax.ppermute(siblings, axis, [(0, 1), (1, 0), (2, 3), (3, 2)])
    lower = (below.astype(F32) + taken[1].astype(F32)).astype(BF16)
    above = lax.ppermute(lower, axis, [(2, 0), (3, 1)])
    return [own, taken, above], taken


def branch_kernel(parts, active_ref, *refs):
    context_refs, (outer_ref, output_ref, out_ref) = refs[:parts], refs[parts:]
    out = dot(active_ref[...], outer_ref[...], NT)
    context = jnp.concatenate([ref[...] for ref in context_refs], axis=0)
    out_ref[...] = (out + dot(context, flat_rows(output_ref), NT)).astype(BF16)


def branch_call(active, contexts, outer, pack, column, tile=512):
    count, hidden = active.shape
    width, inside = outer.shape[0], contexts[0].shape[1]
    rows = width // pack.shape[0]
    return pl.pallas_call(
        functools.partial(branch_kernel, len(contexts)),
        grid=(width // tile,),
        in_specs=[pl.BlockSpec((count, hidden), lambda j: (0, 0))]
        + [pl.BlockSpec(c.shape, lambda j: (0, 0)) for c in contexts]
        + [
            pl.BlockSpec((tile, hidden), lambda j: (j, 0)),
            pl.BlockSpec((tile // rows, rows, inside), lambda j: (j, 0, column)),
        ],
        out_specs=pl.BlockSpec((count, tile), lambda j: (0, j)),
        out_shape=jax.ShapeDtypeStruct((count, width), BF16),
        compiler_params=params("arbitrary"),
        cost_estimate=cost(2 * count * width * (hidden + inside), 2 * width * (hidden + inside), HEADS_WEIGHT),
        name="branch",
    )(active, *contexts, outer, pack)


def upper_kernel(rows_ref, weight_ref, bias_ref, active_ref, slope_ref):
    weight = flat_rows(weight_ref)
    bias = bias_ref[0:1, :]
    count = rows_ref.shape[0]
    piece = count // 4
    for i in range(4):
        here = slice(i * piece, (i + 1) * piece)
        upper = dot(rows_ref[here, :], weight, NN) + bias
        phi = 0.5 * (1.0 + lax.erf(upper * 0.7071067811865476))
        slope = phi + upper * jnp.exp(-0.5 * upper * upper) * 0.3989422804014327
        active_ref[here, :] = (upper * phi).astype(BF16)
        slope_ref[here, :] = slope.astype(BF16)


def upper_call(rows, pack, bias, column, tile=512):
    count, width = rows.shape
    hidden = bias.size
    shards = pack.shape[0]
    out = pl.BlockSpec((count, tile), lambda j: (0, j))
    first = column // tile
    return pl.pallas_call(
        upper_kernel,
        grid=(hidden // tile,),
        in_specs=[
            pl.BlockSpec((count, width), lambda j: (0, 0)),
            pl.BlockSpec((shards, width // shards, tile), lambda j: (0, 0, first + j)),
            pl.BlockSpec((8, tile), lambda j: (0, j)),
        ],
        out_specs=[out, out],
        out_shape=[jax.ShapeDtypeStruct((count, hidden), BF16)] * 2,
        compiler_params=params("arbitrary"),
        cost_estimate=cost(2 * count * width * hidden, 2 * width * (count + hidden)),
        name="upper",
    )(rows, pack, jnp.broadcast_to(bias.reshape(1, -1), (8, hidden)))


def upper_grad_kernel(rows_ref, weight_ref, slope_ref, out_ref, sum_ref):
    grad = dot(rows_ref[...], weight_ref[...], NN) * slope_ref[...].astype(F32)
    low = grad.astype(BF16)
    out_ref[...] = low
    sum_ref[...] = jnp.broadcast_to(
        jnp.sum(low.astype(F32), axis=0, keepdims=True), sum_ref.shape
    )


def upper_grad_call(rows, weight, slope, tile=512):
    count, width = rows.shape
    hidden = weight.shape[1]
    out = pl.BlockSpec((count, tile), lambda j: (0, j))
    return pl.pallas_call(
        upper_grad_kernel,
        grid=(hidden // tile,),
        in_specs=[
            pl.BlockSpec((count, width), lambda j: (0, 0)),
            pl.BlockSpec((width, tile), lambda j: (0, j)),
            out,
        ],
        out_specs=[out, pl.BlockSpec((8, tile), lambda j: (0, j))],
        out_shape=[
            jax.ShapeDtypeStruct((count, hidden), BF16),
            jax.ShapeDtypeStruct((8, hidden), F32),
        ],
        compiler_params=params("arbitrary"),
        cost_estimate=cost(2 * count * width * hidden, 2 * width * (2 * count + hidden), FEED_WEIGHT),
        name="upper_grad",
    )(rows, weight, slope)


def context_grad_kernel(rows_ref, weight_ref, out_ref):
    out_ref[...] = dot(rows_ref[...], flat_rows(weight_ref), NN).astype(BF16)


def context_grad_call(rows, pack, column, inside, tile=512):
    count, width = rows.shape
    return pl.pallas_call(
        context_grad_kernel,
        grid=(count // tile,),
        in_specs=[
            pl.BlockSpec((tile, width), lambda i: (i, 0)),
            pl.BlockSpec(
                (pack.shape[0], width // pack.shape[0], inside), lambda i: (0, 0, column)
            ),
        ],
        out_specs=pl.BlockSpec((tile, inside), lambda i: (i, 0)),
        out_shape=jax.ShapeDtypeStruct((count, inside), BF16),
        compiler_params=params("arbitrary"),
        cost_estimate=cost(2 * count * width * inside, 2 * width * (count + inside), HEADS_WEIGHT),
        name="context_grad",
    )(rows, pack)


def column_sums(grad, normed, out_ref):
    count, tile = grad.shape
    out_ref[0:1, :] = jnp.sum(grad * normed, axis=0, keepdims=True)
    out_ref[1:2, :] = jnp.sum(grad, axis=0, keepdims=True)
    out_ref[2:8, :] = jnp.zeros((6, tile), F32)


def second_kernel(grad_ref, weight_ref, rows_ref, stat_ref, gain_ref, out_ref, sum_ref):
    grad = dot(grad_ref[...], flat_rows(weight_ref), NT)
    normed = (rows_ref[...].astype(F32) - stat_ref[:, 0:1]) * stat_ref[:, 1:2]
    column_sums(grad, normed, sum_ref)
    out_ref[...] = (grad * gain_ref[2:3, :]).astype(BF16)


def second_call(grad, pack, column, rows, stats, gains, tile=512):
    count, hidden = grad.shape
    width = rows.shape[1]
    deep = width // pack.shape[0]
    return pl.pallas_call(
        second_kernel,
        grid=(width // tile,),
        in_specs=[
            pl.BlockSpec((count, hidden), lambda j: (0, 0)),
            pl.BlockSpec((tile // deep, deep, hidden), lambda j: (j, 0, column)),
            pl.BlockSpec((count, tile), lambda j: (0, j)),
            pl.BlockSpec((count, 128), lambda j: (0, 0)),
            pl.BlockSpec((4, tile), lambda j: (0, j)),
        ],
        out_specs=[
            pl.BlockSpec((count, tile), lambda j: (0, j)),
            pl.BlockSpec((8, tile), lambda j: (0, j)),
        ],
        out_shape=[
            jax.ShapeDtypeStruct((count, width), BF16),
            jax.ShapeDtypeStruct((8, width), F32),
        ],
        compiler_params=params("arbitrary"),
        cost_estimate=cost(2 * count * width * hidden, 2 * (width * hidden + 3 * count * width), LAST_WEIGHT),
        name="second_in_grad",
    )(grad, pack, rows, stats, gains)


def joined_grad_kernel(heads, *refs):
    (table_ref, out_ref, sum_ref), refs = refs[-3:], refs[:-3]
    table = table_ref[...]
    local_len = table.shape[0]

    def back(value):
        front = value[:, :128]
        up = pltpu.roll(front, 128 - ROTARY // 2, 1)
        down = pltpu.roll(front, ROTARY // 2, 1)
        front = front * table[:, :128] - up * table[:, 128:256] - down * table[:, 256:]
        return jnp.concatenate([front, value[:, 128:]], axis=1)

    sum_ref[...] = jnp.zeros_like(sum_ref)
    for seq in range(len(refs) // 4):
        query_ref, own_ref, near_ref, far_ref = refs[4 * seq : 4 * seq + 4]
        here = slice(seq * local_len, (seq + 1) * local_len)
        for head in range(heads):
            at = 3 * HEAD * head
            pair = slice(2 * HEAD * head, 2 * HEAD * (head + 1))
            total = own_ref[:, pair].astype(F32) + near_ref[0, :, pair].astype(F32)
            total = total + far_ref[:, pair].astype(F32)
            query = query_ref[:, HEAD * head : HEAD * (head + 1)].astype(F32)
            parts = [back(query), back(total[:, :HEAD]), total[:, HEAD:]]
            for i, part in enumerate(parts):
                cols = slice(at + HEAD * i, at + HEAD * (i + 1))
                low = part.astype(BF16)
                out_ref[here, cols] = low
                sum_ref[0:1, cols] += jnp.sum(low.astype(F32), axis=0, keepdims=True)


def joined_grad_call(queries, sums, table, heads):
    seqs = len(queries)
    count = seqs * queries[0].shape[0]
    width = 3 * heads * HEAD
    flat = [a for query, three in zip(queries, sums) for a in (query, *three)]
    return pl.pallas_call(
        functools.partial(joined_grad_kernel, heads),
        out_shape=[
            jax.ShapeDtypeStruct((count, width), BF16),
            jax.ShapeDtypeStruct((8, width), F32),
        ],
        compiler_params=params(),
        cost_estimate=cost(10 * count * width, 10 * count * width, LAST_WEIGHT),
        name="joined_grad",
    )(*flat, table)


EXTRA = 8


def first_kernel(ranks, order, grad_ref, weight_ref, rows_ref, stat_ref, gain_ref, second_ref, *refs):
    out_refs, (sum_ref, row_ref) = refs[:ranks], refs[ranks:]
    step = pl.program_id(0)
    grad = dot(grad_ref[...], flat_rows(weight_ref), NT)
    count, tile = grad.shape
    normed = (rows_ref[...].astype(F32) - stat_ref[:, 0:1]) * stat_ref[:, 1:2]
    column_sums(grad, normed, sum_ref)
    total = grad * gain_ref[0:1, :] + second_ref[...].astype(F32)
    low = total.astype(BF16)
    for k in range(ranks):

        @pl.when(step == k)
        def _():
            out_refs[k][:count, :] = low

    plain = jnp.sum(total, axis=1, keepdims=True)
    along = jnp.sum(total * normed, axis=1, keepdims=True)
    lane = lax.broadcasted_iota(jnp.int32, row_ref.shape, 1)
    both = jnp.where(lane == 0, plain, along)

    @pl.when(step == 0)
    def _():
        row_ref[...] = both

    @pl.when(step > 0)
    def _():
        row_ref[...] += both

    @pl.when(step == ranks - 1)
    def _():
        turned = row_ref[...].T
        lines = [turned[i : i + 1, j : j + tile] for i in (0, 1) for j in range(0, count, tile)]
        lines.append(jnp.zeros((EXTRA - len(lines), tile), F32))
        extra = jnp.concatenate(lines, axis=0).astype(BF16)
        for ref in out_refs:
            ref[count:, :] = extra


def first_call(order, grad, pack, rows, stats, gains, second, ranks):
    count, inside = grad.shape
    width = rows.shape[1]
    tile = width // ranks
    deep = width // pack.shape[0]
    return pl.pallas_call(
        functools.partial(first_kernel, ranks),
        grid_spec=pltpu.PrefetchScalarGridSpec(
            num_scalar_prefetch=1,
            grid=(ranks,),
            in_specs=[
                pl.BlockSpec((count, inside), lambda j, _: (0, 0)),
                pl.BlockSpec((tile // deep, deep, inside), lambda j, order: (order[j], 0, 0)),
                pl.BlockSpec((count, tile), lambda j, order: (0, order[j])),
                pl.BlockSpec((count, 128), lambda j, _: (0, 0)),
                pl.BlockSpec((4, tile), lambda j, order: (0, order[j])),
                pl.BlockSpec((count, tile), lambda j, order: (0, order[j])),
            ],
            out_specs=[pl.BlockSpec((count + EXTRA, tile), lambda j, _: (0, 0))] * ranks
            + [pl.BlockSpec((8, tile), lambda j, order: (0, order[j]))],
            scratch_shapes=[pltpu.VMEM((count, 128), F32)],
        ),
        out_shape=[jax.ShapeDtypeStruct((count + EXTRA, tile), BF16)] * ranks
        + [jax.ShapeDtypeStruct((8, width), F32)],
        compiler_params=params("arbitrary"),
        cost_estimate=cost(2 * count * width * inside, 2 * (width * inside + 4 * count * width), LAST_WEIGHT),
        name="first_in_grad",
    )(order, grad, pack, rows, stats, gains, second)


def flips(size, by):
    return [(i, i ^ by) for i in range(size)]


def paired(group):
    return lax.axis_size(group[0]) == 2 and lax.axis_size(group[1]) == 4


def member(group):
    return lax.axis_size(group[1]) * lax.axis_index(group[0]) + lax.axis_index(group[1])


def gather_small(vector, group):
    if not paired(group):
        return lax.all_gather(vector.reshape(1, 1, -1), group, axis=0, tiled=True)[:, 0]
    rows = jnp.zeros((8, vector.size), vector.dtype)
    rows = lax.dynamic_update_slice_in_dim(rows, vector.reshape(1, -1), member(group), 0)
    for by in (1, 2, 4):
        rows = rows + lax.ppermute(rows, group, flips(8, by))
    return rows


def weight_grad_kernel(sizes, outs, small, order, *refs):
    parts = len(sizes)
    lhs_refs, rhs_refs, refs = refs[: 4 * parts], refs[4 * parts : 5 * parts], refs[5 * parts :]
    small_ref = refs[0] if small else None
    add_ref = refs[small] if outs > 1 else None
    out_refs, turned = refs[-1 - outs : -1], refs[-1]
    rows = lhs_refs[0].shape[1]
    deep = rows + EXTRA * small
    step = pl.program_id(0)

    def put(k, value, start):
        height = value.shape[0]
        if outs == 1:
            out_refs[0][k * deep + start : k * deep + start + height, :] = value.astype(BF16)
        else:
            add = add_ref[k * deep + start : k * deep + start + height, :].astype(F32)
            out_refs[k][start : start + height, :] = (value + add).astype(BF16)

    first = 0
    for i, size in enumerate(sizes):
        lhs, rhs_ref = lhs_refs[4 * i : 4 * i + 4], rhs_refs[i]

        @pl.when(step == first)
        def _():
            for k in range(4):
                turned[k * rows : (k + 1) * rows, :] = lhs[k][...].T

        @pl.when((step >= first) & (step < first + size))
        def _():
            out = dot(turned[...], rhs_ref[...], NN)
            for k in range(4):
                put(k, out[k * rows : (k + 1) * rows, :], 0)

        first += size
    if small:
        for k in range(4):
            put(k, small_ref[order[k]], rows)


def weight_grad_call(order, pairs, add=None, small=None, tile=512):
    count, width = pairs[0][0].shape
    rows = width // 8
    sizes = [rhs.shape[1] // tile for _, rhs in pairs]
    total = sum(sizes) * tile
    outs = 1 if add is None else 4
    height = rows if small is None else rows + EXTRA
    deep = 4 * height if add is None else height
    firsts = [sum(sizes[:i]) for i in range(len(sizes))]

    def column(k):
        return pl.BlockSpec((count, rows), lambda j, order: (0, order[k]))

    def piece(first, size):
        return pl.BlockSpec(
            (count, tile), lambda j, _: (0, jnp.minimum(jnp.maximum(j - first, 0), size - 1))
        )

    out = pl.BlockSpec((deep, tile), lambda j, *_: (0, j))
    extra_specs, extra = [], []
    if small is not None:
        extra_specs.append(pl.BlockSpec((8, EXTRA, tile), lambda j, *_: (0, 0, j)))
        extra.append(small)
    if add is not None:
        extra_specs.append(pl.BlockSpec((4 * height, tile), lambda j, *_: (0, j)))
        extra.append(add)
    return pl.pallas_call(
        functools.partial(weight_grad_kernel, sizes, outs, int(small is not None)),
        grid_spec=pltpu.PrefetchScalarGridSpec(
            num_scalar_prefetch=1,
            grid=(sum(sizes),),
            in_specs=[column(k) for _ in pairs for k in range(4)]
            + [piece(f, n) for f, n in zip(firsts, sizes)]
            + extra_specs,
            out_specs=[out] * outs,
            scratch_shapes=[pltpu.VMEM((4 * rows, count), BF16)],
        ),
        out_shape=[jax.ShapeDtypeStruct((deep, total), BF16)] * outs,
        compiler_params=params("arbitrary"),
        cost_estimate=cost(8 * rows * count * total, 2 * (count * (4 * rows + total) + 8 * rows * total), LAST_WEIGHT),
        name="weight_grad",
    )(
        order,
        *[lhs for lhs, _ in pairs for _ in range(4)],
        *[rhs for _, rhs in pairs],
        *extra,
    )


def product_kernel(sizes, *refs):
    parts = len(sizes)
    lhs_refs, rhs_refs = refs[:parts], refs[parts : 2 * parts]
    out_ref, turned = refs[2 * parts :]
    step = pl.program_id(0)
    first = 0
    for lhs_ref, rhs_ref, size in zip(lhs_refs, rhs_refs, sizes):

        @pl.when(step == first)
        def _():
            turned[...] = lhs_ref[...].T

        @pl.when((step >= first) & (step < first + size))
        def _():
            out_ref[...] = dot(turned[...], rhs_ref[...], NN).astype(BF16)

        first += size


def product_call(pairs, tile=512):
    count, width = pairs[0][0].shape
    sizes = [rhs.shape[1] // tile for _, rhs in pairs]
    total = sum(sizes) * tile
    firsts = [sum(sizes[:i]) for i in range(len(sizes))]

    def piece(first, size):
        return pl.BlockSpec(
            (count, tile), lambda j: (0, jnp.minimum(jnp.maximum(j - first, 0), size - 1))
        )

    return pl.pallas_call(
        functools.partial(product_kernel, sizes),
        grid=(sum(sizes),),
        in_specs=[pl.BlockSpec((count, width), lambda j: (0, 0)) for _ in pairs]
        + [piece(f, n) for f, n in zip(firsts, sizes)],
        out_specs=pl.BlockSpec((width, tile), lambda j: (0, j)),
        out_shape=jax.ShapeDtypeStruct((width, total), BF16),
        scratch_shapes=[pltpu.VMEM((width, count), BF16)],
        compiler_params=params("arbitrary"),
        cost_estimate=cost(2 * width * count * total, 2 * (count * (width + total) + width * total), FEED_WEIGHT),
        name="product",
    )(*[lhs for lhs, _ in pairs], *[rhs for _, rhs in pairs])


STEPS = (0, 2, 4, 6)


def weight_grad_given(pairs, group, small=None):
    if not paired(group):
        return None
    steps = jnp.array(STEPS, jnp.int32)
    (given,) = weight_grad_call((member(group) ^ 1) ^ steps, pairs, small=small)
    return given


def weight_grad_kept(pairs, given, group, small=None):
    if not paired(group):
        whole = jnp.concatenate([dot(lhs, rhs, TN).astype(BF16) for lhs, rhs in pairs], axis=1)
        return [lax.psum_scatter(whole, group, scatter_dimension=0, tiled=True)]
    taken = lax.ppermute(given, group, flips(8, 1))
    sums = weight_grad_call(
        member(group) ^ jnp.array(STEPS, jnp.int32), pairs, taken, small=small
    )
    return [sums[0]] + [
        lax.ppermute(part, group, flips(8, by)) for part, by in zip(sums[1:], STEPS[1:])
    ]


def total_of(terms):
    return functools.reduce(lambda a, b: a + b, [t.astype(F32) for t in terms])


def line_sum(value, axis):
    size = lax.axis_size(axis)
    terms = [value]
    for step in range(1, size):
        terms.append(lax.ppermute(value, axis, [(i, (i + step) % size) for i in range(size)]))
    return functools.reduce(lambda a, b: a + b, terms)


def body(
    tokens,
    lengths,
    cotangent,
    first_gain,
    first_shift,
    joined_weight,
    joined_bias,
    output_weight,
    output_bias,
    second_gain,
    second_shift,
    inner_weight,
    inner_bias,
    outer_weight,
    outer_bias,
):
    group = ("fsdp", "ctx")
    seqs, local_len, part = tokens.shape
    count = seqs * local_len
    ranks = lax.axis_size("tp")
    width = part * ranks
    shards = lax.axis_size("fsdp") * lax.axis_size("ctx")
    rows_part = width // shards
    heads = joined_weight.shape[1]
    hidden = inner_weight.shape[1]
    me, ctx = lax.axis_index("tp"), lax.axis_index("ctx")

    own_tokens, own_cot = tokens.reshape(count, part), cotangent.reshape(count, part)
    joined_width, inside = heads * 3 * HEAD, heads * HEAD
    vectors = [first_gain, first_shift, second_gain, second_shift, output_bias, outer_bias]
    flat = jnp.concatenate(vectors + [joined_bias.reshape(-1), inner_bias.reshape(-1)])
    small = gather_small(jnp.pad(flat, (0, -flat.size % 256)), group)
    shard = jnp.concatenate(
        [joined_weight.reshape(rows_part, -1), output_weight.reshape(rows_part, -1)], axis=1
    )
    token_pairs = line_gather(own_tokens, "tp")
    cot_start = after(own_cot, token_pairs)
    cot_first = (
        lax.ppermute(cot_start, "tp", [(i, i + 1) for i in range(ranks - 1)]),
        lax.ppermute(cot_start, "tp", [(i + 1, i) for i in range(ranks - 1)]),
    )
    pack = lax.all_gather(shard, group, axis=0, tiled=False)
    inner = lax.all_gather(inner_weight, group, axis=0, tiled=False)

    small = small.astype(F32)
    whole = [small[:, i * rows_part : (i + 1) * rows_part].reshape(width) for i in range(6)]
    at = 6 * rows_part
    whole_joined_bias = (
        small[:, at : at + joined_bias.size]
        .reshape((shards,) + joined_bias.shape)
        .transpose(1, 0, 2)
        .reshape(-1)
    )
    at += joined_bias.size
    whole_inner_bias = (
        small[:, at : at + inner_bias.size]
        .reshape((shards,) + inner_bias.shape)
        .transpose(1, 0, 2)
        .reshape(-1)
    )
    gains = jnp.stack(whole[:4])

    places = jnp.stack([me, ctx]).astype(jnp.int32)
    first_in, second_in, rows, stats = norm_call(places[:1], own_tokens, token_pairs, gains)
    center, inverse = stats[:, 0:1], stats[:, 1:2]
    positions = ctx * local_len + jnp.arange(local_len, dtype=jnp.int32)
    half = ROTARY // 2
    frequency = 1.0 / 10000.0 ** (jnp.arange(half, dtype=F32) * 2.0 / ROTARY)
    angles = positions.astype(F32)[:, None] * frequency[None, :]
    cosine, sine = jnp.cos(angles), jnp.sin(angles)
    ones = jnp.ones((local_len, 128 - ROTARY), F32)
    nothing = jnp.zeros((local_len, half), F32)
    blank = jnp.zeros((local_len, 128 - ROTARY), F32)
    table = jnp.concatenate(
        [cosine, cosine, ones, -sine, nothing, blank, nothing, sine, blank], axis=1
    )
    query, pair = joined_call(after(first_in, cot_first), pack, whole_joined_bias, table, seqs, heads)
    pairs = lax.all_gather(pair, "ctx", axis=0, tiled=False)
    low, odd = ctx - 2, ctx + 1 - 2 * lax.rem(ctx, 2)
    info = jnp.stack([ctx, low, odd, jnp.where(low >= 0, odd - 2, -1), ctx]).astype(jnp.int32)
    active, slope = upper_call(after(second_in, query), inner, whole_inner_bias, 0)
    cot_pairs = line_gather(cot_start, "tp", cot_first, active)
    grad_rows, bias_sums = cot_call(places, after(lengths, active), own_cot, cot_pairs, local_len)
    bias_grad = bias_sums[0]
    outer = lax.all_gather(after(outer_weight, grad_rows, pairs), group, axis=0, tiled=True)
    contexts, lses = [], []
    ready = after(query, grad_rows)
    for seq in range(seqs):
        context, lse = forward_call(info, lengths, ready, pairs, seq, heads)
        ready = after(query, context)
        contexts.append(context)
        lses.append(lse)

    context_grad = context_grad_call(after(grad_rows, ready), pack, joined_width // inside, inside)
    queries, sums = [], []
    for seq in range(seqs):
        query_grad, *pair_grads = backward_call(
            info, lengths, ready, contexts[seq], context_grad, lses[seq], pairs, seq, heads
        )
        ready = after(query, query_grad)
        queries.append(query_grad)
        three, taken = return_pairs(*pair_grads, "ctx")
        ready = after(ready, taken)
        sums.append(three)
    branch = branch_call(
        after(active, query_grad, taken), contexts, outer, pack, joined_width // inside
    )
    summed = lax.psum_scatter(branch, "tp", scatter_dimension=1, tiled=True).astype(F32)
    own_start = me * part
    own_bias = lax.dynamic_slice_in_dim(whole[4] + whole[5], own_start, part)
    valid = (positions[None, :] < lengths[:, None]).astype(F32).reshape(count, 1)
    layer_out = (valid * (own_tokens.astype(F32) + summed + own_bias)).astype(BF16)

    outer_whole = product_call([(after(grad_rows, branch), active)])
    outer_out = lax.psum_scatter(outer_whole, group, scatter_dimension=0, tiled=True)
    grad_late = after(grad_rows, outer_whole)
    upper_grad, upper_sums = upper_grad_call(grad_late, outer, slope)
    inner_bias_grad = upper_sums[0]
    second_scaled, second_sums = second_call(
        upper_grad,
        inner,
        0,
        rows,
        stats,
        gains,
    )
    joined_grad, joined_sums = joined_grad_call(
        after(queries, second_scaled), sums, table, heads
    )
    joined_bias_grad = joined_sums[0]
    order = lax.rem(me + jnp.arange(ranks, dtype=jnp.int32), ranks)
    *scaled, first_sums = first_call(
        order, joined_grad, pack, rows, stats, gains, second_scaled, ranks
    )

    inner_whole = product_call([(after(second_in, scaled[0]), upper_grad)])
    inner_out = lax.psum_scatter(inner_whole, group, scatter_dimension=0, tiled=True)

    column = jnp.concatenate([first_sums[:2], second_sums[:2], bias_grad.reshape(1, -1)])
    by_shard = [
        column.reshape(5, shards, rows_part).transpose(1, 0, 2).reshape(shards, -1),
        joined_bias_grad.reshape(heads, shards, -1).transpose(1, 0, 2).reshape(shards, -1),
        inner_bias_grad.reshape(-1, shards, inner_bias.shape[1])
        .transpose(1, 0, 2)
        .reshape(shards, -1),
    ]
    small_grads = jnp.concatenate(by_shard, axis=1)
    size = joined_width + inside
    riders = None
    if paired(group):
        riders = jnp.pad(
            small_grads.astype(BF16)[:, None, :],
            ((0, 0), (0, EXTRA - 1), (0, size - small_grads.shape[1])),
        )
    context = jnp.concatenate(contexts, axis=0)
    head_pairs = [(after(first_in, inner_whole), joined_grad), (grad_rows, context)]
    head_given = weight_grad_given(head_pairs, group, riders)
    head_pairs = [(after(first_in, head_given), joined_grad), (grad_rows, context)]
    head_terms = weight_grad_kept(head_pairs, head_given, group, riders)
    share = total_of(send_chunks(scaled, "tp"))
    lines = 2 * count // part
    means = share[count : count + lines].reshape(2, count) / width
    share = share[:count]
    own_normed = (own_tokens.astype(F32) - center) * inverse
    own_rows = lax.dynamic_slice_in_dim(grad_rows, own_start, part, 1).astype(F32)
    tokens_grad = own_rows + inverse * (
        share - means[0][:, None] - own_normed * means[1][:, None]
    )

    head_terms = [head_terms[0]] + [after(t, tokens_grad) for t in head_terms[1:]]
    head_out = total_of(head_terms)
    if riders is None:
        small_out = lax.psum_scatter(small_grads, group, scatter_dimension=0, tiled=True)[0]
    else:
        small_out = head_out[rows_part]
    vector = line_sum(small_out[: 4 * rows_part].reshape(-1, 128), "tp").reshape(4, -1)
    at = 5 * rows_part
    joined_bias_out = small_out[at : at + joined_bias.size].reshape(joined_bias.shape)
    at += joined_bias.size
    inner_bias_out = small_out[at : at + inner_bias.size].reshape(inner_bias.shape)
    bias_out = small_out[4 * rows_part : 5 * rows_part]

    return (
        layer_out.reshape(tokens.shape),
        tokens_grad.reshape(tokens.shape),
        vector[0],
        vector[1],
        head_out[:rows_part, :joined_width].reshape(joined_weight.shape),
        joined_bias_out,
        head_out[:rows_part, joined_width:].reshape(output_weight.shape),
        bias_out,
        vector[2],
        vector[3],
        inner_out.astype(F32),
        inner_bias_out,
        outer_out.astype(F32),
        bias_out,
    )


def solution(mesh):
    both = ("fsdp", "ctx")
    return jax.shard_map(
        body,
        mesh=mesh,
        in_specs=(
            P("fsdp", "ctx", "tp"),
            P("fsdp"),
            P("fsdp", "ctx", "tp"),
            P(both),
            P(both),
            P(both, "tp", None),
            P("tp", both),
            P(both, "tp", None),
            P(both),
            P(both),
            P(both),
            P(both, "tp"),
            P("tp", both),
            P(both, "tp"),
            P(both),
        ),
        out_specs=(
            P("fsdp", "ctx", "tp"),
            P("fsdp", "ctx", "tp"),
            P(both),
            P(both),
            P(both, "tp", None),
            P("tp", both),
            P(both, "tp", None),
            P(both),
            P(both),
            P(both),
            P(both, "tp"),
            P("tp", both),
            P(both, "tp"),
            P(both),
        ),
        check_vma=False,
    )
```

```python
import functools

import jax
import jax.numpy as jnp
from jax import lax
from jax.experimental import pallas as pl
from jax.experimental.pallas import tpu as pltpu
from jax.sharding import PartitionSpec as P

HEAD = 256
ROTARY = 64
F32 = jnp.float32
BF16 = jnp.bfloat16
VMEM_LIMIT = 56 << 20
HEADS_WEIGHT = 1.0
FEED_WEIGHT = 1.0
LAST_WEIGHT = 1.0
NN = (((1,), (0,)), ((), ()))
NT = (((1,), (1,)), ((), ()))
TN = (((0,), (0,)), ((), ()))


def dot(a, b, dims):
    return lax.dot_general(a, b, dims, preferred_element_type=F32)


def after(value, *earlier):
    return lax.optimization_barrier((value, earlier))[0]


def params(*semantics):
    return pltpu.CompilerParams(
        dimension_semantics=semantics or None, vmem_limit_bytes=VMEM_LIMIT
    )


def cost(flops, moved, weight=1.0):
    return pl.CostEstimate(
        flops=int(flops * weight), bytes_accessed=int(moved * weight), transcendentals=0
    )


def line_gather(piece, axis, first=None, gate=None):
    size = lax.axis_size(axis)
    up = [(i, i + 1) for i in range(size - 1)]
    down = [(i + 1, i) for i in range(size - 1)]
    right, left = [], []
    a = b = piece
    for step in range(size - 1):
        if step == 2 and gate is not None:
            a, b = after((a, b), gate)
        if step == 0 and first is not None:
            a, b = first
        else:
            a = lax.ppermute(a, axis, up)
            b = lax.ppermute(b, axis, down)
        right.append(a)
        left.append(b)
    return [(right[s - 1], left[size - s - 1]) for s in range(1, size)]


def send_chunks(chunks, axis):
    size = lax.axis_size(axis)
    return [chunks[0]] + [
        lax.ppermute(chunks[k], axis, [(i, (i + k) % size) for i in range(size)])
        for k in range(1, size)
    ]


def norm_kernel(size, me_ref, own, *refs):
    pairs = refs[: 2 * (size - 1)]
    gains, first_out, second_out, token_out, stat_out, work = refs[2 * (size - 1) :]
    part = own.shape[1]
    me = me_ref[0]
    for s in range(size):
        if s == 0:
            piece = own[...].astype(F32)
        else:
            piece = pairs[2 * s - 2][...].astype(F32) + pairs[2 * s - 1][...].astype(F32)
        at = lax.rem(me - s + size, size)
        work[:, pl.ds(pl.multiple_of(at * part, part), part)] = piece
    rows = work[...]
    token_out[...] = rows.astype(BF16)
    width = rows.shape[1]
    center = jnp.sum(rows, axis=1, keepdims=True) * (1.0 / width)
    shifted = rows - center
    inverse = lax.rsqrt(jnp.sum(shifted * shifted, axis=1, keepdims=True) * (1.0 / width) + 1e-05)
    normed = shifted * inverse
    first_out[...] = (normed * gains[0:1, :] + gains[1:2, :]).astype(BF16)
    second_out[...] = (normed * gains[2:3, :] + gains[3:4, :]).astype(BF16)
    lane = lax.broadcasted_iota(jnp.int32, stat_out.shape, 1)
    stat_out[...] = jnp.where(lane == 0, center, inverse)


def norm_call(me, own, pairs, gains, tile=128):
    count, part = own.shape
    size = len(pairs) + 1
    width = part * size
    flat = [p for pair in pairs for p in pair]
    block = pl.BlockSpec((tile, part), lambda i, *_: (i, 0))
    wide = pl.BlockSpec((tile, width), lambda i, *_: (i, 0))
    return pl.pallas_call(
        functools.partial(norm_kernel, size),
        grid_spec=pltpu.PrefetchScalarGridSpec(
            num_scalar_prefetch=1,
            grid=(count // tile,),
            in_specs=[block] * (1 + len(flat)) + [pl.BlockSpec((4, width), lambda i, *_: (0, 0))],
            out_specs=[wide, wide, wide, pl.BlockSpec((tile, 128), lambda i, *_: (i, 0))],
            scratch_shapes=[pltpu.VMEM((tile, width), F32)],
        ),
        out_shape=[
            jax.ShapeDtypeStruct((count, width), BF16),
            jax.ShapeDtypeStruct((count, width), BF16),
            jax.ShapeDtypeStruct((count, width), BF16),
            jax.ShapeDtypeStruct((count, 128), F32),
        ],
        compiler_params=params("arbitrary"),
        cost_estimate=cost(count * width * 16, count * width * 10),
        name="norm",
    )(me, own, *flat, gains)


def cot_kernel(size, local_len, tile, me_ref, len_ref, own, *refs):
    pairs = refs[: 2 * (size - 1)]
    rows_out, sum_out = refs[2 * (size - 1) :]
    part = own.shape[1]
    me, ctx = me_ref[0], me_ref[1]
    step = pl.program_id(0)
    start = step * tile
    seq = start // local_len
    length = len_ref[seq]
    position = ctx * local_len + lax.rem(start, local_len)
    position = position + lax.broadcasted_iota(jnp.int32, (tile, 1), 0)
    keep = position < length

    @pl.when(step == 0)
    def _():
        sum_out[...] = jnp.zeros_like(sum_out)

    for s in range(size):
        if s == 0:
            piece = own[...].astype(F32)
        else:
            piece = pairs[2 * s - 2][...].astype(F32) + pairs[2 * s - 1][...].astype(F32)
        piece = jnp.where(keep, piece, 0.0)
        at = lax.rem(me - s + size, size)
        cols = pl.ds(pl.multiple_of(at * part, part), part)
        rows_out[:, cols] = piece.astype(BF16)
        sum_out[0:1, cols] += jnp.sum(piece, axis=0, keepdims=True)


def cot_call(places, lengths, own, pairs, local_len, tile=256):
    count, part = own.shape
    size = len(pairs) + 1
    width = part * size
    flat = [p for pair in pairs for p in pair]
    block = pl.BlockSpec((tile, part), lambda i, *_: (i, 0))
    return pl.pallas_call(
        functools.partial(cot_kernel, size, local_len, tile),
        grid_spec=pltpu.PrefetchScalarGridSpec(
            num_scalar_prefetch=2,
            grid=(count // tile,),
            in_specs=[block] * (1 + len(flat)),
            out_specs=[
                pl.BlockSpec((tile, width), lambda i, *_: (i, 0)),
                pl.BlockSpec((8, width), lambda i, *_: (0, 0)),
            ],
        ),
        out_shape=[
            jax.ShapeDtypeStruct((count, width), BF16),
            jax.ShapeDtypeStruct((8, width), F32),
        ],
        compiler_params=params("arbitrary"),
        cost_estimate=cost(count * width * 4, count * width * 6),
        name="cotangent_rows",
    )(places, lengths, own, *flat)


def flat_rows(ref):
    value = ref[...]
    return value.reshape(value.shape[0] * value.shape[1], value.shape[2])


def joined_kernel(seqs, rows_ref, weight_ref, bias_ref, table_ref, query_ref, pair_ref):
    kind = lax.rem(pl.program_id(0), 3)
    out = dot(rows_ref[...], flat_rows(weight_ref), NN) + bias_ref[0:1, :]
    local_len = out.shape[0] // seqs

    def turned():
        front = out[:, :128]
        up = pltpu.roll(front, 128 - ROTARY // 2, 1)
        down = pltpu.roll(front, ROTARY // 2, 1)
        table = table_ref[...]
        if seqs > 1:
            table = jnp.concatenate([table] * seqs, axis=0)
        front = front * table[:, :128] + up * table[:, 128:256] + down * table[:, 256:]
        return jnp.concatenate([front, out[:, 128:]], axis=1)

    @pl.when(kind == 0)
    def _():
        query_ref[...] = (turned().astype(BF16).astype(F32) * HEAD ** (-0.5)).astype(BF16)

    @pl.when(kind == 1)
    def _():
        value = turned().astype(BF16)
        for s in range(seqs):
            pair_ref[s] = value[s * local_len : (s + 1) * local_len, :]

    @pl.when(kind == 2)
    def _():
        value = out.astype(BF16)
        for s in range(seqs):
            pair_ref[s] = value[s * local_len : (s + 1) * local_len, :]


def joined_call(rows, pack, bias, table, seqs, heads):
    count, width = rows.shape
    shards = pack.shape[0]
    local_len = count // seqs
    return pl.pallas_call(
        functools.partial(joined_kernel, seqs),
        grid=(3 * heads,),
        in_specs=[
            pl.BlockSpec((count, width), lambda j: (0, 0)),
            pl.BlockSpec((shards, width // shards, HEAD), lambda j: (0, 0, j)),
            pl.BlockSpec((8, HEAD), lambda j: (0, j)),
            pl.BlockSpec(table.shape, lambda j: (0, 0)),
        ],
        out_specs=[
            pl.BlockSpec((count, HEAD), lambda j: (0, j // 3)),
        ]
        + [
            pl.BlockSpec(
                (seqs, local_len, HEAD), lambda j: (0, 0, 2 * (j // 3) + (j % 3) // 2)
            )
        ],
        out_shape=[
            jax.ShapeDtypeStruct((count, heads * HEAD), BF16),
            jax.ShapeDtypeStruct((seqs, local_len, 2 * heads * HEAD), BF16),
        ],
        compiler_params=params("arbitrary"),
        cost_estimate=cost(6 * heads * HEAD * count * width, 2 * (count + 3 * heads * HEAD) * width),
        name="joined",
    )(rows, pack, jnp.broadcast_to(bias.reshape(1, -1), (8, bias.size)), table)


SLOTS = 4


def slot_refs(own_ref, below_ref, both_ref):
    return [own_ref, below_ref, both_ref.at[0], both_ref.at[1]]


def masked(scores, slot, first_key, first_query, length):
    keys = first_key + lax.broadcasted_iota(jnp.int32, (1, scores.shape[1]), 1)
    ok = keys < length
    if slot == 0:
        queries = first_query + lax.broadcasted_iota(jnp.int32, (scores.shape[0], 1), 0)
        ok = ok & (keys <= queries)
    return jnp.where(ok, scores, -1e30)


def forward_kernel(heads, seq, info, lens, query_ref, pair_ref, context_ref, lse_ref, *scratch):
    local_len = query_ref.shape[0]
    length = lens[seq]
    place = info[SLOTS]
    top, total, acc = scratch[:heads], scratch[heads : 2 * heads], scratch[2 * heads :]
    for slot in range(SLOTS):
        block = info[slot]
        first_key = block * local_len

        @pl.when((block >= 0) & (block <= place) & (first_key < length))
        def _():
            for head in range(heads):
                at = 2 * HEAD * head
                query = query_ref[:, HEAD * head : HEAD * (head + 1)]
                keys = pair_ref[block, :, at : at + HEAD]
                vals = pair_ref[block, :, at + HEAD : at + 2 * HEAD]
                scores = dot(query, keys, NT)
                scores = masked(scores, slot, first_key, place * local_len, length)
                best = jnp.max(scores, axis=1, keepdims=True)
                if slot > 0:
                    best = jnp.maximum(best, top[head][...])
                weights = jnp.exp(scores - best)
                summed = jnp.sum(weights, axis=1, keepdims=True)
                mixed = dot(weights.astype(BF16), vals, NN)
                if slot > 0:
                    scale = jnp.exp(top[head][...] - best)
                    summed = summed + total[head][...] * scale
                    mixed = mixed + acc[head][...] * scale
                top[head][...] = best
                total[head][...] = summed
                acc[head][...] = mixed

        if slot == 0:

            @pl.when(first_key >= length)
            def _():
                for head in range(heads):
                    top[head][...] = jnp.full_like(top[head], -1e30)
                    total[head][...] = jnp.zeros_like(total[head])
                    acc[head][...] = jnp.zeros_like(acc[head])

    for head in range(heads):
        cols = slice(HEAD * head, HEAD * (head + 1))
        context_ref[:, cols] = (acc[head][...] / total[head][...]).astype(BF16)
        lse = top[head][...] + jnp.log(total[head][...])
        lse_ref[:, 128 * head : 128 * (head + 1)] = jnp.broadcast_to(lse, (local_len, 128))


def forward_call(info, lengths, query, pairs, seq, heads):
    local_len = pairs.shape[2]
    return pl.pallas_call(
        functools.partial(forward_kernel, heads, seq),
        grid_spec=pltpu.PrefetchScalarGridSpec(
            num_scalar_prefetch=2,
            grid=(1,),
            in_specs=[
                pl.BlockSpec((local_len, heads * HEAD), lambda i, *_: (seq, 0)),
                pl.BlockSpec(
                    (SLOTS, None, local_len, 2 * heads * HEAD), lambda i, *_: (0, seq, 0, 0)
                ),
            ],
            out_specs=[
                pl.BlockSpec((local_len, heads * HEAD), lambda i, *_: (0, 0)),
                pl.BlockSpec((local_len, heads * 128), lambda i, *_: (0, 0)),
            ],
            scratch_shapes=[pltpu.VMEM((local_len, 1), F32)] * (2 * heads)
            + [pltpu.VMEM((local_len, HEAD), F32)] * heads,
        ),
        out_shape=[
            jax.ShapeDtypeStruct((local_len, heads * HEAD), BF16),
            jax.ShapeDtypeStruct((local_len, heads * 128), F32),
        ],
        compiler_params=params("arbitrary"),
        cost_estimate=cost(4 * local_len * heads * HEAD * local_len * SLOTS,
            4 * local_len * heads * HEAD * SLOTS, HEADS_WEIGHT),
        name="attention_forward",
    )(info, lengths, query, pairs)


def backward_kernel(
    heads, seq, info, lens, query_ref, context_ref, grad_ref, lse_ref, pair_ref, query_out, *refs
):
    local_len = query_ref.shape[0]
    pair_outs = slot_refs(*refs[:3])
    accs = refs[3:]
    length = lens[seq]
    place = info[SLOTS]
    for slot in range(SLOTS):
        block = info[slot]
        first_key = block * local_len
        seen = (block >= 0) & (block <= place) & (first_key < length)

        @pl.when(seen)
        def _():
            for head in range(heads):
                at = 2 * HEAD * head
                cols = slice(HEAD * head, HEAD * (head + 1))
                query, grad = query_ref[:, cols], grad_ref[:, cols]
                keys = pair_ref[block, :, at : at + HEAD]
                vals = pair_ref[block, :, at + HEAD : at + 2 * HEAD]
                shared = grad.astype(F32) * context_ref[:, cols].astype(F32)
                shared = jnp.sum(shared, axis=1, keepdims=True)
                scores = dot(query, keys, NT)
                scores = masked(scores, slot, first_key, place * local_len, length)
                probs = jnp.exp(scores - lse_ref[:, 128 * head : 128 * head + 1])
                score_grad = (probs * (dot(grad, vals, NT) - shared)).astype(BF16)
                pair_outs[slot][:, at : at + HEAD] = dot(score_grad, query, TN).astype(BF16)
                pair_outs[slot][:, at + HEAD : at + 2 * HEAD] = dot(
                    probs.astype(BF16), grad, TN
                ).astype(BF16)
                mixed = dot(score_grad, keys, NN)
                accs[head][...] = mixed if slot == 0 else accs[head][...] + mixed

        @pl.when(jnp.logical_not(seen))
        def _():
            pair_outs[slot][...] = jnp.zeros_like(pair_outs[slot])
            if slot == 0:
                for head in range(heads):
                    accs[head][...] = jnp.zeros_like(accs[head])

    for head in range(heads):
        query_out[:, HEAD * head : HEAD * (head + 1)] = (
            accs[head][...] * HEAD ** (-0.5)
        ).astype(BF16)


def backward_call(info, lengths, query, context, grad, lse, pairs, seq, heads):
    local_len = pairs.shape[2]
    here = pl.BlockSpec((local_len, heads * HEAD), lambda i, *_: (seq, 0))
    one = pl.BlockSpec((local_len, heads * HEAD), lambda i, *_: (0, 0))
    two = [pl.BlockSpec((local_len, 2 * heads * HEAD), lambda i, *_: (0, 0))] * 2
    two = two + [pl.BlockSpec((2, local_len, 2 * heads * HEAD), lambda i, *_: (0, 0, 0))]
    return pl.pallas_call(
        functools.partial(backward_kernel, heads, seq),
        grid_spec=pltpu.PrefetchScalarGridSpec(
            num_scalar_prefetch=2,
            grid=(1,),
            in_specs=[
                here,
                one,
                here,
                pl.BlockSpec((local_len, heads * 128), lambda i, *_: (0, 0)),
                pl.BlockSpec(
                    (SLOTS, None, local_len, 2 * heads * HEAD), lambda i, *_: (0, seq, 0, 0)
                ),
            ],
            out_specs=[one] + two,
            scratch_shapes=[pltpu.VMEM((local_len, HEAD), F32)] * heads,
        ),
        out_shape=[jax.ShapeDtypeStruct((local_len, heads * HEAD), BF16)]
        + [jax.ShapeDtypeStruct((local_len, 2 * heads * HEAD), BF16)] * 2
        + [jax.ShapeDtypeStruct((2, local_len, 2 * heads * HEAD), BF16)],
        compiler_params=params("arbitrary"),
        cost_estimate=cost(10 * local_len * heads * HEAD * local_len * SLOTS,
            8 * local_len * heads * HEAD * SLOTS, HEADS_WEIGHT),
        name="attention_backward",
    )(info, lengths, query, context, grad, lse, pairs)


def return_pairs(own, below, siblings, axis):
    taken = lax.ppermute(siblings, axis, [(0, 1), (1, 0), (2, 3), (3, 2)])
    lower = (below.astype(F32) + taken[1].astype(F32)).astype(BF16)
    above = lax.ppermute(lower, axis, [(2, 0), (3, 1)])
    return [own, taken, above], taken


def branch_kernel(parts, active_ref, *refs):
    context_refs, (outer_ref, output_ref, out_ref) = refs[:parts], refs[parts:]
    out = dot(active_ref[...], outer_ref[...], NT)
    context = jnp.concatenate([ref[...] for ref in context_refs], axis=0)
    out_ref[...] = (out + dot(context, flat_rows(output_ref), NT)).astype(BF16)


def branch_call(active, contexts, outer, pack, column, tile=512):
    count, hidden = active.shape
    width, inside = outer.shape[0], contexts[0].shape[1]
    rows = width // pack.shape[0]
    return pl.pallas_call(
        functools.partial(branch_kernel, len(contexts)),
        grid=(width // tile,),
        in_specs=[pl.BlockSpec((count, hidden), lambda j: (0, 0))]
        + [pl.BlockSpec(c.shape, lambda j: (0, 0)) for c in contexts]
        + [
            pl.BlockSpec((tile, hidden), lambda j: (j, 0)),
            pl.BlockSpec((tile // rows, rows, inside), lambda j: (j, 0, column)),
        ],
        out_specs=pl.BlockSpec((count, tile), lambda j: (0, j)),
        out_shape=jax.ShapeDtypeStruct((count, width), BF16),
        compiler_params=params("arbitrary"),
        cost_estimate=cost(2 * count * width * (hidden + inside), 2 * width * (hidden + inside), HEADS_WEIGHT),
        name="branch",
    )(active, *contexts, outer, pack)


def upper_kernel(rows_ref, weight_ref, bias_ref, active_ref, slope_ref):
    weight = flat_rows(weight_ref)
    bias = bias_ref[0:1, :]
    count = rows_ref.shape[0]
    piece = count // 4
    for i in range(4):
        here = slice(i * piece, (i + 1) * piece)
        upper = dot(rows_ref[here, :], weight, NN) + bias
        phi = 0.5 * (1.0 + lax.erf(upper * 0.7071067811865476))
        slope = phi + upper * jnp.exp(-0.5 * upper * upper) * 0.3989422804014327
        active_ref[here, :] = (upper * phi).astype(BF16)
        slope_ref[here, :] = slope.astype(BF16)


def upper_call(rows, pack, bias, column, tile=512):
    count, width = rows.shape
    hidden = bias.size
    shards = pack.shape[0]
    out = pl.BlockSpec((count, tile), lambda j: (0, j))
    first = column // tile
    return pl.pallas_call(
        upper_kernel,
        grid=(hidden // tile,),
        in_specs=[
            pl.BlockSpec((count, width), lambda j: (0, 0)),
            pl.BlockSpec((shards, width // shards, tile), lambda j: (0, 0, first + j)),
            pl.BlockSpec((8, tile), lambda j: (0, j)),
        ],
        out_specs=[out, out],
        out_shape=[jax.ShapeDtypeStruct((count, hidden), BF16)] * 2,
        compiler_params=params("arbitrary"),
        cost_estimate=cost(2 * count * width * hidden, 2 * width * (count + hidden)),
        name="upper",
    )(rows, pack, jnp.broadcast_to(bias.reshape(1, -1), (8, hidden)))


def upper_grad_kernel(rows_ref, weight_ref, slope_ref, out_ref, sum_ref):
    grad = dot(rows_ref[...], weight_ref[...], NN) * slope_ref[...].astype(F32)
    low = grad.astype(BF16)
    out_ref[...] = low
    sum_ref[...] = jnp.broadcast_to(
        jnp.sum(low.astype(F32), axis=0, keepdims=True), sum_ref.shape
    )


def upper_grad_call(rows, weight, slope, tile=512):
    count, width = rows.shape
    hidden = weight.shape[1]
    out = pl.BlockSpec((count, tile), lambda j: (0, j))
    return pl.pallas_call(
        upper_grad_kernel,
        grid=(hidden // tile,),
        in_specs=[
            pl.BlockSpec((count, width), lambda j: (0, 0)),
            pl.BlockSpec((width, tile), lambda j: (0, j)),
            out,
        ],
        out_specs=[out, pl.BlockSpec((8, tile), lambda j: (0, j))],
        out_shape=[
            jax.ShapeDtypeStruct((count, hidden), BF16),
            jax.ShapeDtypeStruct((8, hidden), F32),
        ],
        compiler_params=params("arbitrary"),
        cost_estimate=cost(2 * count * width * hidden, 2 * width * (2 * count + hidden), FEED_WEIGHT),
        name="upper_grad",
    )(rows, weight, slope)


def context_grad_kernel(rows_ref, weight_ref, out_ref):
    out_ref[...] = dot(rows_ref[...], flat_rows(weight_ref), NN).astype(BF16)


def context_grad_call(rows, pack, column, inside, tile=512):
    count, width = rows.shape
    return pl.pallas_call(
        context_grad_kernel,
        grid=(count // tile,),
        in_specs=[
            pl.BlockSpec((tile, width), lambda i: (i, 0)),
            pl.BlockSpec(
                (pack.shape[0], width // pack.shape[0], inside), lambda i: (0, 0, column)
            ),
        ],
        out_specs=pl.BlockSpec((tile, inside), lambda i: (i, 0)),
        out_shape=jax.ShapeDtypeStruct((count, inside), BF16),
        compiler_params=params("arbitrary"),
        cost_estimate=cost(2 * count * width * inside, 2 * width * (count + inside), HEADS_WEIGHT),
        name="context_grad",
    )(rows, pack)


def column_sums(grad, normed, out_ref):
    count, tile = grad.shape
    out_ref[0:1, :] = jnp.sum(grad * normed, axis=0, keepdims=True)
    out_ref[1:2, :] = jnp.sum(grad, axis=0, keepdims=True)
    out_ref[2:8, :] = jnp.zeros((6, tile), F32)


def second_kernel(grad_ref, weight_ref, rows_ref, stat_ref, gain_ref, out_ref, sum_ref):
    grad = dot(grad_ref[...], flat_rows(weight_ref), NT)
    normed = (rows_ref[...].astype(F32) - stat_ref[:, 0:1]) * stat_ref[:, 1:2]
    column_sums(grad, normed, sum_ref)
    out_ref[...] = (grad * gain_ref[2:3, :]).astype(BF16)


def second_call(grad, pack, column, rows, stats, gains, tile=512):
    count, hidden = grad.shape
    width = rows.shape[1]
    deep = width // pack.shape[0]
    return pl.pallas_call(
        second_kernel,
        grid=(width // tile,),
        in_specs=[
            pl.BlockSpec((count, hidden), lambda j: (0, 0)),
            pl.BlockSpec((tile // deep, deep, hidden), lambda j: (j, 0, column)),
            pl.BlockSpec((count, tile), lambda j: (0, j)),
            pl.BlockSpec((count, 128), lambda j: (0, 0)),
            pl.BlockSpec((4, tile), lambda j: (0, j)),
        ],
        out_specs=[
            pl.BlockSpec((count, tile), lambda j: (0, j)),
            pl.BlockSpec((8, tile), lambda j: (0, j)),
        ],
        out_shape=[
            jax.ShapeDtypeStruct((count, width), BF16),
            jax.ShapeDtypeStruct((8, width), F32),
        ],
        compiler_params=params("arbitrary"),
        cost_estimate=cost(2 * count * width * hidden, 2 * (width * hidden + 3 * count * width), LAST_WEIGHT),
        name="second_in_grad",
    )(grad, pack, rows, stats, gains)


def joined_grad_kernel(heads, *refs):
    (table_ref, out_ref, sum_ref), refs = refs[-3:], refs[:-3]
    table = table_ref[...]
    local_len = table.shape[0]

    def back(value):
        front = value[:, :128]
        up = pltpu.roll(front, 128 - ROTARY // 2, 1)
        down = pltpu.roll(front, ROTARY // 2, 1)
        front = front * table[:, :128] - up * table[:, 128:256] - down * table[:, 256:]
        return jnp.concatenate([front, value[:, 128:]], axis=1)

    sum_ref[...] = jnp.zeros_like(sum_ref)
    for seq in range(len(refs) // 4):
        query_ref, own_ref, near_ref, far_ref = refs[4 * seq : 4 * seq + 4]
        here = slice(seq * local_len, (seq + 1) * local_len)
        for head in range(heads):
            at = 3 * HEAD * head
            pair = slice(2 * HEAD * head, 2 * HEAD * (head + 1))
            total = own_ref[:, pair].astype(F32) + near_ref[0, :, pair].astype(F32)
            total = total + far_ref[:, pair].astype(F32)
            query = query_ref[:, HEAD * head : HEAD * (head + 1)].astype(F32)
            parts = [back(query), back(total[:, :HEAD]), total[:, HEAD:]]
            for i, part in enumerate(parts):
                cols = slice(at + HEAD * i, at + HEAD * (i + 1))
                low = part.astype(BF16)
                out_ref[here, cols] = low
                sum_ref[0:1, cols] += jnp.sum(low.astype(F32), axis=0, keepdims=True)


def joined_grad_call(queries, sums, table, heads):
    seqs = len(queries)
    count = seqs * queries[0].shape[0]
    width = 3 * heads * HEAD
    flat = [a for query, three in zip(queries, sums) for a in (query, *three)]
    return pl.pallas_call(
        functools.partial(joined_grad_kernel, heads),
        out_shape=[
            jax.ShapeDtypeStruct((count, width), BF16),
            jax.ShapeDtypeStruct((8, width), F32),
        ],
        compiler_params=params(),
        cost_estimate=cost(10 * count * width, 10 * count * width, LAST_WEIGHT),
        name="joined_grad",
    )(*flat, table)


EXTRA = 8


def first_kernel(ranks, order, grad_ref, weight_ref, rows_ref, stat_ref, gain_ref, second_ref, *refs):
    out_refs, (sum_ref, row_ref) = refs[:ranks], refs[ranks:]
    step = pl.program_id(0)
    grad = dot(grad_ref[...], flat_rows(weight_ref), NT)
    count, tile = grad.shape
    normed = (rows_ref[...].astype(F32) - stat_ref[:, 0:1]) * stat_ref[:, 1:2]
    column_sums(grad, normed, sum_ref)
    total = grad * gain_ref[0:1, :] + second_ref[...].astype(F32)
    low = total.astype(BF16)
    for k in range(ranks):

        @pl.when(step == k)
        def _():
            out_refs[k][:count, :] = low

    plain = jnp.sum(total, axis=1, keepdims=True)
    along = jnp.sum(total * normed, axis=1, keepdims=True)
    lane = lax.broadcasted_iota(jnp.int32, row_ref.shape, 1)
    both = jnp.where(lane == 0, plain, along)

    @pl.when(step == 0)
    def _():
        row_ref[...] = both

    @pl.when(step > 0)
    def _():
        row_ref[...] += both

    @pl.when(step == ranks - 1)
    def _():
        turned = row_ref[...].T
        lines = [turned[i : i + 1, j : j + tile] for i in (0, 1) for j in range(0, count, tile)]
        lines.append(jnp.zeros((EXTRA - len(lines), tile), F32))
        extra = jnp.concatenate(lines, axis=0).astype(BF16)
        for ref in out_refs:
            ref[count:, :] = extra


def first_call(order, grad, pack, rows, stats, gains, second, ranks):
    count, inside = grad.shape
    width = rows.shape[1]
    tile = width // ranks
    deep = width // pack.shape[0]
    return pl.pallas_call(
        functools.partial(first_kernel, ranks),
        grid_spec=pltpu.PrefetchScalarGridSpec(
            num_scalar_prefetch=1,
            grid=(ranks,),
            in_specs=[
                pl.BlockSpec((count, inside), lambda j, _: (0, 0)),
                pl.BlockSpec((tile // deep, deep, inside), lambda j, order: (order[j], 0, 0)),
                pl.BlockSpec((count, tile), lambda j, order: (0, order[j])),
                pl.BlockSpec((count, 128), lambda j, _: (0, 0)),
                pl.BlockSpec((4, tile), lambda j, order: (0, order[j])),
                pl.BlockSpec((count, tile), lambda j, order: (0, order[j])),
            ],
            out_specs=[pl.BlockSpec((count + EXTRA, tile), lambda j, _: (0, 0))] * ranks
            + [pl.BlockSpec((8, tile), lambda j, order: (0, order[j]))],
            scratch_shapes=[pltpu.VMEM((count, 128), F32)],
        ),
        out_shape=[jax.ShapeDtypeStruct((count + EXTRA, tile), BF16)] * ranks
        + [jax.ShapeDtypeStruct((8, width), F32)],
        compiler_params=params("arbitrary"),
        cost_estimate=cost(2 * count * width * inside, 2 * (width * inside + 4 * count * width), LAST_WEIGHT),
        name="first_in_grad",
    )(order, grad, pack, rows, stats, gains, second)


def flips(size, by):
    return [(i, i ^ by) for i in range(size)]


def paired(group):
    return lax.axis_size(group[0]) == 2 and lax.axis_size(group[1]) == 4


def member(group):
    return lax.axis_size(group[1]) * lax.axis_index(group[0]) + lax.axis_index(group[1])


def gather_small(vector, group):
    if not paired(group):
        return lax.all_gather(vector.reshape(1, 1, -1), group, axis=0, tiled=True)[:, 0]
    rows = jnp.zeros((8, vector.size), vector.dtype)
    rows = lax.dynamic_update_slice_in_dim(rows, vector.reshape(1, -1), member(group), 0)
    for by in (1, 2, 4):
        rows = rows + lax.ppermute(rows, group, flips(8, by))
    return rows


def weight_grad_kernel(sizes, outs, small, order, *refs):
    parts = len(sizes)
    lhs_refs, rhs_refs, refs = refs[: 4 * parts], refs[4 * parts : 5 * parts], refs[5 * parts :]
    small_ref = refs[0] if small else None
    add_ref = refs[small] if outs > 1 else None
    out_refs, turned = refs[-1 - outs : -1], refs[-1]
    rows = lhs_refs[0].shape[1]
    deep = rows + EXTRA * small
    step = pl.program_id(0)

    def put(k, value, start):
        height = value.shape[0]
        if outs == 1:
            out_refs[0][k * deep + start : k * deep + start + height, :] = value.astype(BF16)
        else:
            add = add_ref[k * deep + start : k * deep + start + height, :].astype(F32)
            out_refs[k][start : start + height, :] = (value + add).astype(BF16)

    first = 0
    for i, size in enumerate(sizes):
        lhs, rhs_ref = lhs_refs[4 * i : 4 * i + 4], rhs_refs[i]

        @pl.when(step == first)
        def _():
            for k in range(4):
                turned[k * rows : (k + 1) * rows, :] = lhs[k][...].T

        @pl.when((step >= first) & (step < first + size))
        def _():
            out = dot(turned[...], rhs_ref[...], NN)
            for k in range(4):
                put(k, out[k * rows : (k + 1) * rows, :], 0)

        first += size
    if small:
        for k in range(4):
            put(k, small_ref[order[k]], rows)


def weight_grad_call(order, pairs, add=None, small=None, tile=512):
    count, width = pairs[0][0].shape
    rows = width // 8
    sizes = [rhs.shape[1] // tile for _, rhs in pairs]
    total = sum(sizes) * tile
    outs = 1 if add is None else 4
    height = rows if small is None else rows + EXTRA
    deep = 4 * height if add is None else height
    firsts = [sum(sizes[:i]) for i in range(len(sizes))]

    def column(k):
        return pl.BlockSpec((count, rows), lambda j, order: (0, order[k]))

    def piece(first, size):
        return pl.BlockSpec(
            (count, tile), lambda j, _: (0, jnp.minimum(jnp.maximum(j - first, 0), size - 1))
        )

    out = pl.BlockSpec((deep, tile), lambda j, *_: (0, j))
    extra_specs, extra = [], []
    if small is not None:
        extra_specs.append(pl.BlockSpec((8, EXTRA, tile), lambda j, *_: (0, 0, j)))
        extra.append(small)
    if add is not None:
        extra_specs.append(pl.BlockSpec((4 * height, tile), lambda j, *_: (0, j)))
        extra.append(add)
    return pl.pallas_call(
        functools.partial(weight_grad_kernel, sizes, outs, int(small is not None)),
        grid_spec=pltpu.PrefetchScalarGridSpec(
            num_scalar_prefetch=1,
            grid=(sum(sizes),),
            in_specs=[column(k) for _ in pairs for k in range(4)]
            + [piece(f, n) for f, n in zip(firsts, sizes)]
            + extra_specs,
            out_specs=[out] * outs,
            scratch_shapes=[pltpu.VMEM((4 * rows, count), BF16)],
        ),
        out_shape=[jax.ShapeDtypeStruct((deep, total), BF16)] * outs,
        compiler_params=params("arbitrary"),
        cost_estimate=cost(8 * rows * count * total, 2 * (count * (4 * rows + total) + 8 * rows * total), LAST_WEIGHT),
        name="weight_grad",
    )(
        order,
        *[lhs for lhs, _ in pairs for _ in range(4)],
        *[rhs for _, rhs in pairs],
        *extra,
    )


def product_kernel(sizes, *refs):
    parts = len(sizes)
    lhs_refs, rhs_refs = refs[:parts], refs[parts : 2 * parts]
    out_ref, turned = refs[2 * parts :]
    step = pl.program_id(0)
    first = 0
    for lhs_ref, rhs_ref, size in zip(lhs_refs, rhs_refs, sizes):

        @pl.when(step == first)
        def _():
            turned[...] = lhs_ref[...].T

        @pl.when((step >= first) & (step < first + size))
        def _():
            out_ref[...] = dot(turned[...], rhs_ref[...], NN).astype(BF16)

        first += size


def product_call(pairs, tile=512):
    count, width = pairs[0][0].shape
    sizes = [rhs.shape[1] // tile for _, rhs in pairs]
    total = sum(sizes) * tile
    firsts = [sum(sizes[:i]) for i in range(len(sizes))]

    def piece(first, size):
        return pl.BlockSpec(
            (count, tile), lambda j: (0, jnp.minimum(jnp.maximum(j - first, 0), size - 1))
        )

    return pl.pallas_call(
        functools.partial(product_kernel, sizes),
        grid=(sum(sizes),),
        in_specs=[pl.BlockSpec((count, width), lambda j: (0, 0)) for _ in pairs]
        + [piece(f, n) for f, n in zip(firsts, sizes)],
        out_specs=pl.BlockSpec((width, tile), lambda j: (0, j)),
        out_shape=jax.ShapeDtypeStruct((width, total), BF16),
        scratch_shapes=[pltpu.VMEM((width, count), BF16)],
        compiler_params=params("arbitrary"),
        cost_estimate=cost(2 * width * count * total, 2 * (count * (width + total) + width * total), FEED_WEIGHT),
        name="product",
    )(*[lhs for lhs, _ in pairs], *[rhs for _, rhs in pairs])


STEPS = (0, 2, 4, 6)


def weight_grad_given(pairs, group, small=None):
    if not paired(group):
        return None
    steps = jnp.array(STEPS, jnp.int32)
    (given,) = weight_grad_call((member(group) ^ 1) ^ steps, pairs, small=small)
    return given


def weight_grad_kept(pairs, given, group, small=None):
    if not paired(group):
        whole = jnp.concatenate([dot(lhs, rhs, TN).astype(BF16) for lhs, rhs in pairs], axis=1)
        return [lax.psum_scatter(whole, group, scatter_dimension=0, tiled=True)]
    taken = lax.ppermute(given, group, flips(8, 1))
    sums = weight_grad_call(
        member(group) ^ jnp.array(STEPS, jnp.int32), pairs, taken, small=small
    )
    return [sums[0]] + [
        lax.ppermute(part, group, flips(8, by)) for part, by in zip(sums[1:], STEPS[1:])
    ]


def total_of(terms):
    return functools.reduce(lambda a, b: a + b, [t.astype(F32) for t in terms])


def line_sum(value, axis):
    size = lax.axis_size(axis)
    terms = [value]
    for step in range(1, size):
        terms.append(lax.ppermute(value, axis, [(i, (i + step) % size) for i in range(size)]))
    return functools.reduce(lambda a, b: a + b, terms)


def body(
    tokens,
    lengths,
    cotangent,
    first_gain,
    first_shift,
    joined_weight,
    joined_bias,
    output_weight,
    output_bias,
    second_gain,
    second_shift,
    inner_weight,
    inner_bias,
    outer_weight,
    outer_bias,
):
    group = ("fsdp", "ctx")
    seqs, local_len, part = tokens.shape
    count = seqs * local_len
    ranks = lax.axis_size("tp")
    width = part * ranks
    shards = lax.axis_size("fsdp") * lax.axis_size("ctx")
    rows_part = width // shards
    heads = joined_weight.shape[1]
    hidden = inner_weight.shape[1]
    me, ctx = lax.axis_index("tp"), lax.axis_index("ctx")

    own_tokens, own_cot = tokens.reshape(count, part), cotangent.reshape(count, part)
    joined_width, inside = heads * 3 * HEAD, heads * HEAD
    vectors = [first_gain, first_shift, second_gain, second_shift, output_bias, outer_bias]
    flat = jnp.concatenate(vectors + [joined_bias.reshape(-1), inner_bias.reshape(-1)])
    small = gather_small(jnp.pad(flat, (0, -flat.size % 256)), group)
    shard = jnp.concatenate(
        [joined_weight.reshape(rows_part, -1), output_weight.reshape(rows_part, -1)], axis=1
    )
    token_pairs = line_gather(own_tokens, "tp")
    cot_start = after(own_cot, token_pairs)
    cot_first = (
        lax.ppermute(cot_start, "tp", [(i, i + 1) for i in range(ranks - 1)]),
        lax.ppermute(cot_start, "tp", [(i + 1, i) for i in range(ranks - 1)]),
    )
    pack = lax.all_gather(shard, group, axis=0, tiled=False)
    inner = lax.all_gather(inner_weight, group, axis=0, tiled=False)

    small = small.astype(F32)
    whole = [small[:, i * rows_part : (i + 1) * rows_part].reshape(width) for i in range(6)]
    at = 6 * rows_part
    whole_joined_bias = (
        small[:, at : at + joined_bias.size]
        .reshape((shards,) + joined_bias.shape)
        .transpose(1, 0, 2)
        .reshape(-1)
    )
    at += joined_bias.size
    whole_inner_bias = (
        small[:, at : at + inner_bias.size]
        .reshape((shards,) + inner_bias.shape)
        .transpose(1, 0, 2)
        .reshape(-1)
    )
    gains = jnp.stack(whole[:4])

    places = jnp.stack([me, ctx]).astype(jnp.int32)
    first_in, second_in, rows, stats = norm_call(places[:1], own_tokens, token_pairs, gains)
    center, inverse = stats[:, 0:1], stats[:, 1:2]
    positions = ctx * local_len + jnp.arange(local_len, dtype=jnp.int32)
    half = ROTARY // 2
    frequency = 1.0 / 10000.0 ** (jnp.arange(half, dtype=F32) * 2.0 / ROTARY)
    angles = positions.astype(F32)[:, None] * frequency[None, :]
    cosine, sine = jnp.cos(angles), jnp.sin(angles)
    ones = jnp.ones((local_len, 128 - ROTARY), F32)
    nothing = jnp.zeros((local_len, half), F32)
    blank = jnp.zeros((local_len, 128 - ROTARY), F32)
    table = jnp.concatenate(
        [cosine, cosine, ones, -sine, nothing, blank, nothing, sine, blank], axis=1
    )
    query, pair = joined_call(after(first_in, cot_first), pack, whole_joined_bias, table, seqs, heads)
    pairs = lax.all_gather(pair, "ctx", axis=0, tiled=False)
    low, odd = ctx - 2, ctx + 1 - 2 * lax.rem(ctx, 2)
    info = jnp.stack([ctx, low, odd, jnp.where(low >= 0, odd - 2, -1), ctx]).astype(jnp.int32)
    active, slope = upper_call(after(second_in, query), inner, whole_inner_bias, 0)
    cot_pairs = line_gather(cot_start, "tp", cot_first, active)
    grad_rows, bias_sums = cot_call(places, after(lengths, active), own_cot, cot_pairs, local_len)
    bias_grad = bias_sums[0]
    outer = lax.all_gather(after(outer_weight, grad_rows, pairs), group, axis=0, tiled=True)
    contexts, lses = [], []
    ready = after(query, grad_rows)
    for seq in range(seqs):
        context, lse = forward_call(info, lengths, ready, pairs, seq, heads)
        ready = after(query, context)
        contexts.append(context)
        lses.append(lse)

    context_grad = context_grad_call(after(grad_rows, ready), pack, joined_width // inside, inside)
    queries, sums = [], []
    for seq in range(seqs):
        query_grad, *pair_grads = backward_call(
            info, lengths, ready, contexts[seq], context_grad, lses[seq], pairs, seq, heads
        )
        ready = after(query, query_grad)
        queries.append(query_grad)
        three, taken = return_pairs(*pair_grads, "ctx")
        sums.append(three)
    branch = branch_call(
        after(active, query_grad, taken), contexts, outer, pack, joined_width // inside
    )
    summed = lax.psum_scatter(branch, "tp", scatter_dimension=1, tiled=True).astype(F32)
    own_start = me * part
    own_bias = lax.dynamic_slice_in_dim(whole[4] + whole[5], own_start, part)
    valid = (positions[None, :] < lengths[:, None]).astype(F32).reshape(count, 1)
    layer_out = (valid * (own_tokens.astype(F32) + summed + own_bias)).astype(BF16)

    outer_whole = product_call([(after(grad_rows, branch), active)])
    outer_out = lax.psum_scatter(outer_whole, group, scatter_dimension=0, tiled=True)
    grad_late = after(grad_rows, outer_whole)
    upper_grad, upper_sums = upper_grad_call(grad_late, outer, slope)
    inner_bias_grad = upper_sums[0]
    second_scaled, second_sums = second_call(
        upper_grad,
        inner,
        0,
        rows,
        stats,
        gains,
    )
    joined_grad, joined_sums = joined_grad_call(
        after(queries, second_scaled), sums, table, heads
    )
    joined_bias_grad = joined_sums[0]
    order = lax.rem(me + jnp.arange(ranks, dtype=jnp.int32), ranks)
    *scaled, first_sums = first_call(
        order, joined_grad, pack, rows, stats, gains, second_scaled, ranks
    )

    column = jnp.concatenate([first_sums[:2], second_sums[:2], bias_grad.reshape(1, -1)])
    by_shard = [
        column.reshape(5, shards, rows_part).transpose(1, 0, 2).reshape(shards, -1),
        joined_bias_grad.reshape(heads, shards, -1).transpose(1, 0, 2).reshape(shards, -1),
        inner_bias_grad.reshape(-1, shards, inner_bias.shape[1])
        .transpose(1, 0, 2)
        .reshape(shards, -1),
    ]
    small_grads = jnp.concatenate(by_shard, axis=1)
    size = joined_width + inside
    riders = None
    if paired(group):
        riders = jnp.pad(
            small_grads.astype(BF16)[:, None, :],
            ((0, 0), (0, EXTRA - 1), (0, size - small_grads.shape[1])),
        )
    context = jnp.concatenate(contexts, axis=0)
    head_pairs = [(after(first_in, scaled[0]), joined_grad), (grad_rows, context)]
    head_given = weight_grad_given(head_pairs, group, riders)
    inner_whole = product_call([(after(second_in, head_given), upper_grad)])
    inner_out = lax.psum_scatter(inner_whole, group, scatter_dimension=0, tiled=True)
    head_pairs = [(after(first_in, head_given, inner_whole), joined_grad), (grad_rows, context)]
    head_terms = weight_grad_kept(head_pairs, head_given, group, riders)
    share = total_of(send_chunks(scaled, "tp"))
    lines = 2 * count // part
    means = share[count : count + lines].reshape(2, count) / width
    share = share[:count]
    own_normed = (own_tokens.astype(F32) - center) * inverse
    own_rows = lax.dynamic_slice_in_dim(grad_rows, own_start, part, 1).astype(F32)
    tokens_grad = own_rows + inverse * (
        share - means[0][:, None] - own_normed * means[1][:, None]
    )

    head_terms = [head_terms[0]] + [after(t, tokens_grad) for t in head_terms[1:]]
    head_out = total_of(head_terms)
    if riders is None:
        small_out = lax.psum_scatter(small_grads, group, scatter_dimension=0, tiled=True)[0]
    else:
        small_out = head_out[rows_part]
    vector = line_sum(small_out[: 4 * rows_part].reshape(-1, 128), "tp").reshape(4, -1)
    at = 5 * rows_part
    joined_bias_out = small_out[at : at + joined_bias.size].reshape(joined_bias.shape)
    at += joined_bias.size
    inner_bias_out = small_out[at : at + inner_bias.size].reshape(inner_bias.shape)
    bias_out = small_out[4 * rows_part : 5 * rows_part]

    return (
        layer_out.reshape(tokens.shape),
        tokens_grad.reshape(tokens.shape),
        vector[0],
        vector[1],
        head_out[:rows_part, :joined_width].reshape(joined_weight.shape),
        joined_bias_out,
        head_out[:rows_part, joined_width:].reshape(output_weight.shape),
        bias_out,
        vector[2],
        vector[3],
        inner_out.astype(F32),
        inner_bias_out,
        outer_out.astype(F32),
        bias_out,
    )


def solution(mesh):
    both = ("fsdp", "ctx")
    return jax.shard_map(
        body,
        mesh=mesh,
        in_specs=(
            P("fsdp", "ctx", "tp"),
            P("fsdp"),
            P("fsdp", "ctx", "tp"),
            P(both),
            P(both),
            P(both, "tp", None),
            P("tp", both),
            P(both, "tp", None),
            P(both),
            P(both),
            P(both),
            P(both, "tp"),
            P("tp", both),
            P(both, "tp"),
            P(both),
        ),
        out_specs=(
            P("fsdp", "ctx", "tp"),
            P("fsdp", "ctx", "tp"),
            P(both),
            P(both),
            P(both, "tp", None),
            P("tp", both),
            P(both, "tp", None),
            P(both),
            P(both),
            P(both),
            P(both, "tp"),
            P("tp", both),
            P(both, "tp"),
            P(both),
        ),
        check_vma=False,
    )
```

```python
import functools

import jax
import jax.numpy as jnp
from jax import lax
from jax.experimental import pallas as pl
from jax.experimental.pallas import tpu as pltpu
from jax.sharding import PartitionSpec as P

HEAD = 256
ROTARY = 64
F32 = jnp.float32
BF16 = jnp.bfloat16
VMEM_LIMIT = 56 << 20
HEADS_WEIGHT = 1.0
FEED_WEIGHT = 1.0
LAST_WEIGHT = 1.0
NN = (((1,), (0,)), ((), ()))
NT = (((1,), (1,)), ((), ()))
TN = (((0,), (0,)), ((), ()))


def dot(a, b, dims):
    return lax.dot_general(a, b, dims, preferred_element_type=F32)


def after(value, *earlier):
    return lax.optimization_barrier((value, earlier))[0]


def params(*semantics):
    return pltpu.CompilerParams(
        dimension_semantics=semantics or None, vmem_limit_bytes=VMEM_LIMIT
    )


def cost(flops, moved, weight=1.0):
    return pl.CostEstimate(
        flops=int(flops * weight), bytes_accessed=int(moved * weight), transcendentals=0
    )


def line_gather(piece, axis, first=None, gate=None):
    size = lax.axis_size(axis)
    up = [(i, i + 1) for i in range(size - 1)]
    down = [(i + 1, i) for i in range(size - 1)]
    right, left = [], []
    a = b = piece
    for step in range(size - 1):
        if step == 2 and gate is not None:
            a, b = after((a, b), gate)
        if step == 0 and first is not None:
            a, b = first
        else:
            a = lax.ppermute(a, axis, up)
            b = lax.ppermute(b, axis, down)
        right.append(a)
        left.append(b)
    return [(right[s - 1], left[size - s - 1]) for s in range(1, size)]


def send_chunks(chunks, axis):
    size = lax.axis_size(axis)
    return [chunks[0]] + [
        lax.ppermute(chunks[k], axis, [(i, (i + k) % size) for i in range(size)])
        for k in range(1, size)
    ]


def norm_kernel(size, me_ref, own, *refs):
    pairs = refs[: 2 * (size - 1)]
    gains, first_out, second_out, token_out, stat_out, work = refs[2 * (size - 1) :]
    part = own.shape[1]
    me = me_ref[0]
    for s in range(size):
        if s == 0:
            piece = own[...].astype(F32)
        else:
            piece = pairs[2 * s - 2][...].astype(F32) + pairs[2 * s - 1][...].astype(F32)
        at = lax.rem(me - s + size, size)
        work[:, pl.ds(pl.multiple_of(at * part, part), part)] = piece
    rows = work[...]
    token_out[...] = rows.astype(BF16)
    width = rows.shape[1]
    center = jnp.sum(rows, axis=1, keepdims=True) * (1.0 / width)
    shifted = rows - center
    inverse = lax.rsqrt(jnp.sum(shifted * shifted, axis=1, keepdims=True) * (1.0 / width) + 1e-05)
    normed = shifted * inverse
    first_out[...] = (normed * gains[0:1, :] + gains[1:2, :]).astype(BF16)
    second_out[...] = (normed * gains[2:3, :] + gains[3:4, :]).astype(BF16)
    lane = lax.broadcasted_iota(jnp.int32, stat_out.shape, 1)
    stat_out[...] = jnp.where(lane == 0, center, inverse)


def norm_call(me, own, pairs, gains, tile=128):
    count, part = own.shape
    size = len(pairs) + 1
    width = part * size
    flat = [p for pair in pairs for p in pair]
    block = pl.BlockSpec((tile, part), lambda i, *_: (i, 0))
    wide = pl.BlockSpec((tile, width), lambda i, *_: (i, 0))
    return pl.pallas_call(
        functools.partial(norm_kernel, size),
        grid_spec=pltpu.PrefetchScalarGridSpec(
            num_scalar_prefetch=1,
            grid=(count // tile,),
            in_specs=[block] * (1 + len(flat)) + [pl.BlockSpec((4, width), lambda i, *_: (0, 0))],
            out_specs=[wide, wide, wide, pl.BlockSpec((tile, 128), lambda i, *_: (i, 0))],
            scratch_shapes=[pltpu.VMEM((tile, width), F32)],
        ),
        out_shape=[
            jax.ShapeDtypeStruct((count, width), BF16),
            jax.ShapeDtypeStruct((count, width), BF16),
            jax.ShapeDtypeStruct((count, width), BF16),
            jax.ShapeDtypeStruct((count, 128), F32),
        ],
        compiler_params=params("arbitrary"),
        cost_estimate=cost(count * width * 16, count * width * 10),
        name="norm",
    )(me, own, *flat, gains)


def cot_kernel(size, local_len, tile, me_ref, len_ref, own, *refs):
    pairs = refs[: 2 * (size - 1)]
    rows_out, sum_out = refs[2 * (size - 1) :]
    part = own.shape[1]
    me, ctx = me_ref[0], me_ref[1]
    step = pl.program_id(0)
    start = step * tile
    seq = start // local_len
    length = len_ref[seq]
    position = ctx * local_len + lax.rem(start, local_len)
    position = position + lax.broadcasted_iota(jnp.int32, (tile, 1), 0)
    keep = position < length

    @pl.when(step == 0)
    def _():
        sum_out[...] = jnp.zeros_like(sum_out)

    for s in range(size):
        if s == 0:
            piece = own[...].astype(F32)
        else:
            piece = pairs[2 * s - 2][...].astype(F32) + pairs[2 * s - 1][...].astype(F32)
        piece = jnp.where(keep, piece, 0.0)
        at = lax.rem(me - s + size, size)
        cols = pl.ds(pl.multiple_of(at * part, part), part)
        rows_out[:, cols] = piece.astype(BF16)
        sum_out[0:1, cols] += jnp.sum(piece, axis=0, keepdims=True)


def cot_call(places, lengths, own, pairs, local_len, tile=256):
    count, part = own.shape
    size = len(pairs) + 1
    width = part * size
    flat = [p for pair in pairs for p in pair]
    block = pl.BlockSpec((tile, part), lambda i, *_: (i, 0))
    return pl.pallas_call(
        functools.partial(cot_kernel, size, local_len, tile),
        grid_spec=pltpu.PrefetchScalarGridSpec(
            num_scalar_prefetch=2,
            grid=(count // tile,),
            in_specs=[block] * (1 + len(flat)),
            out_specs=[
                pl.BlockSpec((tile, width), lambda i, *_: (i, 0)),
                pl.BlockSpec((8, width), lambda i, *_: (0, 0)),
            ],
        ),
        out_shape=[
            jax.ShapeDtypeStruct((count, width), BF16),
            jax.ShapeDtypeStruct((8, width), F32),
        ],
        compiler_params=params("arbitrary"),
        cost_estimate=cost(count * width * 4, count * width * 6),
        name="cotangent_rows",
    )(places, lengths, own, *flat)


def flat_rows(ref):
    value = ref[...]
    return value.reshape(value.shape[0] * value.shape[1], value.shape[2])


def joined_kernel(seqs, rows_ref, weight_ref, bias_ref, table_ref, query_ref, pair_ref):
    kind = lax.rem(pl.program_id(0), 3)
    out = dot(rows_ref[...], flat_rows(weight_ref), NN) + bias_ref[0:1, :]
    local_len = out.shape[0] // seqs

    def turned():
        front = out[:, :128]
        up = pltpu.roll(front, 128 - ROTARY // 2, 1)
        down = pltpu.roll(front, ROTARY // 2, 1)
        table = table_ref[...]
        if seqs > 1:
            table = jnp.concatenate([table] * seqs, axis=0)
        front = front * table[:, :128] + up * table[:, 128:256] + down * table[:, 256:]
        return jnp.concatenate([front, out[:, 128:]], axis=1)

    @pl.when(kind == 0)
    def _():
        query_ref[...] = (turned().astype(BF16).astype(F32) * HEAD ** (-0.5)).astype(BF16)

    @pl.when(kind == 1)
    def _():
        value = turned().astype(BF16)
        for s in range(seqs):
            pair_ref[s] = value[s * local_len : (s + 1) * local_len, :]

    @pl.when(kind == 2)
    def _():
        value = out.astype(BF16)
        for s in range(seqs):
            pair_ref[s] = value[s * local_len : (s + 1) * local_len, :]


def joined_call(rows, pack, bias, table, seqs, heads):
    count, width = rows.shape
    shards = pack.shape[0]
    local_len = count // seqs
    return pl.pallas_call(
        functools.partial(joined_kernel, seqs),
        grid=(3 * heads,),
        in_specs=[
            pl.BlockSpec((count, width), lambda j: (0, 0)),
            pl.BlockSpec((shards, width // shards, HEAD), lambda j: (0, 0, j)),
            pl.BlockSpec((8, HEAD), lambda j: (0, j)),
            pl.BlockSpec(table.shape, lambda j: (0, 0)),
        ],
        out_specs=[
            pl.BlockSpec((count, HEAD), lambda j: (0, j // 3)),
        ]
        + [
            pl.BlockSpec(
                (seqs, local_len, HEAD), lambda j: (0, 0, 2 * (j // 3) + (j % 3) // 2)
            )
        ],
        out_shape=[
            jax.ShapeDtypeStruct((count, heads * HEAD), BF16),
            jax.ShapeDtypeStruct((seqs, local_len, 2 * heads * HEAD), BF16),
        ],
        compiler_params=params("arbitrary"),
        cost_estimate=cost(6 * heads * HEAD * count * width, 2 * (count + 3 * heads * HEAD) * width),
        name="joined",
    )(rows, pack, jnp.broadcast_to(bias.reshape(1, -1), (8, bias.size)), table)


SLOTS = 4


def slot_refs(own_ref, below_ref, both_ref):
    return [own_ref, below_ref, both_ref.at[0], both_ref.at[1]]


def masked(scores, slot, first_key, first_query, length):
    keys = first_key + lax.broadcasted_iota(jnp.int32, (1, scores.shape[1]), 1)
    ok = keys < length
    if slot == 0:
        queries = first_query + lax.broadcasted_iota(jnp.int32, (scores.shape[0], 1), 0)
        ok = ok & (keys <= queries)
    return jnp.where(ok, scores, -1e30)


def forward_kernel(heads, seq, info, lens, query_ref, pair_ref, context_ref, lse_ref, *scratch):
    local_len = query_ref.shape[0]
    length = lens[seq]
    place = info[SLOTS]
    top, total, acc = scratch[:heads], scratch[heads : 2 * heads], scratch[2 * heads :]
    for slot in range(SLOTS):
        block = info[slot]
        first_key = block * local_len

        @pl.when((block >= 0) & (block <= place) & (first_key < length))
        def _():
            for head in range(heads):
                at = 2 * HEAD * head
                query = query_ref[:, HEAD * head : HEAD * (head + 1)]
                keys = pair_ref[block, :, at : at + HEAD]
                vals = pair_ref[block, :, at + HEAD : at + 2 * HEAD]
                scores = dot(query, keys, NT)
                scores = masked(scores, slot, first_key, place * local_len, length)
                best = jnp.max(scores, axis=1, keepdims=True)
                if slot > 0:
                    best = jnp.maximum(best, top[head][...])
                weights = jnp.exp(scores - best)
                summed = jnp.sum(weights, axis=1, keepdims=True)
                mixed = dot(weights.astype(BF16), vals, NN)
                if slot > 0:
                    scale = jnp.exp(top[head][...] - best)
                    summed = summed + total[head][...] * scale
                    mixed = mixed + acc[head][...] * scale
                top[head][...] = best
                total[head][...] = summed
                acc[head][...] = mixed

        if slot == 0:

            @pl.when(first_key >= length)
            def _():
                for head in range(heads):
                    top[head][...] = jnp.full_like(top[head], -1e30)
                    total[head][...] = jnp.zeros_like(total[head])
                    acc[head][...] = jnp.zeros_like(acc[head])

    for head in range(heads):
        cols = slice(HEAD * head, HEAD * (head + 1))
        context_ref[:, cols] = (acc[head][...] / total[head][...]).astype(BF16)
        lse = top[head][...] + jnp.log(total[head][...])
        lse_ref[:, 128 * head : 128 * (head + 1)] = jnp.broadcast_to(lse, (local_len, 128))


def forward_call(info, lengths, query, pairs, seq, heads):
    local_len = pairs.shape[2]
    return pl.pallas_call(
        functools.partial(forward_kernel, heads, seq),
        grid_spec=pltpu.PrefetchScalarGridSpec(
            num_scalar_prefetch=2,
            grid=(1,),
            in_specs=[
                pl.BlockSpec((local_len, heads * HEAD), lambda i, *_: (seq, 0)),
                pl.BlockSpec(
                    (SLOTS, None, local_len, 2 * heads * HEAD), lambda i, *_: (0, seq, 0, 0)
                ),
            ],
            out_specs=[
                pl.BlockSpec((local_len, heads * HEAD), lambda i, *_: (0, 0)),
                pl.BlockSpec((local_len, heads * 128), lambda i, *_: (0, 0)),
            ],
            scratch_shapes=[pltpu.VMEM((local_len, 1), F32)] * (2 * heads)
            + [pltpu.VMEM((local_len, HEAD), F32)] * heads,
        ),
        out_shape=[
            jax.ShapeDtypeStruct((local_len, heads * HEAD), BF16),
            jax.ShapeDtypeStruct((local_len, heads * 128), F32),
        ],
        compiler_params=params("arbitrary"),
        cost_estimate=cost(4 * local_len * heads * HEAD * local_len * SLOTS,
            4 * local_len * heads * HEAD * SLOTS, HEADS_WEIGHT),
        name="attention_forward",
    )(info, lengths, query, pairs)


def backward_kernel(
    heads, seq, info, lens, query_ref, context_ref, grad_ref, lse_ref, pair_ref, query_out, *refs
):
    local_len = query_ref.shape[0]
    pair_outs = slot_refs(*refs[:3])
    accs = refs[3:]
    length = lens[seq]
    place = info[SLOTS]
    for slot in range(SLOTS):
        block = info[slot]
        first_key = block * local_len
        seen = (block >= 0) & (block <= place) & (first_key < length)

        @pl.when(seen)
        def _():
            for head in range(heads):
                at = 2 * HEAD * head
                cols = slice(HEAD * head, HEAD * (head + 1))
                query, grad = query_ref[:, cols], grad_ref[:, cols]
                keys = pair_ref[block, :, at : at + HEAD]
                vals = pair_ref[block, :, at + HEAD : at + 2 * HEAD]
                shared = grad.astype(F32) * context_ref[:, cols].astype(F32)
                shared = jnp.sum(shared, axis=1, keepdims=True)
                scores = dot(query, keys, NT)
                scores = masked(scores, slot, first_key, place * local_len, length)
                probs = jnp.exp(scores - lse_ref[:, 128 * head : 128 * head + 1])
                score_grad = (probs * (dot(grad, vals, NT) - shared)).astype(BF16)
                pair_outs[slot][:, at : at + HEAD] = dot(score_grad, query, TN).astype(BF16)
                pair_outs[slot][:, at + HEAD : at + 2 * HEAD] = dot(
                    probs.astype(BF16), grad, TN
                ).astype(BF16)
                mixed = dot(score_grad, keys, NN)
                accs[head][...] = mixed if slot == 0 else accs[head][...] + mixed

        @pl.when(jnp.logical_not(seen))
        def _():
            pair_outs[slot][...] = jnp.zeros_like(pair_outs[slot])
            if slot == 0:
                for head in range(heads):
                    accs[head][...] = jnp.zeros_like(accs[head])

    for head in range(heads):
        query_out[:, HEAD * head : HEAD * (head + 1)] = (
            accs[head][...] * HEAD ** (-0.5)
        ).astype(BF16)


def backward_call(info, lengths, query, context, grad, lse, pairs, seq, heads):
    local_len = pairs.shape[2]
    here = pl.BlockSpec((local_len, heads * HEAD), lambda i, *_: (seq, 0))
    one = pl.BlockSpec((local_len, heads * HEAD), lambda i, *_: (0, 0))
    two = [pl.BlockSpec((local_len, 2 * heads * HEAD), lambda i, *_: (0, 0))] * 2
    two = two + [pl.BlockSpec((2, local_len, 2 * heads * HEAD), lambda i, *_: (0, 0, 0))]
    return pl.pallas_call(
        functools.partial(backward_kernel, heads, seq),
        grid_spec=pltpu.PrefetchScalarGridSpec(
            num_scalar_prefetch=2,
            grid=(1,),
            in_specs=[
                here,
                one,
                here,
                pl.BlockSpec((local_len, heads * 128), lambda i, *_: (0, 0)),
                pl.BlockSpec(
                    (SLOTS, None, local_len, 2 * heads * HEAD), lambda i, *_: (0, seq, 0, 0)
                ),
            ],
            out_specs=[one] + two,
            scratch_shapes=[pltpu.VMEM((local_len, HEAD), F32)] * heads,
        ),
        out_shape=[jax.ShapeDtypeStruct((local_len, heads * HEAD), BF16)]
        + [jax.ShapeDtypeStruct((local_len, 2 * heads * HEAD), BF16)] * 2
        + [jax.ShapeDtypeStruct((2, local_len, 2 * heads * HEAD), BF16)],
        compiler_params=params("arbitrary"),
        cost_estimate=cost(10 * local_len * heads * HEAD * local_len * SLOTS,
            8 * local_len * heads * HEAD * SLOTS, HEADS_WEIGHT),
        name="attention_backward",
    )(info, lengths, query, context, grad, lse, pairs)


def return_pairs(own, below, siblings, axis):
    taken = lax.ppermute(siblings, axis, [(0, 1), (1, 0), (2, 3), (3, 2)])
    lower = (below.astype(F32) + taken[1].astype(F32)).astype(BF16)
    above = lax.ppermute(lower, axis, [(2, 0), (3, 1)])
    return [own, taken, above], taken


def branch_kernel(parts, active_ref, *refs):
    context_refs, (outer_ref, output_ref, out_ref) = refs[:parts], refs[parts:]
    out = dot(active_ref[...], outer_ref[...], NT)
    context = jnp.concatenate([ref[...] for ref in context_refs], axis=0)
    out_ref[...] = (out + dot(context, flat_rows(output_ref), NT)).astype(BF16)


def branch_call(active, contexts, outer, pack, column, tile=512):
    count, hidden = active.shape
    width, inside = outer.shape[0], contexts[0].shape[1]
    rows = width // pack.shape[0]
    return pl.pallas_call(
        functools.partial(branch_kernel, len(contexts)),
        grid=(width // tile,),
        in_specs=[pl.BlockSpec((count, hidden), lambda j: (0, 0))]
        + [pl.BlockSpec(c.shape, lambda j: (0, 0)) for c in contexts]
        + [
            pl.BlockSpec((tile, hidden), lambda j: (j, 0)),
            pl.BlockSpec((tile // rows, rows, inside), lambda j: (j, 0, column)),
        ],
        out_specs=pl.BlockSpec((count, tile), lambda j: (0, j)),
        out_shape=jax.ShapeDtypeStruct((count, width), BF16),
        compiler_params=params("arbitrary"),
        cost_estimate=cost(2 * count * width * (hidden + inside), 2 * width * (hidden + inside), HEADS_WEIGHT),
        name="branch",
    )(active, *contexts, outer, pack)


def upper_kernel(rows_ref, weight_ref, bias_ref, active_ref, slope_ref):
    weight = flat_rows(weight_ref)
    bias = bias_ref[0:1, :]
    count = rows_ref.shape[0]
    piece = count // 4
    for i in range(4):
        here = slice(i * piece, (i + 1) * piece)
        upper = dot(rows_ref[here, :], weight, NN) + bias
        phi = 0.5 * (1.0 + lax.erf(upper * 0.7071067811865476))
        slope = phi + upper * jnp.exp(-0.5 * upper * upper) * 0.3989422804014327
        active_ref[here, :] = (upper * phi).astype(BF16)
        slope_ref[here, :] = slope.astype(BF16)


def upper_call(rows, pack, bias, column, tile=512):
    count, width = rows.shape
    hidden = bias.size
    shards = pack.shape[0]
    out = pl.BlockSpec((count, tile), lambda j: (0, j))
    first = column // tile
    return pl.pallas_call(
        upper_kernel,
        grid=(hidden // tile,),
        in_specs=[
            pl.BlockSpec((count, width), lambda j: (0, 0)),
            pl.BlockSpec((shards, width // shards, tile), lambda j: (0, 0, first + j)),
            pl.BlockSpec((8, tile), lambda j: (0, j)),
        ],
        out_specs=[out, out],
        out_shape=[jax.ShapeDtypeStruct((count, hidden), BF16)] * 2,
        compiler_params=params("arbitrary"),
        cost_estimate=cost(2 * count * width * hidden, 2 * width * (count + hidden)),
        name="upper",
    )(rows, pack, jnp.broadcast_to(bias.reshape(1, -1), (8, hidden)))


def upper_grad_kernel(rows_ref, weight_ref, slope_ref, out_ref, sum_ref):
    grad = dot(rows_ref[...], weight_ref[...], NN) * slope_ref[...].astype(F32)
    low = grad.astype(BF16)
    out_ref[...] = low
    sum_ref[...] = jnp.broadcast_to(
        jnp.sum(low.astype(F32), axis=0, keepdims=True), sum_ref.shape
    )


def upper_grad_call(rows, weight, slope, tile=512):
    count, width = rows.shape
    hidden = weight.shape[1]
    out = pl.BlockSpec((count, tile), lambda j: (0, j))
    return pl.pallas_call(
        upper_grad_kernel,
        grid=(hidden // tile,),
        in_specs=[
            pl.BlockSpec((count, width), lambda j: (0, 0)),
            pl.BlockSpec((width, tile), lambda j: (0, j)),
            out,
        ],
        out_specs=[out, pl.BlockSpec((8, tile), lambda j: (0, j))],
        out_shape=[
            jax.ShapeDtypeStruct((count, hidden), BF16),
            jax.ShapeDtypeStruct((8, hidden), F32),
        ],
        compiler_params=params("arbitrary"),
        cost_estimate=cost(2 * count * width * hidden, 2 * width * (2 * count + hidden), FEED_WEIGHT),
        name="upper_grad",
    )(rows, weight, slope)


def context_grad_kernel(rows_ref, weight_ref, out_ref):
    out_ref[...] = dot(rows_ref[...], flat_rows(weight_ref), NN).astype(BF16)


def context_grad_call(rows, pack, column, inside, tile=512):
    count, width = rows.shape
    return pl.pallas_call(
        context_grad_kernel,
        grid=(count // tile,),
        in_specs=[
            pl.BlockSpec((tile, width), lambda i: (i, 0)),
            pl.BlockSpec(
                (pack.shape[0], width // pack.shape[0], inside), lambda i: (0, 0, column)
            ),
        ],
        out_specs=pl.BlockSpec((tile, inside), lambda i: (i, 0)),
        out_shape=jax.ShapeDtypeStruct((count, inside), BF16),
        compiler_params=params("arbitrary"),
        cost_estimate=cost(2 * count * width * inside, 2 * width * (count + inside), HEADS_WEIGHT),
        name="context_grad",
    )(rows, pack)


def column_sums(grad, normed, out_ref):
    count, tile = grad.shape
    out_ref[0:1, :] = jnp.sum(grad * normed, axis=0, keepdims=True)
    out_ref[1:2, :] = jnp.sum(grad, axis=0, keepdims=True)
    out_ref[2:8, :] = jnp.zeros((6, tile), F32)


def second_kernel(grad_ref, weight_ref, rows_ref, stat_ref, gain_ref, out_ref, sum_ref):
    grad = dot(grad_ref[...], flat_rows(weight_ref), NT)
    normed = (rows_ref[...].astype(F32) - stat_ref[:, 0:1]) * stat_ref[:, 1:2]
    column_sums(grad, normed, sum_ref)
    out_ref[...] = (grad * gain_ref[2:3, :]).astype(BF16)


def second_call(grad, pack, column, rows, stats, gains, tile=512):
    count, hidden = grad.shape
    width = rows.shape[1]
    deep = width // pack.shape[0]
    return pl.pallas_call(
        second_kernel,
        grid=(width // tile,),
        in_specs=[
            pl.BlockSpec((count, hidden), lambda j: (0, 0)),
            pl.BlockSpec((tile // deep, deep, hidden), lambda j: (j, 0, column)),
            pl.BlockSpec((count, tile), lambda j: (0, j)),
            pl.BlockSpec((count, 128), lambda j: (0, 0)),
            pl.BlockSpec((4, tile), lambda j: (0, j)),
        ],
        out_specs=[
            pl.BlockSpec((count, tile), lambda j: (0, j)),
            pl.BlockSpec((8, tile), lambda j: (0, j)),
        ],
        out_shape=[
            jax.ShapeDtypeStruct((count, width), BF16),
            jax.ShapeDtypeStruct((8, width), F32),
        ],
        compiler_params=params("arbitrary"),
        cost_estimate=cost(2 * count * width * hidden, 2 * (width * hidden + 3 * count * width), LAST_WEIGHT),
        name="second_in_grad",
    )(grad, pack, rows, stats, gains)


def joined_grad_kernel(heads, *refs):
    (table_ref, out_ref, sum_ref), refs = refs[-3:], refs[:-3]
    table = table_ref[...]
    local_len = table.shape[0]

    def back(value):
        front = value[:, :128]
        up = pltpu.roll(front, 128 - ROTARY // 2, 1)
        down = pltpu.roll(front, ROTARY // 2, 1)
        front = front * table[:, :128] - up * table[:, 128:256] - down * table[:, 256:]
        return jnp.concatenate([front, value[:, 128:]], axis=1)

    sum_ref[...] = jnp.zeros_like(sum_ref)
    for seq in range(len(refs) // 4):
        query_ref, own_ref, near_ref, far_ref = refs[4 * seq : 4 * seq + 4]
        here = slice(seq * local_len, (seq + 1) * local_len)
        for head in range(heads):
            at = 3 * HEAD * head
            pair = slice(2 * HEAD * head, 2 * HEAD * (head + 1))
            total = own_ref[:, pair].astype(F32) + near_ref[0, :, pair].astype(F32)
            total = total + far_ref[:, pair].astype(F32)
            query = query_ref[:, HEAD * head : HEAD * (head + 1)].astype(F32)
            parts = [back(query), back(total[:, :HEAD]), total[:, HEAD:]]
            for i, part in enumerate(parts):
                cols = slice(at + HEAD * i, at + HEAD * (i + 1))
                low = part.astype(BF16)
                out_ref[here, cols] = low
                sum_ref[0:1, cols] += jnp.sum(low.astype(F32), axis=0, keepdims=True)


def joined_grad_call(queries, sums, table, heads):
    seqs = len(queries)
    count = seqs * queries[0].shape[0]
    width = 3 * heads * HEAD
    flat = [a for query, three in zip(queries, sums) for a in (query, *three)]
    return pl.pallas_call(
        functools.partial(joined_grad_kernel, heads),
        out_shape=[
            jax.ShapeDtypeStruct((count, width), BF16),
            jax.ShapeDtypeStruct((8, width), F32),
        ],
        compiler_params=params(),
        cost_estimate=cost(10 * count * width, 10 * count * width, LAST_WEIGHT),
        name="joined_grad",
    )(*flat, table)


EXTRA = 8


def first_kernel(ranks, order, grad_ref, weight_ref, rows_ref, stat_ref, gain_ref, second_ref, *refs):
    out_refs, (sum_ref, row_ref) = refs[:ranks], refs[ranks:]
    step = pl.program_id(0)
    grad = dot(grad_ref[...], flat_rows(weight_ref), NT)
    count, tile = grad.shape
    normed = (rows_ref[...].astype(F32) - stat_ref[:, 0:1]) * stat_ref[:, 1:2]
    column_sums(grad, normed, sum_ref)
    total = grad * gain_ref[0:1, :] + second_ref[...].astype(F32)
    low = total.astype(BF16)
    for k in range(ranks):

        @pl.when(step == k)
        def _():
            out_refs[k][:count, :] = low

    plain = jnp.sum(total, axis=1, keepdims=True)
    along = jnp.sum(total * normed, axis=1, keepdims=True)
    lane = lax.broadcasted_iota(jnp.int32, row_ref.shape, 1)
    both = jnp.where(lane == 0, plain, along)

    @pl.when(step == 0)
    def _():
        row_ref[...] = both

    @pl.when(step > 0)
    def _():
        row_ref[...] += both

    @pl.when(step == ranks - 1)
    def _():
        turned = row_ref[...].T
        lines = [turned[i : i + 1, j : j + tile] for i in (0, 1) for j in range(0, count, tile)]
        lines.append(jnp.zeros((EXTRA - len(lines), tile), F32))
        extra = jnp.concatenate(lines, axis=0).astype(BF16)
        for ref in out_refs:
            ref[count:, :] = extra


def first_call(order, grad, pack, rows, stats, gains, second, ranks):
    count, inside = grad.shape
    width = rows.shape[1]
    tile = width // ranks
    deep = width // pack.shape[0]
    return pl.pallas_call(
        functools.partial(first_kernel, ranks),
        grid_spec=pltpu.PrefetchScalarGridSpec(
            num_scalar_prefetch=1,
            grid=(ranks,),
            in_specs=[
                pl.BlockSpec((count, inside), lambda j, _: (0, 0)),
                pl.BlockSpec((tile // deep, deep, inside), lambda j, order: (order[j], 0, 0)),
                pl.BlockSpec((count, tile), lambda j, order: (0, order[j])),
                pl.BlockSpec((count, 128), lambda j, _: (0, 0)),
                pl.BlockSpec((4, tile), lambda j, order: (0, order[j])),
                pl.BlockSpec((count, tile), lambda j, order: (0, order[j])),
            ],
            out_specs=[pl.BlockSpec((count + EXTRA, tile), lambda j, _: (0, 0))] * ranks
            + [pl.BlockSpec((8, tile), lambda j, order: (0, order[j]))],
            scratch_shapes=[pltpu.VMEM((count, 128), F32)],
        ),
        out_shape=[jax.ShapeDtypeStruct((count + EXTRA, tile), BF16)] * ranks
        + [jax.ShapeDtypeStruct((8, width), F32)],
        compiler_params=params("arbitrary"),
        cost_estimate=cost(2 * count * width * inside, 2 * (width * inside + 4 * count * width), LAST_WEIGHT),
        name="first_in_grad",
    )(order, grad, pack, rows, stats, gains, second)


def flips(size, by):
    return [(i, i ^ by) for i in range(size)]


def paired(group):
    return lax.axis_size(group[0]) == 2 and lax.axis_size(group[1]) == 4


def member(group):
    return lax.axis_size(group[1]) * lax.axis_index(group[0]) + lax.axis_index(group[1])


def gather_small(vector, group):
    if not paired(group):
        return lax.all_gather(vector.reshape(1, 1, -1), group, axis=0, tiled=True)[:, 0]
    rows = jnp.zeros((8, vector.size), vector.dtype)
    rows = lax.dynamic_update_slice_in_dim(rows, vector.reshape(1, -1), member(group), 0)
    for by in (1, 2, 4):
        rows = rows + lax.ppermute(rows, group, flips(8, by))
    return rows


def weight_grad_kernel(sizes, outs, small, order, *refs):
    parts = len(sizes)
    lhs_refs, rhs_refs, refs = refs[: 4 * parts], refs[4 * parts : 5 * parts], refs[5 * parts :]
    small_ref = refs[0] if small else None
    add_ref = refs[small] if outs > 1 else None
    out_refs, turned = refs[-1 - outs : -1], refs[-1]
    rows = lhs_refs[0].shape[1]
    deep = rows + EXTRA * small
    step = pl.program_id(0)

    def put(k, value, start):
        height = value.shape[0]
        if outs == 1:
            out_refs[0][k * deep + start : k * deep + start + height, :] = value.astype(BF16)
        else:
            add = add_ref[k * deep + start : k * deep + start + height, :].astype(F32)
            out_refs[k][start : start + height, :] = (value + add).astype(BF16)

    first = 0
    for i, size in enumerate(sizes):
        lhs, rhs_ref = lhs_refs[4 * i : 4 * i + 4], rhs_refs[i]

        @pl.when(step == first)
        def _():
            for k in range(4):
                turned[k * rows : (k + 1) * rows, :] = lhs[k][...].T

        @pl.when((step >= first) & (step < first + size))
        def _():
            out = dot(turned[...], rhs_ref[...], NN)
            for k in range(4):
                put(k, out[k * rows : (k + 1) * rows, :], 0)

        first += size
    if small:
        for k in range(4):
            put(k, small_ref[order[k]], rows)


def weight_grad_call(order, pairs, add=None, small=None, tile=512):
    count, width = pairs[0][0].shape
    rows = width // 8
    sizes = [rhs.shape[1] // tile for _, rhs in pairs]
    total = sum(sizes) * tile
    outs = 1 if add is None else 4
    height = rows if small is None else rows + EXTRA
    deep = 4 * height if add is None else height
    firsts = [sum(sizes[:i]) for i in range(len(sizes))]

    def column(k):
        return pl.BlockSpec((count, rows), lambda j, order: (0, order[k]))

    def piece(first, size):
        return pl.BlockSpec(
            (count, tile), lambda j, _: (0, jnp.minimum(jnp.maximum(j - first, 0), size - 1))
        )

    out = pl.BlockSpec((deep, tile), lambda j, *_: (0, j))
    extra_specs, extra = [], []
    if small is not None:
        extra_specs.append(pl.BlockSpec((8, EXTRA, tile), lambda j, *_: (0, 0, j)))
        extra.append(small)
    if add is not None:
        extra_specs.append(pl.BlockSpec((4 * height, tile), lambda j, *_: (0, j)))
        extra.append(add)
    return pl.pallas_call(
        functools.partial(weight_grad_kernel, sizes, outs, int(small is not None)),
        grid_spec=pltpu.PrefetchScalarGridSpec(
            num_scalar_prefetch=1,
            grid=(sum(sizes),),
            in_specs=[column(k) for _ in pairs for k in range(4)]
            + [piece(f, n) for f, n in zip(firsts, sizes)]
            + extra_specs,
            out_specs=[out] * outs,
            scratch_shapes=[pltpu.VMEM((4 * rows, count), BF16)],
        ),
        out_shape=[jax.ShapeDtypeStruct((deep, total), BF16)] * outs,
        compiler_params=params("arbitrary"),
        cost_estimate=cost(8 * rows * count * total, 2 * (count * (4 * rows + total) + 8 * rows * total), LAST_WEIGHT),
        name="weight_grad",
    )(
        order,
        *[lhs for lhs, _ in pairs for _ in range(4)],
        *[rhs for _, rhs in pairs],
        *extra,
    )


def product_kernel(sizes, *refs):
    parts = len(sizes)
    lhs_refs, rhs_refs = refs[:parts], refs[parts : 2 * parts]
    out_ref, turned = refs[2 * parts :]
    step = pl.program_id(0)
    first = 0
    for lhs_ref, rhs_ref, size in zip(lhs_refs, rhs_refs, sizes):

        @pl.when(step == first)
        def _():
            turned[...] = lhs_ref[...].T

        @pl.when((step >= first) & (step < first + size))
        def _():
            out_ref[...] = dot(turned[...], rhs_ref[...], NN).astype(BF16)

        first += size


def product_call(pairs, tile=512):
    count, width = pairs[0][0].shape
    sizes = [rhs.shape[1] // tile for _, rhs in pairs]
    total = sum(sizes) * tile
    firsts = [sum(sizes[:i]) for i in range(len(sizes))]

    def piece(first, size):
        return pl.BlockSpec(
            (count, tile), lambda j: (0, jnp.minimum(jnp.maximum(j - first, 0), size - 1))
        )

    return pl.pallas_call(
        functools.partial(product_kernel, sizes),
        grid=(sum(sizes),),
        in_specs=[pl.BlockSpec((count, width), lambda j: (0, 0)) for _ in pairs]
        + [piece(f, n) for f, n in zip(firsts, sizes)],
        out_specs=pl.BlockSpec((width, tile), lambda j: (0, j)),
        out_shape=jax.ShapeDtypeStruct((width, total), BF16),
        scratch_shapes=[pltpu.VMEM((width, count), BF16)],
        compiler_params=params("arbitrary"),
        cost_estimate=cost(2 * width * count * total, 2 * (count * (width + total) + width * total), FEED_WEIGHT),
        name="product",
    )(*[lhs for lhs, _ in pairs], *[rhs for _, rhs in pairs])


STEPS = (0, 2, 4, 6)


def weight_grad_given(pairs, group, small=None):
    if not paired(group):
        return None
    steps = jnp.array(STEPS, jnp.int32)
    (given,) = weight_grad_call((member(group) ^ 1) ^ steps, pairs, small=small)
    return given


def weight_grad_kept(pairs, given, group, small=None):
    if not paired(group):
        whole = jnp.concatenate([dot(lhs, rhs, TN).astype(BF16) for lhs, rhs in pairs], axis=1)
        return [lax.psum_scatter(whole, group, scatter_dimension=0, tiled=True)]
    taken = lax.ppermute(given, group, flips(8, 1))
    sums = weight_grad_call(
        member(group) ^ jnp.array(STEPS, jnp.int32), pairs, taken, small=small
    )
    return [sums[0]] + [
        lax.ppermute(part, group, flips(8, by)) for part, by in zip(sums[1:], STEPS[1:])
    ]


def total_of(terms):
    return functools.reduce(lambda a, b: a + b, [t.astype(F32) for t in terms])


def line_sum(value, axis):
    size = lax.axis_size(axis)
    terms = [value]
    for step in range(1, size):
        terms.append(lax.ppermute(value, axis, [(i, (i + step) % size) for i in range(size)]))
    return functools.reduce(lambda a, b: a + b, terms)


def body(
    tokens,
    lengths,
    cotangent,
    first_gain,
    first_shift,
    joined_weight,
    joined_bias,
    output_weight,
    output_bias,
    second_gain,
    second_shift,
    inner_weight,
    inner_bias,
    outer_weight,
    outer_bias,
):
    group = ("fsdp", "ctx")
    seqs, local_len, part = tokens.shape
    count = seqs * local_len
    ranks = lax.axis_size("tp")
    width = part * ranks
    shards = lax.axis_size("fsdp") * lax.axis_size("ctx")
    rows_part = width // shards
    heads = joined_weight.shape[1]
    hidden = inner_weight.shape[1]
    me, ctx = lax.axis_index("tp"), lax.axis_index("ctx")

    own_tokens, own_cot = tokens.reshape(count, part), cotangent.reshape(count, part)
    joined_width, inside = heads * 3 * HEAD, heads * HEAD
    vectors = [first_gain, first_shift, second_gain, second_shift, output_bias, outer_bias]
    flat = jnp.concatenate(vectors + [joined_bias.reshape(-1), inner_bias.reshape(-1)])
    small = gather_small(jnp.pad(flat, (0, -flat.size % 256)), group)
    shard = jnp.concatenate(
        [joined_weight.reshape(rows_part, -1), output_weight.reshape(rows_part, -1)], axis=1
    )
    small = small.astype(F32)
    whole = [small[:, i * rows_part : (i + 1) * rows_part].reshape(width) for i in range(6)]
    at = 6 * rows_part
    whole_joined_bias = (
        small[:, at : at + joined_bias.size]
        .reshape((shards,) + joined_bias.shape)
        .transpose(1, 0, 2)
        .reshape(-1)
    )
    at += joined_bias.size
    whole_inner_bias = (
        small[:, at : at + inner_bias.size]
        .reshape((shards,) + inner_bias.shape)
        .transpose(1, 0, 2)
        .reshape(-1)
    )
    gains = jnp.stack(whole[:4])
    positions = ctx * local_len + jnp.arange(local_len, dtype=jnp.int32)
    half = ROTARY // 2
    frequency = 1.0 / 10000.0 ** (jnp.arange(half, dtype=F32) * 2.0 / ROTARY)
    angles = positions.astype(F32)[:, None] * frequency[None, :]
    cosine, sine = jnp.cos(angles), jnp.sin(angles)
    ones = jnp.ones((local_len, 128 - ROTARY), F32)
    nothing = jnp.zeros((local_len, half), F32)
    blank = jnp.zeros((local_len, 128 - ROTARY), F32)
    table = jnp.concatenate(
        [cosine, cosine, ones, -sine, nothing, blank, nothing, sine, blank], axis=1
    )
    early = (table, gains)
    token_pairs = line_gather(own_tokens, "tp", None, early)
    cot_start = after(own_cot, token_pairs)
    cot_first = (
        lax.ppermute(cot_start, "tp", [(i, i + 1) for i in range(ranks - 1)]),
        lax.ppermute(cot_start, "tp", [(i + 1, i) for i in range(ranks - 1)]),
    )
    pack = lax.all_gather(shard, group, axis=0, tiled=False)
    inner = lax.all_gather(inner_weight, group, axis=0, tiled=False)

    places = jnp.stack([me, ctx]).astype(jnp.int32)
    first_in, second_in, rows, stats = norm_call(places[:1], own_tokens, token_pairs, gains)
    center, inverse = stats[:, 0:1], stats[:, 1:2]
    query, pair = joined_call(after(first_in, cot_first), pack, whole_joined_bias, table, seqs, heads)
    pairs = lax.all_gather(pair, "ctx", axis=0, tiled=False)
    low, odd = ctx - 2, ctx + 1 - 2 * lax.rem(ctx, 2)
    info = jnp.stack([ctx, low, odd, jnp.where(low >= 0, odd - 2, -1), ctx]).astype(jnp.int32)
    active, slope = upper_call(after(second_in, query), inner, whole_inner_bias, 0)
    cot_pairs = line_gather(cot_start, "tp", cot_first, active)
    grad_rows, bias_sums = cot_call(places, after(lengths, active), own_cot, cot_pairs, local_len)
    bias_grad = bias_sums[0]
    outer = lax.all_gather(after(outer_weight, grad_rows, pairs), group, axis=0, tiled=True)
    contexts, lses = [], []
    ready = after(query, grad_rows)
    for seq in range(seqs):
        context, lse = forward_call(info, lengths, ready, pairs, seq, heads)
        ready = after(query, context)
        contexts.append(context)
        lses.append(lse)

    context_grad = context_grad_call(after(grad_rows, ready), pack, joined_width // inside, inside)
    queries, sums = [], []
    for seq in range(seqs):
        query_grad, *pair_grads = backward_call(
            info, lengths, ready, contexts[seq], context_grad, lses[seq], pairs, seq, heads
        )
        ready = after(query, query_grad)
        queries.append(query_grad)
        three, taken = return_pairs(*pair_grads, "ctx")
        sums.append(three)
    branch = branch_call(
        after(active, query_grad, taken), contexts, outer, pack, joined_width // inside
    )
    summed = lax.psum_scatter(branch, "tp", scatter_dimension=1, tiled=True).astype(F32)
    own_start = me * part
    own_bias = lax.dynamic_slice_in_dim(whole[4] + whole[5], own_start, part)
    valid = (positions[None, :] < lengths[:, None]).astype(F32).reshape(count, 1)
    layer_out = (valid * (own_tokens.astype(F32) + summed + own_bias)).astype(BF16)

    outer_whole = product_call([(after(grad_rows, branch), active)])
    outer_out = lax.psum_scatter(outer_whole, group, scatter_dimension=0, tiled=True)
    grad_late = after(grad_rows, outer_whole)
    upper_grad, upper_sums = upper_grad_call(grad_late, outer, slope)
    inner_bias_grad = upper_sums[0]
    second_scaled, second_sums = second_call(
        upper_grad,
        inner,
        0,
        rows,
        stats,
        gains,
    )
    joined_grad, joined_sums = joined_grad_call(
        after(queries, second_scaled), sums, table, heads
    )
    joined_bias_grad = joined_sums[0]
    order = lax.rem(me + jnp.arange(ranks, dtype=jnp.int32), ranks)
    *scaled, first_sums = first_call(
        order, joined_grad, pack, rows, stats, gains, second_scaled, ranks
    )

    column = jnp.concatenate([first_sums[:2], second_sums[:2], bias_grad.reshape(1, -1)])
    by_shard = [
        column.reshape(5, shards, rows_part).transpose(1, 0, 2).reshape(shards, -1),
        joined_bias_grad.reshape(heads, shards, -1).transpose(1, 0, 2).reshape(shards, -1),
        inner_bias_grad.reshape(-1, shards, inner_bias.shape[1])
        .transpose(1, 0, 2)
        .reshape(shards, -1),
    ]
    small_grads = jnp.concatenate(by_shard, axis=1)
    size = joined_width + inside
    riders = None
    if paired(group):
        riders = jnp.pad(
            small_grads.astype(BF16)[:, None, :],
            ((0, 0), (0, EXTRA - 1), (0, size - small_grads.shape[1])),
        )
    context = jnp.concatenate(contexts, axis=0)
    head_pairs = [(after(first_in, scaled[0]), joined_grad), (grad_rows, context)]
    head_given = weight_grad_given(head_pairs, group, riders)
    inner_whole = product_call([(after(second_in, head_given), upper_grad)])
    inner_out = lax.psum_scatter(inner_whole, group, scatter_dimension=0, tiled=True)
    head_pairs = [(after(first_in, head_given, inner_whole), joined_grad), (grad_rows, context)]
    head_terms = weight_grad_kept(head_pairs, head_given, group, riders)
    share = total_of(send_chunks(scaled, "tp"))
    lines = 2 * count // part
    means = share[count : count + lines].reshape(2, count) / width
    share = share[:count]
    own_normed = (own_tokens.astype(F32) - center) * inverse
    own_rows = lax.dynamic_slice_in_dim(grad_rows, own_start, part, 1).astype(F32)
    tokens_grad = own_rows + inverse * (
        share - means[0][:, None] - own_normed * means[1][:, None]
    )

    head_terms = [head_terms[0]] + [after(t, tokens_grad) for t in head_terms[1:]]
    head_out = total_of(head_terms)
    if riders is None:
        small_out = lax.psum_scatter(small_grads, group, scatter_dimension=0, tiled=True)[0]
    else:
        small_out = head_out[rows_part]
    vector = line_sum(small_out[: 4 * rows_part].reshape(-1, 128), "tp").reshape(4, -1)
    at = 5 * rows_part
    joined_bias_out = small_out[at : at + joined_bias.size].reshape(joined_bias.shape)
    at += joined_bias.size
    inner_bias_out = small_out[at : at + inner_bias.size].reshape(inner_bias.shape)
    bias_out = small_out[4 * rows_part : 5 * rows_part]

    return (
        layer_out.reshape(tokens.shape),
        tokens_grad.reshape(tokens.shape),
        vector[0],
        vector[1],
        head_out[:rows_part, :joined_width].reshape(joined_weight.shape),
        joined_bias_out,
        head_out[:rows_part, joined_width:].reshape(output_weight.shape),
        bias_out,
        vector[2],
        vector[3],
        inner_out.astype(F32),
        inner_bias_out,
        outer_out.astype(F32),
        bias_out,
    )


def solution(mesh):
    both = ("fsdp", "ctx")
    return jax.shard_map(
        body,
        mesh=mesh,
        in_specs=(
            P("fsdp", "ctx", "tp"),
            P("fsdp"),
            P("fsdp", "ctx", "tp"),
            P(both),
            P(both),
            P(both, "tp", None),
            P("tp", both),
            P(both, "tp", None),
            P(both),
            P(both),
            P(both),
            P(both, "tp"),
            P("tp", both),
            P(both, "tp"),
            P(both),
        ),
        out_specs=(
            P("fsdp", "ctx", "tp"),
            P("fsdp", "ctx", "tp"),
            P(both),
            P(both),
            P(both, "tp", None),
            P("tp", both),
            P(both, "tp", None),
            P(both),
            P(both),
            P(both),
            P(both, "tp"),
            P("tp", both),
            P(both, "tp"),
            P(both),
        ),
        check_vma=False,
    )
```
